32 devices in a mesh: groups: 2 (over y), expert: 16 (over z, x, core).
Axes of the slice: x: 2, y: 2, z: 4, core: 2. Of those that a mesh axis runs over, the one named last changes fastest.
Arguments:
- queries: bfloat16 [192, 6144], P(('groups', 'expert')), parts along dimension 0, may hold values from -8 to 8
- tree_key_value: bfloat16 [192, 2, 1024], P(('groups', 'expert')), parts along dimension 0, may hold values from -6 to 6
- key_value_cache: bfloat16 [32, 2, 512, 1024], P(('groups', 'expert')), parts along dimension 0, may hold values from -8 to 8
- lengths: int32 [32], P(('groups', 'expert')), parts along dimension 0, may hold values from 128 to 512, as said below
- parents: int32 [192], P(('groups', 'expert')), parts along dimension 0, may hold values from 0 to 4, as said below
- residual: bfloat16 [192, 6144], P(('groups', 'expert')), parts along dimension 0, may hold values from -6 to 6
- ffn_gain: bfloat16 [6144], replicated, may hold values from 0.099609375 to 1.8984375
- router: bfloat16 [6144, 4], replicated, may hold values from -0.078125 to 0.078125
- routes: int32 [192, 2], P(('groups', 'expert')), parts along dimension 0, may hold values from 0 to 3, all different within a row; in each aligned block of 6 rows (0 to 5, 6 to 11, ...) at most 4 rows name the same one
- gate_weight: bfloat16 [6144, 32768], P(None, 'expert'), may hold values from -0.078125 to 0.078125
- up_weight: bfloat16 [6144, 32768], P(None, 'expert'), may hold values from -0.078125 to 0.078125
- down_weight: bfloat16 [32768, 6144], P('expert'), may hold values from -0.0625 to 0.0625
- accepted: int32 [32], P(('groups', 'expert')), parts along dimension 0, may hold values from 0 to 5
- next_embed: bfloat16 [32, 6144], P(('groups', 'expert')), parts along dimension 0, may hold values from -6 to 6
- draft_fc: bfloat16 [12288, 6144], P('expert'), may hold values from -0.0546875 to 0.0546875
Outputs:
- layer_out: bfloat16 [192, 6144], P(('groups', 'expert')), parts along dimension 0
- draft_out: bfloat16 [32, 6144], P(('groups', 'expert')), parts along dimension 0
The draws below stay inside these ranges and needn't reach their ends.
There are 2 independent parts, one for each index of `groups`. The reference program is written for one: setup_inputs(seed, part) draws one part's arguments, and reference() takes and returns one part's arrays. A program takes and returns all parts, laid end to end along the dimension named above; an argument that names none is the same for every part. Nothing has to cross between parts.
Inputs may be any that keep to these rules, and one draw needn't show every extreme that they name: `lengths`: both ends are reached by some request. `parents`: entry i of a request's 6 entries names an earlier node as its parent; entry 0, the root, names itself. `routes`: among the rows of one device no expert is named more than 4 times, a bound that some block reaches.
All inputs are finite; a program needn't handle non-finite values.
Results may differ from the reference program's by a relative error of at most 0.0051.
Values may be sent and summed in bfloat16 or wider, within the bound.
A program may use at most 128 MiB of HBM per device.

```python
import math
import jax
import jax.numpy as jnp
import numpy as np
from jax import lax

D = 6144
QUERY_HEADS = 48
KEY_VALUE_HEADS = 8
HEAD_SIZE = 128
FF = 8192
EXPERTS = 4
TREE_NODES = 6
CACHE_SLOTS = 512
TOK_DEV = 6
CAP = 4
REQUEST_COUNT = 16
TREE_TOKENS = 96
N_EXPERT = 16


def draw_queries(key, part):
    own_key = jax.random.fold_in(key, 31)
    base_draw = jnp.clip(jax.random.normal(own_key, (TREE_TOKENS, QUERY_HEADS * HEAD_SIZE), jnp.float32), -6.0, 6.0)
    return base_draw.astype(jnp.bfloat16)


def draw_key_value_cache(key, part):
    own_key = jax.random.fold_in(key, 47)
    whole_shape = (REQUEST_COUNT, 2, CACHE_SLOTS, KEY_VALUE_HEADS * HEAD_SIZE)
    base_draw = jnp.clip(jax.random.normal(own_key, whole_shape, jnp.float32), -6.0, 6.0)
    return base_draw.astype(jnp.bfloat16)


def draw_lengths(key, part):
    first_key, second_key = jax.random.split(jax.random.fold_in(key, 5))
    drawn_lengths = jax.random.randint(first_key, (REQUEST_COUNT,), CACHE_SLOTS // 4, CACHE_SLOTS + 1)
    chosen = jax.random.randint(second_key, (), 0, REQUEST_COUNT)
    drawn_lengths = drawn_lengths.at[chosen].set(CACHE_SLOTS)
    drawn_lengths = drawn_lengths.at[(chosen + 1) % REQUEST_COUNT].set(CACHE_SLOTS // 4)
    return drawn_lengths.astype(jnp.int32)


def draw_parents(key, part):
    node_index = jnp.arange(TREE_TOKENS, dtype=jnp.int32) % TREE_NODES
    chosen = jax.random.randint(jax.random.fold_in(key, 71), (TREE_TOKENS,), 0, jnp.maximum(node_index, 1))
    chained = jnp.maximum(node_index - 1, 0)
    return jnp.where(jnp.arange(TREE_TOKENS) < TREE_NODES, chained, chosen).astype(jnp.int32)


def touch_ends(values, key, smallest, top_value):
    extent = values.shape
    index_at = [jax.random.randint(jax.random.fold_in(key, axis), (), 0, extent[axis]) for axis in range(len(extent))]
    values = values.at[tuple(index_at)].set(smallest)
    longest = extent.index(max(extent))
    index_at[longest] = (index_at[longest] + 1) % extent[longest]
    return values.at[tuple(index_at)].set(top_value)


def steps_of(rng, dims, shards, smallest, high):
    def one(position, blocks):
        steps = jax.random.uniform(jax.random.fold_in(jax.random.fold_in(rng, 6), position), (blocks,), jnp.float32, smallest / len(shards), high / len(shards))
        return jnp.repeat(jnp.exp(steps), dims[position] // blocks).reshape((-1,) + (1,) * (len(dims) - position - 1))

    loudness = one(*shards[0])
    for cut in shards[1:]:
        loudness = loudness * one(*cut)
    return loudness


def routed_block(rng, own, number, rows, number_of, top, reach, skew):
    ranking = jax.random.permutation(rng, number_of)
    packed, ordinary = load_shares(number_of, rows * top, reach, skew, True), load_shares(number_of, rows * top, reach, skew, False)
    places = jnp.arange(number_of)

    def named(tallies, offset_by):
        used = int((tallies > 0).sum())
        fixed = max(1, used // 4)
        passed = fixed + (places - fixed + offset_by * (used - fixed)) % max(1, number_of - fixed)
        return jnp.zeros((number_of,), jnp.int32).at[ranking[jnp.where(places < fixed, places, passed)]].set(jnp.asarray(tallies, jnp.int32))

    tallies = jnp.where(number % 4 == 0, named(packed, number // 4), named(ordinary, number - number // 4 - 1))
    mixed = jax.random.permutation(jax.random.fold_in(own, 3), number_of)
    source_of, taker = mixed[0:number_of // 2 * 2:2], mixed[1:number_of // 2 * 2:2]
    room = jnp.minimum(tallies[source_of] - 1, reach - tallies[taker]) // 2
    room = jnp.where((source_of == ranking[0]) | (taker == ranking[0]) | (tallies[taker] == 0), 0, jnp.maximum(room, 0))
    passed = jax.random.randint(jax.random.fold_in(own, 4), (number_of // 2,), 0, 1 << 20) % (room + 1)
    tallies = tallies.at[source_of].add(-passed).at[taker].add(passed)
    members = jnp.searchsorted(jnp.cumsum(tallies), jnp.arange(rows * top), side="right").astype(jnp.int32)
    grid = members.reshape(top, rows).T
    grid = grid[jax.random.permutation(jax.random.fold_in(own, 1), rows)]
    offset_by = jax.random.randint(jax.random.fold_in(own, 2), (rows, 1), 0, top)
    return jnp.take_along_axis(grid, (jnp.arange(top)[None, :] + offset_by) % top, axis=1)


def load_shares(number_of, total, limit, slope, full):
    weights = [(1 << 20) // math.isqrt(standing ** slope) + 1 for standing in range(1, number_of + 1)]
    largest = limit if full else min(limit, max(-(-total // number_of), total * weights[0] // sum(weights)))
    least = 1 if total - largest >= number_of - 1 else 0
    given, surplus = [largest] + [least] * (number_of - 1), total - largest - least * (number_of - 1)
    while surplus > 0:
        free = [i for i in range(1, number_of) if given[i] < largest] or [i for i in range(1, number_of) if given[i] < limit]
        mass, left = sum([weights[i] for i in free]), surplus
        for i in free:
            addition = min(limit - given[i], max(1, left * weights[i] // mass), surplus)
            given[i] = given[i] + addition
            surplus = surplus - addition
    return np.array(given)


def centred(key, dims, width, reach, cuts=(), held_as=jnp.bfloat16):
    result = width * jax.random.normal(key, dims, jnp.float32)
    if cuts:
        result = result * steps_of(key, dims, cuts, -0.22, 0.18)
    return jnp.clip(result, -reach, reach).astype(held_as)


def setup_inputs(seed: int = 0, part: int = 0) -> dict:
    key_list = jax.random.split(jax.random.key(seed), 16)
    part_splits = jax.random.split(jax.random.fold_in(key_list[15], part), 16)
    queries = draw_queries(jax.random.fold_in(jax.random.fold_in(key_list[15], part), 71), part)
    tree_key_value = centred(part_splits[1], (TREE_TOKENS, 2, KEY_VALUE_HEADS * HEAD_SIZE), 1.0, 6.0, ((0, 16),))
    key_value_cache = draw_key_value_cache(jax.random.fold_in(jax.random.fold_in(key_list[15], part), 71), part)
    lengths = draw_lengths(jax.random.fold_in(jax.random.fold_in(key_list[15], part), 71), part)
    parents = draw_parents(jax.random.fold_in(jax.random.fold_in(key_list[15], part), 71), part)
    residual = centred(part_splits[5], (TREE_TOKENS, D), 1.0, 6.0, ((0, 16),))
    ffn_gain = jnp.clip(1.0 + 0.18 * jax.random.normal(key_list[6], (D,), jnp.float32), 0.099609375, 1.8984375).astype(jnp.bfloat16)
    router = centred(key_list[7], (D, EXPERTS), D ** -0.5, 0.078125)
    routes_keys = jax.random.split(jax.random.fold_in(part_splits[8], 1), TREE_TOKENS // TOK_DEV)
    routes_turns = jax.random.permutation(jax.random.fold_in(part_splits[8], 3), TREE_TOKENS // TOK_DEV)
    routes = jax.vmap(lambda own, number: routed_block(jax.random.fold_in(part_splits[8], 2), own, number, TOK_DEV, EXPERTS, 2, CAP, 2))(routes_keys, routes_turns).reshape((TREE_TOKENS, 2))
    gate_weight = centred(key_list[9], (D, EXPERTS * FF), D ** -0.5, 0.078125, ((1, 16),))
    up_weight = centred(key_list[10], (D, EXPERTS * FF), D ** -0.5, 0.078125, ((1, 16),))
    down_weight = centred(key_list[11], (EXPERTS * FF, D), FF ** -0.5, 0.0625, ((0, 16),))
    accepted = touch_ends(jax.random.randint(part_splits[12], (REQUEST_COUNT,), 0, TREE_NODES), jax.random.fold_in(part_splits[12], 1), 0, TREE_NODES - 1).astype(jnp.int32)
    next_embed = centred(part_splits[13], (REQUEST_COUNT, D), 1.0, 6.0, ((0, 16),))
    draft_fc = centred(key_list[14], (2 * D, D), (2 * D) ** -0.5, 0.0546875, ((0, 16),))
    return dict(queries=queries, tree_key_value=tree_key_value, key_value_cache=key_value_cache, lengths=lengths, parents=parents, residual=residual, ffn_gain=ffn_gain, router=router, routes=routes, gate_weight=gate_weight, up_weight=up_weight, down_weight=down_weight, accepted=accepted, next_embed=next_embed, draft_fc=draft_fc)


EPSILON = 1e-05

def round_trip(values):
    return lax.optimization_barrier(values.astype(jnp.bfloat16)).astype(jnp.float32)

def ancestors(parent_ids):
    node_ids = jnp.arange(TREE_NODES, dtype=jnp.int32)
    parent_map = (parent_ids[:, :, None] == node_ids[None, None, :]).astype(jnp.float32)
    current = jnp.broadcast_to(jnp.eye(TREE_NODES, dtype=jnp.float32), parent_map.shape)
    reached = current
    for repeat in range(TREE_NODES):
        current = jnp.einsum('rij,rjk->rik', current, parent_map, precision=lax.Precision.HIGHEST)
        reached = reached + current
    return reached > 0.5

def attention(queries, tree_key_value, key_value_cache, lengths, parents):
    request_total = lengths.shape[0]
    query_head_count = queries.astype(jnp.float32).reshape(request_total, TREE_NODES, KEY_VALUE_HEADS, QUERY_HEADS // KEY_VALUE_HEADS, HEAD_SIZE)
    cached_key_rows = key_value_cache[:, 0].astype(jnp.float32).reshape(request_total, CACHE_SLOTS, KEY_VALUE_HEADS, HEAD_SIZE)
    cached_value_rows = key_value_cache[:, 1].astype(jnp.float32).reshape(request_total, CACHE_SLOTS, KEY_VALUE_HEADS, HEAD_SIZE)
    tree_key_rows = tree_key_value[:, 0].astype(jnp.float32).reshape(request_total, TREE_NODES, KEY_VALUE_HEADS, HEAD_SIZE)
    tree_value_rows = tree_key_value[:, 1].astype(jnp.float32).reshape(request_total, TREE_NODES, KEY_VALUE_HEADS, HEAD_SIZE)
    score_scale = HEAD_SIZE ** (-0.5)
    cache_scores = jnp.einsum('rtgqd,rlgd->rgtql', query_head_count, cached_key_rows) * score_scale
    tree_scores = jnp.einsum('rtgqd,rugd->rgtqu', query_head_count, tree_key_rows) * score_scale
    visible = jnp.arange(CACHE_SLOTS, dtype=jnp.int32)[None, :] < lengths[:, None]
    related = ancestors(parents.reshape(request_total, TREE_NODES))
    cache_scores = jnp.where(visible[:, None, None, None, :], cache_scores, -1e+30)
    tree_scores = jnp.where(related[:, None, :, None, :], tree_scores, -1e+30)
    row_peak = jnp.maximum(lax.optimization_barrier(jnp.max(cache_scores, axis=-1)), lax.optimization_barrier(jnp.max(tree_scores, axis=-1)))[..., None]
    cache_exp = jnp.exp(cache_scores - row_peak)
    tree_exp = jnp.exp(tree_scores - row_peak)
    denominator = (lax.optimization_barrier(jnp.sum(cache_exp, axis=-1)) + lax.optimization_barrier(jnp.sum(tree_exp, axis=-1)))[..., None]
    cache_weights = round_trip(cache_exp / denominator)
    tree_weights = round_trip(tree_exp / denominator)
    context = jnp.einsum('rgtql,rlgd->rtgqd', cache_weights, cached_value_rows) + jnp.einsum('rgtqu,rugd->rtgqd', tree_weights, tree_value_rows)
    return context.reshape(request_total * TREE_NODES, QUERY_HEADS * HEAD_SIZE)

def reference(queries, tree_key_value, key_value_cache, lengths, parents, residual, ffn_gain, router, routes, gate_weight, up_weight, down_weight, accepted, next_embed, draft_fc):
    context = attention(queries, tree_key_value, key_value_cache, lengths, parents)
    hidden_state = residual.astype(jnp.float32) + context
    normed = (hidden_state * lax.rsqrt(lax.optimization_barrier(jnp.mean(hidden_state * hidden_state, axis=-1, keepdims=True)) + EPSILON) * ffn_gain.astype(jnp.float32)).astype(jnp.bfloat16)
    logits = jnp.dot(normed, router, preferred_element_type=jnp.float32)
    expert_ids = jnp.arange(EXPERTS, dtype=jnp.int32)
    first_hit = (routes[:, 0:1] == expert_ids[None, :]).astype(jnp.float32)
    second_hit = (routes[:, 1:2] == expert_ids[None, :]).astype(jnp.float32)
    first_logit = lax.optimization_barrier(jnp.sum(logits * first_hit, axis=-1))
    second_logit = lax.optimization_barrier(jnp.sum(logits * second_hit, axis=-1))
    first_share = jax.nn.sigmoid(first_logit - second_logit)
    mixing = first_share[:, None] * first_hit + (1.0 - first_share)[:, None] * second_hit
    shard_width = EXPERTS * FF // N_EXPERT
    group_size = N_EXPERT // EXPERTS

    def shard_step(running, shard_index):
        first_col = (shard_index * shard_width).astype(jnp.int32)
        gate_cols = lax.dynamic_slice_in_dim(gate_weight, first_col, shard_width, 1)
        up_cols = lax.dynamic_slice_in_dim(up_weight, first_col, shard_width, 1)
        down_rows = lax.dynamic_slice_in_dim(down_weight, first_col, shard_width, 0)
        gate_val = jnp.dot(normed, gate_cols, preferred_element_type=jnp.float32)
        up_val = jnp.dot(normed, up_cols, preferred_element_type=jnp.float32)
        activation = (jax.nn.silu(gate_val) * up_val).astype(jnp.bfloat16)
        partial_out = round_trip(jnp.dot(activation, down_rows, preferred_element_type=jnp.float32))
        mix_share = lax.dynamic_slice_in_dim(mixing, (shard_index // group_size).astype(jnp.int32), 1, 1)
        return (running + mix_share * partial_out, None)
    shard_ids = jnp.arange(N_EXPERT, dtype=jnp.int32)
    expert_sum, unused = lax.scan(shard_step, jnp.zeros(hidden_state.shape, jnp.float32), shard_ids)
    layer_out = (hidden_state + expert_sum).astype(jnp.bfloat16)
    request_total = lengths.shape[0]
    picker = (accepted[:, None] == jnp.arange(TREE_NODES, dtype=jnp.int32)[None, :]).astype(jnp.float32)
    picked = jnp.einsum('rt,rtd->rd', picker, layer_out.astype(jnp.float32).reshape(request_total, TREE_NODES, D)).astype(jnp.bfloat16)
    draft_in = jnp.concatenate([picked, next_embed], axis=1)
    draft_out = jnp.dot(draft_in, draft_fc, preferred_element_type=jnp.float32).astype(jnp.bfloat16)
    return (layer_out, draft_out)
```

```python
import functools

import jax
import jax.numpy as jnp
from jax import lax
from jax.experimental import pallas as pl
from jax.experimental.pallas import tpu as pltpu
from jax.sharding import PartitionSpec as P

QUERY_HEADS = 48
KEY_VALUE_HEADS = 8
HEAD_SIZE = 128
EXPERTS = 4
TREE_NODES = 6
CACHE_SLOTS = 512
CAP = 4


EPSILON = 1e-05


def related_kernel(parents, out):
    node_ids = lax.broadcasted_iota(jnp.int32, (1, out.shape[2]), 1)
    for request in range(out.shape[0]):
        reached = []
        for node in range(TREE_NODES):
            row = (node_ids == node).astype(jnp.float32)
            parent = parents[request * TREE_NODES + node]
            for earlier in range(node):
                row = row + jnp.where(parent == earlier, reached[earlier], 0.0)
            reached.append(row)
            out[request, node : node + 1, :] = row


def ancestors(parent_ids):
    table = pl.pallas_call(
        related_kernel,
        out_shape=jax.ShapeDtypeStruct((parent_ids.shape[0] // TREE_NODES, TREE_NODES, 128), jnp.float32),
        in_specs=[pl.BlockSpec(memory_space=pltpu.SMEM)],
        out_specs=pl.BlockSpec(memory_space=pltpu.VMEM),
        name="related",
    )(parent_ids)
    return table[:, :, :TREE_NODES] > 0.5


def attention(queries, tree_key_value, key_value_cache, lengths, parents):
    request_total = lengths.shape[0]
    query_head_count = queries.reshape(
        request_total, TREE_NODES, KEY_VALUE_HEADS, QUERY_HEADS // KEY_VALUE_HEADS, HEAD_SIZE
    )
    cached_key_rows = key_value_cache[:, 0].reshape(
        request_total, CACHE_SLOTS, KEY_VALUE_HEADS, HEAD_SIZE
    )
    cached_value_rows = key_value_cache[:, 1].reshape(
        request_total, CACHE_SLOTS, KEY_VALUE_HEADS, HEAD_SIZE
    )
    tree_key_rows = tree_key_value[:, 0].reshape(
        request_total, TREE_NODES, KEY_VALUE_HEADS, HEAD_SIZE
    )
    tree_value_rows = tree_key_value[:, 1].reshape(
        request_total, TREE_NODES, KEY_VALUE_HEADS, HEAD_SIZE
    )
    score_scale = HEAD_SIZE ** (-0.5)
    cache_scores = (
        jnp.einsum(
            "rtgqd,rlgd->rgtql",
            query_head_count,
            cached_key_rows,
            preferred_element_type=jnp.float32,
        )
        * score_scale
    )
    tree_scores = (
        jnp.einsum(
            "rtgqd,rugd->rgtqu", query_head_count, tree_key_rows, preferred_element_type=jnp.float32
        )
        * score_scale
    )
    visible = jnp.arange(CACHE_SLOTS, dtype=jnp.int32)[None, :] < lengths[:, None]
    related = ancestors(parents)
    cache_scores = jnp.where(visible[:, None, None, None, :], cache_scores, -1e30)
    tree_scores = jnp.where(related[:, None, :, None, :], tree_scores, -1e30)
    row_peak = jnp.maximum(jnp.max(cache_scores, axis=-1), jnp.max(tree_scores, axis=-1))[..., None]
    cache_exp = jnp.exp(cache_scores - row_peak)
    tree_exp = jnp.exp(tree_scores - row_peak)
    denominator = (jnp.sum(cache_exp, axis=-1) + jnp.sum(tree_exp, axis=-1))[..., None]
    cache_weights = (cache_exp / denominator).astype(jnp.bfloat16)
    tree_weights = (tree_exp / denominator).astype(jnp.bfloat16)
    context = jnp.einsum(
        "rgtql,rlgd->rtgqd", cache_weights, cached_value_rows, preferred_element_type=jnp.float32
    ) + jnp.einsum(
        "rgtqu,rugd->rtgqd", tree_weights, tree_value_rows, preferred_element_type=jnp.float32
    )
    return context.reshape(request_total * TREE_NODES, QUERY_HEADS * HEAD_SIZE)


VMEM_LIMIT = 66_000_000


def greet(n, me):
    barrier = pltpu.get_barrier_semaphore()

    def hello(k, carry):
        pl.semaphore_signal(barrier, inc=1, device_id={"expert": lax.rem(me + k, n)})
        return carry

    lax.fori_loop(1, n, hello, 0)
    pl.semaphore_wait(barrier, n - 1)


def push(src, dst, send_sem, recv_sem, peer):
    return pltpu.make_async_remote_copy(
        src_ref=src,
        dst_ref=dst,
        send_sem=send_sem,
        recv_sem=recv_sem,
        device_id={"expert": peer},
        device_id_type=pl.DeviceIdType.MESH,
    )


def moe_kernel(
    n,
    group_size,
    pair_slots,
    down_slots,
    packed,
    gate_hbm,
    up_hbm,
    down_hbm,
    grouped,
    gate_buf,
    up_buf,
    down_buf,
    arrived,
    rows_wide,
    rows,
    activation,
    result,
    leaving,
    returned,
    pair_sem,
    down_sem,
    out_sem,
    in_sem,
    back_out_sem,
    back_in_sem,
    own_sem,
):
    me = lax.axis_index("expert")
    width = gate_hbm.shape[1]
    chunk = gate_buf.shape[2]
    pair_count = width // chunk
    piece = down_buf.shape[2]
    piece_count = down_hbm.shape[1] // piece

    def pair_copies(i):
        slot = lax.rem(i, pair_slots)
        cols = pl.ds(pl.multiple_of(i * chunk, chunk), chunk)
        return (
            pltpu.make_async_copy(gate_hbm.at[:, cols], gate_buf.at[slot], pair_sem.at[0, slot]),
            pltpu.make_async_copy(up_hbm.at[:, cols], up_buf.at[slot], pair_sem.at[1, slot]),
        )

    def down_copy(i):
        slot = lax.rem(i, down_slots)
        cols = pl.ds(pl.multiple_of(i * piece, piece), piece)
        return pltpu.make_async_copy(down_hbm.at[:, cols], down_buf.at[slot], down_sem.at[slot])

    def start_pair(i, carry):
        for copy in pair_copies(i):
            copy.start()
        return carry

    def start_down(i, carry):
        down_copy(i).start()
        return carry

    lax.fori_loop(0, pair_slots, start_pair, 0)
    greet(n, me)

    def dispatch(k, carry):
        peer = lax.rem(me + k, n)
        push(
            packed.at[peer // group_size], arrived.at[me], out_sem.at[peer], in_sem.at[me], peer
        ).start()
        return carry

    lax.fori_loop(1, n, dispatch, 0)
    own = pltpu.make_async_copy(packed.at[me // group_size], arrived.at[me], own_sem)
    own.start()
    lax.fori_loop(0, down_slots, start_down, 0)
    own.wait()

    def take(k, carry):
        source = lax.rem(me + n - k, n)
        push(
            packed.at[0], arrived.at[source], out_sem.at[source], in_sem.at[source], source
        ).wait_recv()
        return carry

    lax.fori_loop(1, n, take, 0)

    def both(pair):
        return pl.ds(pl.multiple_of(pair * 2 * CAP, 2 * CAP), 2 * CAP)

    def widen(pair, carry):
        rows_wide[both(pair), :] = jnp.concatenate(
            [arrived[2 * pair].astype(jnp.float32), arrived[2 * pair + 1].astype(jnp.float32)],
            axis=0,
        )
        return carry

    lax.fori_loop(0, n // 2, widen, 0)
    rows[...] = rows_wide[...].astype(jnp.bfloat16)

    def pair_step(i, carry):
        slot = lax.rem(i, pair_slots)
        for copy in pair_copies(i):
            copy.wait()
        gate_val = jnp.dot(rows[...], gate_buf[slot], preferred_element_type=jnp.float32)
        up_val = jnp.dot(rows[...], up_buf[slot], preferred_element_type=jnp.float32)
        cols = pl.ds(pl.multiple_of(i * chunk, chunk), chunk)
        activation[:, cols] = (jax.nn.silu(gate_val) * up_val).astype(jnp.bfloat16)

        @pl.when(i + pair_slots < pair_count)
        def _():
            start_pair(i + pair_slots, 0)

        return carry

    lax.fori_loop(0, pair_count, pair_step, 0)

    def down_step(i, carry):
        slot = lax.rem(i, down_slots)
        down_copy(i).wait()
        result[...] = jnp.dot(
            activation[...], down_buf[slot], preferred_element_type=jnp.float32
        )

        @pl.when(i + down_slots < piece_count)
        def _():
            start_down(i + down_slots, 0)

        def narrow(pair, inner):
            block = result[both(pair), :]
            leaving[2 * pair, i] = block[:CAP].astype(jnp.bfloat16)
            leaving[2 * pair + 1, i] = block[CAP:].astype(jnp.bfloat16)
            return inner

        lax.fori_loop(0, n // 2, narrow, 0)

        def send_back(k, inner):
            peer = lax.rem(me + k, n)
            push(
                leaving.at[peer, i],
                returned.at[me, i],
                back_out_sem.at[peer],
                back_in_sem.at[me],
                peer,
            ).start()
            return inner

        lax.fori_loop(1, n, send_back, 0)
        return carry

    lax.fori_loop(0, piece_count, down_step, 0)
    returned[me] = leaving[me]

    def drain(k, carry):
        peer = lax.rem(me + n - k, n)
        push(
            leaving.at[peer], returned.at[peer], back_out_sem.at[peer], back_in_sem.at[peer], peer
        ).wait()
        push(
            packed.at[0], arrived.at[peer], out_sem.at[peer], in_sem.at[peer], peer
        ).wait_send()
        return carry

    lax.fori_loop(1, n, drain, 0)

    def gather(expert, carry):
        for i in range(piece_count):

            def add(member, total):
                return total + returned[expert * group_size + member, i].astype(jnp.float32)

            grouped[expert, :, i * piece : (i + 1) * piece] = lax.fori_loop(
                0, group_size, add, jnp.zeros((CAP, piece), jnp.float32)
            )
        return carry

    lax.fori_loop(0, EXPERTS, gather, 0)


def moe(packed, gate_weight, up_weight, down_weight, n):
    model_width, width = gate_weight.shape
    row_count = n * CAP
    chunk = min(512, width)
    piece = model_width // 4
    pair_slots = min(3, width // chunk)
    down_slots = min(2, model_width // piece)
    anywhere = pl.BlockSpec(memory_space=pl.ANY)
    whole = pl.BlockSpec(memory_space=pltpu.VMEM)
    bf16, f32 = jnp.bfloat16, jnp.float32
    return pl.pallas_call(
        functools.partial(moe_kernel, n, n // EXPERTS, pair_slots, down_slots),
        out_shape=jax.ShapeDtypeStruct((EXPERTS, CAP, model_width), f32),
        in_specs=[whole, anywhere, anywhere, anywhere],
        out_specs=whole,
        scratch_shapes=[
            pltpu.VMEM((pair_slots, model_width, chunk), bf16),
            pltpu.VMEM((pair_slots, model_width, chunk), bf16),
            pltpu.VMEM((down_slots, width, piece), bf16),
            pltpu.VMEM((n, CAP, model_width), bf16),
            pltpu.VMEM((row_count, model_width), f32),
            pltpu.VMEM((row_count, model_width), bf16),
            pltpu.VMEM((row_count, width), bf16),
            pltpu.VMEM((row_count, piece), f32),
            pltpu.VMEM((n, model_width // piece, CAP, piece), bf16),
            pltpu.VMEM((n, model_width // piece, CAP, piece), bf16),
            pltpu.SemaphoreType.DMA((2, pair_slots)),
            pltpu.SemaphoreType.DMA((down_slots,)),
            pltpu.SemaphoreType.DMA((n,)),
            pltpu.SemaphoreType.DMA((n,)),
            pltpu.SemaphoreType.DMA((n,)),
            pltpu.SemaphoreType.DMA((n,)),
            pltpu.SemaphoreType.DMA,
        ],
        compiler_params=pltpu.CompilerParams(
            collective_id=0, has_side_effects=True, vmem_limit_bytes=VMEM_LIMIT
        ),
        name="moe",
    )(packed, gate_weight, up_weight, down_weight)


def draft_kernel(
    n,
    share,
    piece,
    blocks,
    fc_hbm,
    out,
    fc_buf,
    arrived,
    rows_wide,
    result,
    leaving,
    returned,
    fc_sem,
    out_sem,
    in_sem,
    back_out_sem,
    back_in_sem,
):
    me = lax.axis_index("expert")
    piece_count = fc_hbm.shape[1] // piece
    half = piece // 2

    def fc_copy(i):
        cols = pl.ds(pl.multiple_of(i * piece, piece), piece)
        return pltpu.make_async_copy(fc_hbm.at[:, cols], fc_buf.at[i], fc_sem.at[i])

    def start_fc(i, carry):
        fc_copy(i).start()
        return carry

    lax.fori_loop(0, piece_count, start_fc, 0)
    greet(n, me)

    def dispatch(k, carry):
        peer = lax.rem(me + k, n)
        push(blocks.at[peer], arrived.at[me], out_sem.at[peer], in_sem.at[me], peer).start()
        return carry

    lax.fori_loop(1, n, dispatch, 0)
    rows_wide[pl.ds(me * share, share), :] = blocks[me]

    def take(k, carry):
        source = lax.rem(me + n - k, n)
        push(
            blocks.at[source], arrived.at[source], out_sem.at[source], in_sem.at[source], source
        ).wait()
        rows_wide[pl.ds(source * share, share), :] = arrived[source]
        return carry

    lax.fori_loop(1, n, take, 0)

    def step(i, carry):
        fc_copy(i).wait()
        result[...] = jnp.dot(
            rows_wide[...].astype(jnp.bfloat16), fc_buf[i], preferred_element_type=jnp.float32
        )

        def split(source, inner):
            block = result[pl.ds(source * share, share), :]
            leaving[source, i] = jnp.concatenate(
                [block[:, :half], block[:, half:]], axis=0
            ).astype(jnp.bfloat16)
            return inner

        lax.fori_loop(0, n, split, 0)

        def send_back(k, inner):
            peer = lax.rem(me + k, n)
            push(
                leaving.at[peer, i],
                returned.at[me, i],
                back_out_sem.at[peer],
                back_in_sem.at[me],
                peer,
            ).start()
            return inner

        lax.fori_loop(1, n, send_back, 0)
        return carry

    lax.fori_loop(0, piece_count, step, 0)
    returned[me] = leaving[me]

    def drain(k, carry):
        peer = lax.rem(me + n - k, n)
        push(
            leaving.at[peer], returned.at[peer], back_out_sem.at[peer], back_in_sem.at[peer], peer
        ).wait()
        return carry

    lax.fori_loop(1, n, drain, 0)
    for i in range(piece_count):

        def add(source, total):
            return total + returned[source, i].astype(jnp.float32)

        total = lax.fori_loop(0, n, add, jnp.zeros((2 * share, half), jnp.float32))
        out[:, i * piece : i * piece + half] = total[:share]
        out[:, i * piece + half : (i + 1) * piece] = total[share:]


def draft(blocks, draft_fc):
    n, share, depth = blocks.shape
    model_width = draft_fc.shape[1]
    piece = model_width // 4
    pieces = model_width // piece
    whole = pl.BlockSpec(memory_space=pltpu.VMEM)
    f32 = jnp.float32
    return pl.pallas_call(
        functools.partial(draft_kernel, n, share, piece),
        out_shape=jax.ShapeDtypeStruct((share, model_width), f32),
        in_specs=[whole, pl.BlockSpec(memory_space=pl.ANY)],
        out_specs=whole,
        scratch_shapes=[
            pltpu.VMEM((pieces, depth, piece), jnp.bfloat16),
            pltpu.VMEM((n, share, depth), f32),
            pltpu.VMEM((n * share, depth), f32),
            pltpu.VMEM((n * share, piece), f32),
            pltpu.VMEM((n, pieces, 2 * share, piece // 2), jnp.bfloat16),
            pltpu.VMEM((n, pieces, 2 * share, piece // 2), jnp.bfloat16),
            pltpu.SemaphoreType.DMA((pieces,)),
            pltpu.SemaphoreType.DMA((n,)),
            pltpu.SemaphoreType.DMA((n,)),
            pltpu.SemaphoreType.DMA((n,)),
            pltpu.SemaphoreType.DMA((n,)),
        ],
        compiler_params=pltpu.CompilerParams(
            collective_id=1, has_side_effects=True, vmem_limit_bytes=VMEM_LIMIT
        ),
        name="draft",
    )(blocks, draft_fc)


SLICE = 1024


def greet_all(n, me):
    barrier = pltpu.get_barrier_semaphore()

    def hello(k, carry):
        pl.semaphore_signal(barrier, inc=1, device_id={"expert": lax.rem(me + k, n)})
        return carry

    lax.fori_loop(1, n, hello, 0)
    return barrier


def fused_kernel(
    n,
    slots,
    lengths,
    parents,
    routes,
    accepted,
    queries_hbm,
    tree_hbm,
    cache_hbm,
    residual_hbm,
    gain_hbm,
    router_hbm,
    embed_hbm,
    gate_hbm,
    up_hbm,
    down_hbm,
    fc_hbm,
    layer_out,
    draft_out,
    weights,
    queries,
    tree,
    keys,
    values,
    residual,
    gain,
    router,
    embed,
    tree_rows,
    hidden,
    normed,
    packed,
    arrived,
    rows,
    gate_sum,
    up_sum,
    activation,
    leaving,
    returned,
    home_leaving,
    home_returned,
    picked,
    embed_row,
    blocks,
    block_rows,
    draft_leaving,
    draft_returned,
    load_sem,
    input_sem,
    out_sem,
    in_sem,
    plane_out_sem,
    plane_in_sem,
    back_out_sem,
    back_in_sem,
    home_out_sem,
    home_in_sem,
    block_out_sem,
    block_in_sem,
    draft_out_sem,
    draft_in_sem,
):
    bf16, f32 = jnp.bfloat16, jnp.float32
    me = lax.axis_index("expert")
    group = n // EXPERTS
    mine = me // group
    lane = lax.rem(me, group)
    model_width = down_hbm.shape[1]
    width = down_hbm.shape[0]
    depth = fc_hbm.shape[0]
    chunk_count = model_width // width
    half_count = width // SLICE
    piece_count = model_width // SLICE
    stacked = width // depth
    pair_loads = 2 * chunk_count * half_count
    down_loads = pair_loads + piece_count
    load_count = down_loads + -(-piece_count // stacked)
    block_count = model_width // depth
    half = SLICE // 2
    padded = 8
    share = EXPERTS * CAP
    cache_slots = cache_hbm.shape[2]
    key_rows = keys.shape[0]

    def fc_copy(p):
        i, part = down_loads + p // stacked, p % stacked
        return pltpu.make_async_copy(
            fc_hbm.at[:, p * SLICE : (p + 1) * SLICE],
            weights.at[i % slots, part * depth : (part + 1) * depth, :],
            load_sem.at[i, part],
        )

    def load_copies(i):
        slot = weights.at[i % slots]
        if i < pair_loads:
            source = gate_hbm if i % 2 == 0 else up_hbm
            k, h = i // (2 * half_count), i // 2 % half_count
            view = source.at[k * width : (k + 1) * width, h * SLICE : (h + 1) * SLICE]
            return [pltpu.make_async_copy(view, slot, load_sem.at[i, 0])]
        if i < down_loads:
            p = i - pair_loads
            view = down_hbm.at[:, p * SLICE : (p + 1) * SLICE]
            return [pltpu.make_async_copy(view, slot, load_sem.at[i, 0])]
        first = (i - down_loads) * stacked
        return [fc_copy(p) for p in range(first, min(first + stacked, piece_count))]

    def start_load(i):
        if i < load_count:
            for copy in load_copies(i):
                copy.start()

    inputs = [
        pltpu.make_async_copy(source, target, input_sem.at[i])
        for i, (source, target) in enumerate(
            [
                (queries_hbm, queries),
                (tree_hbm, tree),
                (cache_hbm.at[0, 0], keys.at[0:cache_slots, :]),
                (residual_hbm, residual),
                (cache_hbm.at[0, 1], values.at[0:cache_slots, :]),
                (gain_hbm, gain),
                (router_hbm, router),
                (embed_hbm, embed),
            ]
        )
    ]
    for copy in inputs:
        copy.start()
    for i in range(slots):
        start_load(i)
    barrier = greet_all(n, me)

    row8 = lax.broadcasted_iota(jnp.int32, (padded, 128), 0)
    col8 = lax.broadcasted_iota(jnp.int32, (padded, 128), 1)
    node_ids = lax.broadcasted_iota(jnp.int32, (1, 128), 1)
    reached = []
    related = jnp.zeros((padded, 128), f32)
    for node in range(TREE_NODES):
        row = (node_ids == node).astype(f32)
        parent = parents[node]
        for earlier in range(node):
            row = row + jnp.where(parent == earlier, reached[earlier], 0.0)
        reached.append(row)
        related = related + jnp.where(row8 == node, row, 0.0)
    slot_ids = lax.broadcasted_iota(jnp.int32, (padded, cache_slots), 1)
    bias = jnp.concatenate(
        [
            jnp.where(slot_ids < lengths[0], 0.0, -1e30),
            jnp.where(related > 0.5, 0.0, -1e30),
        ],
        axis=1,
    )
    heads_each = QUERY_HEADS // KEY_VALUE_HEADS
    bias = jnp.concatenate([bias] * heads_each, axis=0)

    def named(choice, token):
        expert = routes[choice, token]
        rank = jnp.int32(0)
        for earlier in range(token):
            for other in range(2):
                rank = rank + jnp.where(routes[other, earlier] == expert, 1, 0)
        return expert, rank

    places = [[named(choice, token) for choice in range(2)] for token in range(TREE_NODES)]

    for copy in inputs[:3]:
        copy.wait()
    tree_rows[...] = jnp.zeros_like(tree_rows)
    for token in range(TREE_NODES):
        both = tree[token].astype(f32)
        tree_rows[0, token : token + 1, :] = both[0:1]
        tree_rows[1, token : token + 1, :] = both[1:2]
    tile = tree_rows.shape[1]
    keys[cache_slots : cache_slots + tile, :] = tree_rows[0].astype(bf16)
    keys[cache_slots + tile :, :] = jnp.zeros((key_rows - cache_slots - tile, keys.shape[1]), bf16)
    values[cache_slots : cache_slots + tile, :] = tree_rows[1].astype(bf16)
    values[cache_slots + tile :, :] = jnp.zeros(
        (key_rows - cache_slots - tile, keys.shape[1]), bf16
    )
    spare = jnp.zeros((padded - TREE_NODES, HEAD_SIZE), f32)
    score_scale = HEAD_SIZE ** (-0.5)
    weights_of = []
    for g in range(KEY_VALUE_HEADS):
        parts = []
        for q in range(heads_each):
            head = g * heads_each + q
            parts.append(queries[:, head * HEAD_SIZE : (head + 1) * HEAD_SIZE].astype(f32))
            parts.append(spare)
        head_queries = jnp.concatenate(parts, axis=0).astype(bf16)
        scores = (
            lax.dot_general(
                head_queries,
                keys[:, g * HEAD_SIZE : (g + 1) * HEAD_SIZE],
                (((1,), (1,)), ((), ())),
                preferred_element_type=f32,
            )
            * score_scale
            + bias
        )
        peak = jnp.max(scores, axis=-1, keepdims=True)
        grown = jnp.exp(scores - peak)
        total = jnp.sum(grown, axis=-1, keepdims=True)
        weights_of.append((grown * (1.0 / total)).astype(bf16))
    for copy in inputs[3:5]:
        copy.wait()
    square = jnp.zeros((padded, HEAD_SIZE), f32)
    for g in range(KEY_VALUE_HEADS):
        context = jnp.dot(
            weights_of[g],
            values[:, g * HEAD_SIZE : (g + 1) * HEAD_SIZE],
            preferred_element_type=f32,
        )
        for q in range(heads_each):
            head = g * heads_each + q
            cols = slice(head * HEAD_SIZE, (head + 1) * HEAD_SIZE)
            state = context[q * padded : (q + 1) * padded] + jnp.concatenate(
                [residual[:, cols].astype(f32), spare], axis=0
            )
            hidden[:, cols] = state
            square = square + state * state
    for copy in inputs[5:]:
        copy.wait()
    level = lax.rsqrt(jnp.sum(square, axis=-1, keepdims=True) / model_width + EPSILON)

    slot_row = lax.broadcasted_iota(jnp.int32, (EXPERTS * padded, padded), 0)
    slot_col = lax.broadcasted_iota(jnp.int32, (EXPERTS * padded, padded), 1)
    placing = jnp.zeros((EXPERTS * padded, padded), f32)
    for token, choices in enumerate(places):
        for expert, rank in choices:
            placing = placing + jnp.where(
                (slot_row == expert * padded + rank) & (slot_col == token), 1.0, 0.0
            )
    placing = placing.astype(bf16)

    pl.semaphore_wait(barrier, n - 1)

    def push(src, dst, send_sem, recv_sem, peer):
        return pltpu.make_async_remote_copy(
            src_ref=src,
            dst_ref=dst,
            send_sem=send_sem,
            recv_sem=recv_sem,
            device_id={"expert": peer},
            device_id_type=pl.DeviceIdType.MESH,
        )

    def to_plane(k, step):
        peer_plane = lax.rem(mine + step, EXPERTS)
        return push(
            packed.at[k, peer_plane],
            arrived.at[k, mine],
            out_sem.at[k, peer_plane],
            in_sem.at[k, mine],
            peer_plane * group + lane,
        )

    def from_plane(k, step):
        source = lax.rem(mine + EXPERTS - step, EXPERTS)
        return push(
            packed.at[k, source],
            arrived.at[k, source],
            out_sem.at[k, source],
            in_sem.at[k, source],
            source * group + lane,
        )

    for k in range(chunk_count):
        cols = slice(k * width, (k + 1) * width)
        normal = (hidden[:, cols] * level * gain[:, cols].astype(f32)).astype(bf16)
        normed[:, cols] = normal
        spread = jnp.dot(placing, normal, preferred_element_type=f32)
        for e in range(EXPERTS):
            packed[k, e] = spread[e * padded : e * padded + CAP].astype(bf16)
        for step in range(1, EXPERTS):
            to_plane(k, step).start()
        arrived[k, mine] = packed[k, mine]

    embed_row[...] = embed[...].astype(f32)

    def block_push(source, j):
        target = blocks.at[me]
        return push(source, target, block_out_sem.at[j], block_in_sem.at[me], j)

    def send_block(row, b, j):
        source = row.at[:, b * depth : (b + 1) * depth]

        @pl.when(me != j)
        def _():
            block_push(source, j).start()

        @pl.when(me == j)
        def _():
            blocks[j] = row[:, b * depth : (b + 1) * depth]

    def wait_block(row, b, j):
        @pl.when(me != j)
        def _():
            block_push(row.at[:, b * depth : (b + 1) * depth], j).wait_send()

    for b in range(block_count):
        send_block(embed_row, b, block_count + b)

    logits = [jnp.zeros((padded, 1), f32) for _ in range(EXPERTS)]
    for k in range(chunk_count):
        cols = slice(k * width, (k + 1) * width)
        normal = normed[:, cols].astype(f32)
        for e in range(EXPERTS):
            logits[e] = logits[e] + jnp.sum(
                normal * router[e : e + 1, cols].astype(f32), axis=-1, keepdims=True
            )
    ids = [jnp.full((padded, 1), -1, jnp.int32) for _ in range(4)]
    token_row = row8[:, 0:1]
    for token, choices in enumerate(places):
        for choice, (expert, rank) in enumerate(choices):
            ids[choice] = jnp.where(token_row == token, expert, ids[choice])
            ids[2 + choice] = jnp.where(token_row == token, expert * CAP + rank, ids[2 + choice])
    first_logit = jnp.zeros((padded, 1), f32)
    second_logit = jnp.zeros((padded, 1), f32)
    for e in range(EXPERTS):
        first_logit = first_logit + jnp.where(ids[0] == e, logits[e], 0.0)
        second_logit = second_logit + jnp.where(ids[1] == e, logits[e], 0.0)
    first_share = jax.nn.sigmoid(first_logit - second_logit)
    share_col = col8[:, :share]
    weighted = jnp.where(share_col == ids[2], first_share, 0.0) + jnp.where(
        share_col == ids[3], 1.0 - first_share, 0.0
    )
    high = weighted.astype(bf16)
    middle = (weighted - high.astype(f32)).astype(bf16)
    low = (weighted - high.astype(f32) - middle.astype(f32)).astype(bf16)
    mixers = jnp.concatenate(
        [high.astype(f32), middle.astype(f32), low.astype(f32)], axis=0
    ).astype(bf16)

    own_rows = pl.ds(pl.multiple_of(lane * share, share), share)

    def in_plane(k, step):
        peer = mine * group + lax.rem(lane + step, group)
        return push(
            rows.at[k, own_rows, :],
            rows.at[k, own_rows, :],
            plane_out_sem.at[k, step],
            plane_in_sem.at[k, step],
            peer,
        )

    def out_of_plane(k, step):
        source = lax.rem(lane + group - step, group)
        block = rows.at[k, pl.ds(pl.multiple_of(source * share, share), share), :]
        return push(
            block,
            block,
            plane_out_sem.at[k, step],
            plane_in_sem.at[k, step],
            mine * group + source,
        )

    for k in range(chunk_count):
        for step in range(1, EXPERTS):
            from_plane(k, step).wait_recv()
        rows[k, own_rows, :] = jnp.concatenate(
            [arrived[k, s].astype(f32) for s in range(EXPERTS)], axis=0
        ).astype(bf16)
        for step in range(1, group):
            in_plane(k, step).start()

    for k in range(chunk_count):
        for step in range(1, group):
            out_of_plane(k, step).wait_recv()
        for h in range(half_count):
            cols = slice(h * SLICE, (h + 1) * SLICE)
            sums = []
            for i, total in ((2 * (k * half_count + h), gate_sum), (2 * (k * half_count + h) + 1, up_sum)):
                for copy in load_copies(i):
                    copy.wait()
                value = jnp.dot(rows[k], weights[i % slots], preferred_element_type=f32)
                if k > 0:
                    value = value + total[:, cols]
                if k < chunk_count - 1:
                    total[:, cols] = value
                sums.append(value)
                start_load(i + slots)
            if k == chunk_count - 1:
                activation[:, cols] = (jax.nn.silu(sums[0]) * sums[1]).astype(bf16)

    def to_owner_lane(p, step):
        peer = lax.rem(lane + step, group)
        return push(
            leaving.at[p, peer],
            returned.at[p, lane],
            back_out_sem.at[p, peer],
            back_in_sem.at[p, lane],
            mine * group + peer,
        )

    def from_member(p, step):
        source = lax.rem(lane + group - step, group)
        return push(
            leaving.at[p, source],
            returned.at[p, source],
            back_out_sem.at[p, source],
            back_in_sem.at[p, source],
            mine * group + source,
        )

    def to_home(p, step):
        plane = lax.rem(mine + step, EXPERTS)
        return push(
            home_leaving.at[p, plane],
            home_returned.at[p, mine],
            home_out_sem.at[p, plane],
            home_in_sem.at[p, mine],
            plane * group + lane,
        )

    def from_expert(p, step):
        plane = lax.rem(mine + EXPERTS - step, EXPERTS)
        return push(
            home_leaving.at[p, plane],
            home_returned.at[p, plane],
            home_out_sem.at[p, plane],
            home_in_sem.at[p, plane],
            plane * group + lane,
        )

    def partial_step(p):
        i = pair_loads + p
        for copy in load_copies(i):
            copy.wait()
        partial = jnp.dot(activation[...], weights[i % slots], preferred_element_type=f32)
        start_load(i + slots)
        for member in range(group):
            leaving[p, member] = partial[member * share : (member + 1) * share].astype(bf16)
        for step in range(1, group):
            to_owner_lane(p, step).start()
        returned[p, lane] = leaving[p, lane]

    def plane_step(p):
        for step in range(1, group):
            from_member(p, step).wait_recv()
        total = returned[p, 0].astype(f32)
        for member in range(1, group):
            total = total + returned[p, member].astype(f32)
        for s in range(EXPERTS):
            home_leaving[p, s] = total[s * CAP : (s + 1) * CAP].astype(bf16)
        for step in range(1, EXPERTS):
            to_home(p, step).start()
        home_returned[p, mine] = home_leaving[p, mine]

    sent = [0]

    def home_step(p):
        for step in range(1, EXPERTS):
            from_expert(p, step).wait_recv()
        cols = slice(p * SLICE, (p + 1) * SLICE)
        block = jnp.concatenate(
            [home_returned[p, e].astype(f32) for e in range(EXPERTS)], axis=0
        ).astype(bf16)
        mixed = jnp.dot(mixers, block, preferred_element_type=f32)
        expert_sum = mixed[:padded] + mixed[padded : 2 * padded] + mixed[2 * padded :]
        result = (hidden[:, cols] + expert_sum).astype(bf16)
        layer_out[:, cols] = result[:TREE_NODES]
        picked[:, cols] = jnp.sum(
            jnp.where(token_row == accepted[0], result.astype(f32), 0.0), axis=0, keepdims=True
        )
        while sent[0] < block_count and (sent[0] + 1) * depth <= (p + 1) * SLICE:
            send_block(picked, sent[0], sent[0])
            sent[0] += 1

    lag_plane, lag_home = 1, 3
    for p in range(piece_count + lag_home):
        if p < piece_count:
            partial_step(p)
        if 0 <= p - lag_plane < piece_count:
            plane_step(p - lag_plane)
        if 0 <= p - lag_home < piece_count:
            home_step(p - lag_home)

    def take(k, carry):
        source = lax.rem(me + n - k, n)
        push(
            blocks.at[source], blocks.at[source], block_out_sem.at[source], block_in_sem.at[source], source
        ).wait_recv()
        block_rows[pl.ds(source, 1), :] = blocks[source]
        return carry

    block_rows[pl.ds(me, 1), :] = blocks[me]
    lax.fori_loop(1, n, take, 0)
    draft_rows = block_rows[...].astype(bf16)
    for p in range(piece_count):
        i = down_loads + p // stacked
        fc_copy(p).wait()
        first = p % stacked * depth
        partial = jnp.dot(
            draft_rows, weights[i % slots, first : first + depth, :], preferred_element_type=f32
        )
        for source in range(n):
            line = partial[source : source + 1]
            draft_leaving[source, p] = jnp.concatenate(
                [line[:, :half], line[:, half:]], axis=0
            ).astype(bf16)

    def send_partial(k, carry):
        peer = lax.rem(me + k, n)
        push(
            draft_leaving.at[peer],
            draft_returned.at[me],
            draft_out_sem.at[peer],
            draft_in_sem.at[me],
            peer,
        ).start()
        return carry

    lax.fori_loop(1, n, send_partial, 0)
    draft_returned[me] = draft_leaving[me]

    def drain(k, carry):
        peer = lax.rem(me + n - k, n)
        push(
            draft_leaving.at[peer],
            draft_returned.at[peer],
            draft_out_sem.at[peer],
            draft_in_sem.at[peer],
            peer,
        ).wait()
        return carry

    lax.fori_loop(1, n, drain, 0)
    for p in range(piece_count):
        total = draft_returned[0, p].astype(f32)
        for source in range(1, n):
            total = total + draft_returned[source, p].astype(f32)
        start = p * SLICE
        draft_out[:, start : start + half] = total[0:1].astype(bf16)
        draft_out[:, start + half : start + SLICE] = total[1:2].astype(bf16)

    for k in range(chunk_count):
        for step in range(1, EXPERTS):
            from_plane(k, step).wait_send()
        for step in range(1, group):
            in_plane(k, step).wait_send()
    for p in range(piece_count):
        for step in range(1, group):
            from_member(p, step).wait_send()
        for step in range(1, EXPERTS):
            from_expert(p, step).wait_send()
    for b in range(block_count):
        wait_block(picked, b, b)
        wait_block(embed_row, b, block_count + b)


def fused(
    queries,
    tree_key_value,
    key_value_cache,
    lengths,
    parents,
    residual,
    ffn_gain,
    router,
    routes,
    gate_weight,
    up_weight,
    down_weight,
    accepted,
    next_embed,
    draft_fc,
    n,
):
    width, model_width = down_weight.shape
    depth = draft_fc.shape[0]
    group = n // EXPERTS
    share = EXPERTS * CAP
    slots = 13
    chunks = model_width // width
    pieces = model_width // SLICE
    stacked = width // depth
    loads = 2 * chunks * (width // SLICE) + pieces + -(-pieces // stacked)
    kv_width = tree_key_value.shape[2]
    key_rows = key_value_cache.shape[2] + 128
    anywhere = pl.BlockSpec(memory_space=pl.ANY)
    scalars = pl.BlockSpec(memory_space=pltpu.SMEM)
    whole = pl.BlockSpec(memory_space=pltpu.VMEM)
    bf16, f32 = jnp.bfloat16, jnp.float32
    dma = pltpu.SemaphoreType.DMA
    return pl.pallas_call(
        functools.partial(fused_kernel, n, slots),
        out_shape=(
            jax.ShapeDtypeStruct((TREE_NODES, model_width), bf16),
            jax.ShapeDtypeStruct((1, model_width), bf16),
        ),
        in_specs=[scalars] * 4 + [anywhere] * 11,
        out_specs=(whole, whole),
        scratch_shapes=[
            pltpu.VMEM((slots, width, SLICE), bf16),
            pltpu.VMEM((TREE_NODES, model_width), bf16),
            pltpu.VMEM((TREE_NODES, 2, kv_width), bf16),
            pltpu.VMEM((key_rows, kv_width), bf16),
            pltpu.VMEM((key_rows, kv_width), bf16),
            pltpu.VMEM((TREE_NODES, model_width), bf16),
            pltpu.VMEM((1, model_width), bf16),
            pltpu.VMEM((EXPERTS, model_width), bf16),
            pltpu.VMEM((1, model_width), bf16),
            pltpu.VMEM((2, 16, kv_width), f32),
            pltpu.VMEM((8, model_width), f32),
            pltpu.VMEM((8, model_width), bf16),
            pltpu.VMEM((chunks, EXPERTS, CAP, width), bf16),
            pltpu.VMEM((chunks, EXPERTS, CAP, width), bf16),
            pltpu.VMEM((chunks, group * share, width), bf16),
            pltpu.VMEM((group * share, width), f32),
            pltpu.VMEM((group * share, width), f32),
            pltpu.VMEM((group * share, width), bf16),
            pltpu.VMEM((pieces, group, share, SLICE), bf16),
            pltpu.VMEM((pieces, group, share, SLICE), bf16),
            pltpu.VMEM((pieces, EXPERTS, CAP, SLICE), bf16),
            pltpu.VMEM((pieces, EXPERTS, CAP, SLICE), bf16),
            pltpu.VMEM((1, model_width), f32),
            pltpu.VMEM((1, model_width), f32),
            pltpu.VMEM((n, 1, depth), f32),
            pltpu.VMEM((n, depth), f32),
            pltpu.VMEM((n, pieces, 2, SLICE // 2), bf16),
            pltpu.VMEM((n, pieces, 2, SLICE // 2), bf16),
            dma((loads, stacked)),
            dma((8,)),
            dma((chunks, EXPERTS)),
            dma((chunks, EXPERTS)),
            dma((chunks, group)),
            dma((chunks, group)),
            dma((pieces, group)),
            dma((pieces, group)),
            dma((pieces, EXPERTS)),
            dma((pieces, EXPERTS)),
            dma((n,)),
            dma((n,)),
            dma((n,)),
            dma((n,)),
        ],
        compiler_params=pltpu.CompilerParams(
            collective_id=0, has_side_effects=True, vmem_limit_bytes=67_000_000
        ),
        name="fused",
    )(
        lengths,
        parents,
        routes.T,
        accepted,
        queries,
        tree_key_value,
        key_value_cache,
        residual,
        ffn_gain.reshape(1, model_width),
        router.T,
        next_embed,
        gate_weight,
        up_weight,
        down_weight,
        draft_fc,
    )


def fits(lengths, gate_weight, draft_fc, n):
    model_width, width = gate_weight.shape
    depth = draft_fc.shape[0]
    return (
        lengths.shape[0] == 1
        and n % EXPERTS == 0
        and width % SLICE == 0
        and model_width % width == 0
        and model_width % SLICE == 0
        and depth % 128 == 0
        and width % depth <= width // 2
        and depth <= width
        and n * depth == 2 * model_width
        and n * CAP <= 128
    )


def per_device(
    queries,
    tree_key_value,
    key_value_cache,
    lengths,
    parents,
    residual,
    ffn_gain,
    router,
    routes,
    gate_weight,
    up_weight,
    down_weight,
    accepted,
    next_embed,
    draft_fc,
):
    devices = lax.axis_size("expert")
    if fits(lengths, gate_weight, draft_fc, devices):
        return fused(
            queries,
            tree_key_value,
            key_value_cache,
            lengths,
            parents,
            residual,
            ffn_gain,
            router,
            routes,
            gate_weight,
            up_weight,
            down_weight,
            accepted,
            next_embed,
            draft_fc,
            devices,
        )
    context = attention(queries, tree_key_value, key_value_cache, lengths, parents)
    hidden_state = residual.astype(jnp.float32) + context
    normed = (
        hidden_state
        * lax.rsqrt(jnp.mean(hidden_state * hidden_state, axis=-1, keepdims=True) + EPSILON)
        * ffn_gain.astype(jnp.float32)
    ).astype(jnp.bfloat16)
    tokens_here, model_width = normed.shape
    logits = jnp.dot(normed, router, preferred_element_type=jnp.float32)
    expert_ids = jnp.arange(EXPERTS, dtype=jnp.int32)
    first_hit = (routes[:, 0:1] == expert_ids[None, :]).astype(jnp.float32)
    second_hit = (routes[:, 1:2] == expert_ids[None, :]).astype(jnp.float32)
    first_logit = jnp.sum(logits * first_hit, axis=-1)
    second_logit = jnp.sum(logits * second_hit, axis=-1)
    first_share = jax.nn.sigmoid(first_logit - second_logit)
    mixing = first_share[:, None] * first_hit + (1.0 - first_share)[:, None] * second_hit
    hit_table = first_hit + second_hit
    slot_rank = jnp.cumsum(hit_table, axis=0) - 1.0
    slot_ids = jnp.arange(CAP, dtype=jnp.float32)
    placing = hit_table.T[:, None, :] * (slot_rank.T[:, None, :] == slot_ids[None, :, None]).astype(
        jnp.float32
    )
    packed = jnp.einsum(
        "ect,td->ecd", placing.astype(jnp.bfloat16), normed, preferred_element_type=jnp.float32
    ).astype(jnp.bfloat16)
    grouped = moe(packed, gate_weight, up_weight, down_weight, devices)
    weighted = placing * mixing.T[:, None, :]
    expert_sum = jnp.einsum("ect,ecd->td", weighted, grouped, precision=lax.Precision.HIGHEST)
    layer_out = (hidden_state + expert_sum).astype(jnp.bfloat16)
    request_total = lengths.shape[0]
    picker = (accepted[:, None] == jnp.arange(TREE_NODES, dtype=jnp.int32)[None, :]).astype(
        jnp.bfloat16
    )
    picked = jnp.einsum(
        "rt,rtd->rd",
        picker,
        layer_out.reshape(request_total, TREE_NODES, model_width),
        preferred_element_type=jnp.float32,
    ).astype(jnp.bfloat16)
    draft_in = jnp.concatenate([picked, next_embed], axis=1)
    depth = draft_fc.shape[0]
    blocks = draft_in.reshape(request_total, devices, depth).transpose(1, 0, 2)
    draft_out = draft(blocks.astype(jnp.float32), draft_fc).astype(jnp.bfloat16)
    return (layer_out, draft_out)


def solution(mesh):
    return jax.shard_map(
        per_device,
        mesh=mesh,
        in_specs=(
            P(("groups", "expert"), None),
            P(("groups", "expert"), None, None),
            P(("groups", "expert"), None, None, None),
            P(("groups", "expert")),
            P(("groups", "expert")),
            P(("groups", "expert"), None),
            P(),
            P(),
            P(("groups", "expert"), None),
            P(None, "expert"),
            P(None, "expert"),
            P("expert", None),
            P(("groups", "expert")),
            P(("groups", "expert"), None),
            P("expert", None),
        ),
        out_specs=(P(("groups", "expert"), None), P(("groups", "expert"), None)),
        check_vma=False,
    )
```

```python
import functools

import jax
import jax.numpy as jnp
from jax import lax
from jax.experimental import pallas as pl
from jax.experimental.pallas import tpu as pltpu
from jax.sharding import PartitionSpec as P

QUERY_HEADS = 48
KEY_VALUE_HEADS = 8
HEAD_SIZE = 128
EXPERTS = 4
TREE_NODES = 6
CACHE_SLOTS = 512
CAP = 4


EPSILON = 1e-05


def related_kernel(parents, out):
    node_ids = lax.broadcasted_iota(jnp.int32, (1, out.shape[2]), 1)
    for request in range(out.shape[0]):
        reached = []
        for node in range(TREE_NODES):
            row = (node_ids == node).astype(jnp.float32)
            parent = parents[request * TREE_NODES + node]
            for earlier in range(node):
                row = row + jnp.where(parent == earlier, reached[earlier], 0.0)
            reached.append(row)
            out[request, node : node + 1, :] = row


def ancestors(parent_ids):
    table = pl.pallas_call(
        related_kernel,
        out_shape=jax.ShapeDtypeStruct((parent_ids.shape[0] // TREE_NODES, TREE_NODES, 128), jnp.float32),
        in_specs=[pl.BlockSpec(memory_space=pltpu.SMEM)],
        out_specs=pl.BlockSpec(memory_space=pltpu.VMEM),
        name="related",
    )(parent_ids)
    return table[:, :, :TREE_NODES] > 0.5


def attention(queries, tree_key_value, key_value_cache, lengths, parents):
    request_total = lengths.shape[0]
    query_head_count = queries.reshape(
        request_total, TREE_NODES, KEY_VALUE_HEADS, QUERY_HEADS // KEY_VALUE_HEADS, HEAD_SIZE
    )
    cached_key_rows = key_value_cache[:, 0].reshape(
        request_total, CACHE_SLOTS, KEY_VALUE_HEADS, HEAD_SIZE
    )
    cached_value_rows = key_value_cache[:, 1].reshape(
        request_total, CACHE_SLOTS, KEY_VALUE_HEADS, HEAD_SIZE
    )
    tree_key_rows = tree_key_value[:, 0].reshape(
        request_total, TREE_NODES, KEY_VALUE_HEADS, HEAD_SIZE
    )
    tree_value_rows = tree_key_value[:, 1].reshape(
        request_total, TREE_NODES, KEY_VALUE_HEADS, HEAD_SIZE
    )
    score_scale = HEAD_SIZE ** (-0.5)
    cache_scores = (
        jnp.einsum(
            "rtgqd,rlgd->rgtql",
            query_head_count,
            cached_key_rows,
            preferred_element_type=jnp.float32,
        )
        * score_scale
    )
    tree_scores = (
        jnp.einsum(
            "rtgqd,rugd->rgtqu", query_head_count, tree_key_rows, preferred_element_type=jnp.float32
        )
        * score_scale
    )
    visible = jnp.arange(CACHE_SLOTS, dtype=jnp.int32)[None, :] < lengths[:, None]
    related = ancestors(parents)
    cache_scores = jnp.where(visible[:, None, None, None, :], cache_scores, -1e30)
    tree_scores = jnp.where(related[:, None, :, None, :], tree_scores, -1e30)
    row_peak = jnp.maximum(jnp.max(cache_scores, axis=-1), jnp.max(tree_scores, axis=-1))[..., None]
    cache_exp = jnp.exp(cache_scores - row_peak)
    tree_exp = jnp.exp(tree_scores - row_peak)
    denominator = (jnp.sum(cache_exp, axis=-1) + jnp.sum(tree_exp, axis=-1))[..., None]
    cache_weights = (cache_exp / denominator).astype(jnp.bfloat16)
    tree_weights = (tree_exp / denominator).astype(jnp.bfloat16)
    context = jnp.einsum(
        "rgtql,rlgd->rtgqd", cache_weights, cached_value_rows, preferred_element_type=jnp.float32
    ) + jnp.einsum(
        "rgtqu,rugd->rtgqd", tree_weights, tree_value_rows, preferred_element_type=jnp.float32
    )
    return context.reshape(request_total * TREE_NODES, QUERY_HEADS * HEAD_SIZE)


VMEM_LIMIT = 66_000_000


def greet(n, me):
    barrier = pltpu.get_barrier_semaphore()

    def hello(k, carry):
        pl.semaphore_signal(barrier, inc=1, device_id={"expert": lax.rem(me + k, n)})
        return carry

    lax.fori_loop(1, n, hello, 0)
    pl.semaphore_wait(barrier, n - 1)


def push(src, dst, send_sem, recv_sem, peer):
    return pltpu.make_async_remote_copy(
        src_ref=src,
        dst_ref=dst,
        send_sem=send_sem,
        recv_sem=recv_sem,
        device_id={"expert": peer},
        device_id_type=pl.DeviceIdType.MESH,
    )


def moe_kernel(
    n,
    group_size,
    pair_slots,
    down_slots,
    packed,
    gate_hbm,
    up_hbm,
    down_hbm,
    grouped,
    gate_buf,
    up_buf,
    down_buf,
    arrived,
    rows_wide,
    rows,
    activation,
    result,
    leaving,
    returned,
    pair_sem,
    down_sem,
    out_sem,
    in_sem,
    back_out_sem,
    back_in_sem,
    own_sem,
):
    me = lax.axis_index("expert")
    width = gate_hbm.shape[1]
    chunk = gate_buf.shape[2]
    pair_count = width // chunk
    piece = down_buf.shape[2]
    piece_count = down_hbm.shape[1] // piece

    def pair_copies(i):
        slot = lax.rem(i, pair_slots)
        cols = pl.ds(pl.multiple_of(i * chunk, chunk), chunk)
        return (
            pltpu.make_async_copy(gate_hbm.at[:, cols], gate_buf.at[slot], pair_sem.at[0, slot]),
            pltpu.make_async_copy(up_hbm.at[:, cols], up_buf.at[slot], pair_sem.at[1, slot]),
        )

    def down_copy(i):
        slot = lax.rem(i, down_slots)
        cols = pl.ds(pl.multiple_of(i * piece, piece), piece)
        return pltpu.make_async_copy(down_hbm.at[:, cols], down_buf.at[slot], down_sem.at[slot])

    def start_pair(i, carry):
        for copy in pair_copies(i):
            copy.start()
        return carry

    def start_down(i, carry):
        down_copy(i).start()
        return carry

    lax.fori_loop(0, pair_slots, start_pair, 0)
    greet(n, me)

    def dispatch(k, carry):
        peer = lax.rem(me + k, n)
        push(
            packed.at[peer // group_size], arrived.at[me], out_sem.at[peer], in_sem.at[me], peer
        ).start()
        return carry

    lax.fori_loop(1, n, dispatch, 0)
    own = pltpu.make_async_copy(packed.at[me // group_size], arrived.at[me], own_sem)
    own.start()
    lax.fori_loop(0, down_slots, start_down, 0)
    own.wait()

    def take(k, carry):
        source = lax.rem(me + n - k, n)
        push(
            packed.at[0], arrived.at[source], out_sem.at[source], in_sem.at[source], source
        ).wait_recv()
        return carry

    lax.fori_loop(1, n, take, 0)

    def both(pair):
        return pl.ds(pl.multiple_of(pair * 2 * CAP, 2 * CAP), 2 * CAP)

    def widen(pair, carry):
        rows_wide[both(pair), :] = jnp.concatenate(
            [arrived[2 * pair].astype(jnp.float32), arrived[2 * pair + 1].astype(jnp.float32)],
            axis=0,
        )
        return carry

    lax.fori_loop(0, n // 2, widen, 0)
    rows[...] = rows_wide[...].astype(jnp.bfloat16)

    def pair_step(i, carry):
        slot = lax.rem(i, pair_slots)
        for copy in pair_copies(i):
            copy.wait()
        gate_val = jnp.dot(rows[...], gate_buf[slot], preferred_element_type=jnp.float32)
        up_val = jnp.dot(rows[...], up_buf[slot], preferred_element_type=jnp.float32)
        cols = pl.ds(pl.multiple_of(i * chunk, chunk), chunk)
        activation[:, cols] = (jax.nn.silu(gate_val) * up_val).astype(jnp.bfloat16)

        @pl.when(i + pair_slots < pair_count)
        def _():
            start_pair(i + pair_slots, 0)

        return carry

    lax.fori_loop(0, pair_count, pair_step, 0)

    def down_step(i, carry):
        slot = lax.rem(i, down_slots)
        down_copy(i).wait()
        result[...] = jnp.dot(
            activation[...], down_buf[slot], preferred_element_type=jnp.float32
        )

        @pl.when(i + down_slots < piece_count)
        def _():
            start_down(i + down_slots, 0)

        def narrow(pair, inner):
            block = result[both(pair), :]
            leaving[2 * pair, i] = block[:CAP].astype(jnp.bfloat16)
            leaving[2 * pair + 1, i] = block[CAP:].astype(jnp.bfloat16)
            return inner

        lax.fori_loop(0, n // 2, narrow, 0)

        def send_back(k, inner):
            peer = lax.rem(me + k, n)
            push(
                leaving.at[peer, i],
                returned.at[me, i],
                back_out_sem.at[peer],
                back_in_sem.at[me],
                peer,
            ).start()
            return inner

        lax.fori_loop(1, n, send_back, 0)
        return carry

    lax.fori_loop(0, piece_count, down_step, 0)
    returned[me] = leaving[me]

    def drain(k, carry):
        peer = lax.rem(me + n - k, n)
        push(
            leaving.at[peer], returned.at[peer], back_out_sem.at[peer], back_in_sem.at[peer], peer
        ).wait()
        push(
            packed.at[0], arrived.at[peer], out_sem.at[peer], in_sem.at[peer], peer
        ).wait_send()
        return carry

    lax.fori_loop(1, n, drain, 0)

    def gather(expert, carry):
        for i in range(piece_count):

            def add(member, total):
                return total + returned[expert * group_size + member, i].astype(jnp.float32)

            grouped[expert, :, i * piece : (i + 1) * piece] = lax.fori_loop(
                0, group_size, add, jnp.zeros((CAP, piece), jnp.float32)
            )
        return carry

    lax.fori_loop(0, EXPERTS, gather, 0)


def moe(packed, gate_weight, up_weight, down_weight, n):
    model_width, width = gate_weight.shape
    row_count = n * CAP
    chunk = min(512, width)
    piece = model_width // 4
    pair_slots = min(3, width // chunk)
    down_slots = min(2, model_width // piece)
    anywhere = pl.BlockSpec(memory_space=pl.ANY)
    whole = pl.BlockSpec(memory_space=pltpu.VMEM)
    bf16, f32 = jnp.bfloat16, jnp.float32
    return pl.pallas_call(
        functools.partial(moe_kernel, n, n // EXPERTS, pair_slots, down_slots),
        out_shape=jax.ShapeDtypeStruct((EXPERTS, CAP, model_width), f32),
        in_specs=[whole, anywhere, anywhere, anywhere],
        out_specs=whole,
        scratch_shapes=[
            pltpu.VMEM((pair_slots, model_width, chunk), bf16),
            pltpu.VMEM((pair_slots, model_width, chunk), bf16),
            pltpu.VMEM((down_slots, width, piece), bf16),
            pltpu.VMEM((n, CAP, model_width), bf16),
            pltpu.VMEM((row_count, model_width), f32),
            pltpu.VMEM((row_count, model_width), bf16),
            pltpu.VMEM((row_count, width), bf16),
            pltpu.VMEM((row_count, piece), f32),
            pltpu.VMEM((n, model_width // piece, CAP, piece), bf16),
            pltpu.VMEM((n, model_width // piece, CAP, piece), bf16),
            pltpu.SemaphoreType.DMA((2, pair_slots)),
            pltpu.SemaphoreType.DMA((down_slots,)),
            pltpu.SemaphoreType.DMA((n,)),
            pltpu.SemaphoreType.DMA((n,)),
            pltpu.SemaphoreType.DMA((n,)),
            pltpu.SemaphoreType.DMA((n,)),
            pltpu.SemaphoreType.DMA,
        ],
        compiler_params=pltpu.CompilerParams(
            collective_id=0, has_side_effects=True, vmem_limit_bytes=VMEM_LIMIT
        ),
        name="moe",
    )(packed, gate_weight, up_weight, down_weight)


def draft_kernel(
    n,
    share,
    piece,
    blocks,
    fc_hbm,
    out,
    fc_buf,
    arrived,
    rows_wide,
    result,
    leaving,
    returned,
    fc_sem,
    out_sem,
    in_sem,
    back_out_sem,
    back_in_sem,
):
    me = lax.axis_index("expert")
    piece_count = fc_hbm.shape[1] // piece
    half = piece // 2

    def fc_copy(i):
        cols = pl.ds(pl.multiple_of(i * piece, piece), piece)
        return pltpu.make_async_copy(fc_hbm.at[:, cols], fc_buf.at[i], fc_sem.at[i])

    def start_fc(i, carry):
        fc_copy(i).start()
        return carry

    lax.fori_loop(0, piece_count, start_fc, 0)
    greet(n, me)

    def dispatch(k, carry):
        peer = lax.rem(me + k, n)
        push(blocks.at[peer], arrived.at[me], out_sem.at[peer], in_sem.at[me], peer).start()
        return carry

    lax.fori_loop(1, n, dispatch, 0)
    rows_wide[pl.ds(me * share, share), :] = blocks[me]

    def take(k, carry):
        source = lax.rem(me + n - k, n)
        push(
            blocks.at[source], arrived.at[source], out_sem.at[source], in_sem.at[source], source
        ).wait()
        rows_wide[pl.ds(source * share, share), :] = arrived[source]
        return carry

    lax.fori_loop(1, n, take, 0)

    def step(i, carry):
        fc_copy(i).wait()
        result[...] = jnp.dot(
            rows_wide[...].astype(jnp.bfloat16), fc_buf[i], preferred_element_type=jnp.float32
        )

        def split(source, inner):
            block = result[pl.ds(source * share, share), :]
            leaving[source, i] = jnp.concatenate(
                [block[:, :half], block[:, half:]], axis=0
            ).astype(jnp.bfloat16)
            return inner

        lax.fori_loop(0, n, split, 0)

        def send_back(k, inner):
            peer = lax.rem(me + k, n)
            push(
                leaving.at[peer, i],
                returned.at[me, i],
                back_out_sem.at[peer],
                back_in_sem.at[me],
                peer,
            ).start()
            return inner

        lax.fori_loop(1, n, send_back, 0)
        return carry

    lax.fori_loop(0, piece_count, step, 0)
    returned[me] = leaving[me]

    def drain(k, carry):
        peer = lax.rem(me + n - k, n)
        push(
            leaving.at[peer], returned.at[peer], back_out_sem.at[peer], back_in_sem.at[peer], peer
        ).wait()
        return carry

    lax.fori_loop(1, n, drain, 0)
    for i in range(piece_count):

        def add(source, total):
            return total + returned[source, i].astype(jnp.float32)

        total = lax.fori_loop(0, n, add, jnp.zeros((2 * share, half), jnp.float32))
        out[:, i * piece : i * piece + half] = total[:share]
        out[:, i * piece + half : (i + 1) * piece] = total[share:]


def draft(blocks, draft_fc):
    n, share, depth = blocks.shape
    model_width = draft_fc.shape[1]
    piece = model_width // 4
    pieces = model_width // piece
    whole = pl.BlockSpec(memory_space=pltpu.VMEM)
    f32 = jnp.float32
    return pl.pallas_call(
        functools.partial(draft_kernel, n, share, piece),
        out_shape=jax.ShapeDtypeStruct((share, model_width), f32),
        in_specs=[whole, pl.BlockSpec(memory_space=pl.ANY)],
        out_specs=whole,
        scratch_shapes=[
            pltpu.VMEM((pieces, depth, piece), jnp.bfloat16),
            pltpu.VMEM((n, share, depth), f32),
            pltpu.VMEM((n * share, depth), f32),
            pltpu.VMEM((n * share, piece), f32),
            pltpu.VMEM((n, pieces, 2 * share, piece // 2), jnp.bfloat16),
            pltpu.VMEM((n, pieces, 2 * share, piece // 2), jnp.bfloat16),
            pltpu.SemaphoreType.DMA((pieces,)),
            pltpu.SemaphoreType.DMA((n,)),
            pltpu.SemaphoreType.DMA((n,)),
            pltpu.SemaphoreType.DMA((n,)),
            pltpu.SemaphoreType.DMA((n,)),
        ],
        compiler_params=pltpu.CompilerParams(
            collective_id=1, has_side_effects=True, vmem_limit_bytes=VMEM_LIMIT
        ),
        name="draft",
    )(blocks, draft_fc)


SLICE = 1024
LANES = 128


def greet_all(n, me):
    barrier = pltpu.get_barrier_semaphore()

    def hello(k, carry):
        pl.semaphore_signal(barrier, inc=1, device_id={"expert": lax.rem(me + k, n)})
        return carry

    lax.fori_loop(1, n, hello, 0)
    return barrier


def fused_kernel(
    n,
    slots,
    lengths,
    parents,
    routes,
    accepted,
    queries_hbm,
    tree_hbm,
    cache_hbm,
    residual_hbm,
    gain_hbm,
    router_hbm,
    embed_hbm,
    gate_hbm,
    up_hbm,
    down_hbm,
    fc_hbm,
    layer_out,
    draft_out,
    weights,
    queries,
    tree,
    keys,
    values,
    residual,
    gain,
    router,
    embed,
    tree_rows,
    hidden,
    normed,
    packed,
    arrived,
    rows,
    gate_sum,
    up_sum,
    activation,
    kept,
    leaving,
    returned,
    chip_sum,
    chip_leaving,
    chip_returned,
    home_leaving,
    home_returned,
    picked,
    embed_row,
    blocks,
    block_rows,
    draft_wide,
    draft_leaving,
    draft_returned,
    load_sem,
    input_sem,
    out_sem,
    in_sem,
    plane_out_sem,
    plane_in_sem,
    core_out_sem,
    core_in_sem,
    chip_out_sem,
    chip_in_sem,
    home_out_sem,
    home_in_sem,
    block_out_sem,
    block_in_sem,
    draft_out_sem,
    draft_in_sem,
):
    bf16, f32 = jnp.bfloat16, jnp.float32
    me = lax.axis_index("expert")
    group = n // EXPERTS
    mine = me // group
    lane = lax.rem(me, group)
    core = lax.rem(lane, 2)
    across = lane // 2
    core_peer = mine * group + across * 2 + (1 - core)
    chip_peer = mine * group + (1 - across) * 2 + core
    model_width = down_hbm.shape[1]
    width = down_hbm.shape[0]
    depth = fc_hbm.shape[0]
    chunk_count = model_width // SLICE
    half_count = width // SLICE
    piece_count = model_width // SLICE
    block_count = model_width // depth
    padded = 8
    share = EXPERTS * CAP
    cache_slots = cache_hbm.shape[2]
    key_rows = keys.shape[0]
    line_count = model_width // LANES
    lines = SLICE // LANES
    part_count = draft_leaving.shape[0]

    pairs = [
        ("pair", k, h, i) for k in range(chunk_count) for h in range(half_count) for i in range(2)
    ]
    downs = [("down", p, a) for p in range(piece_count) for a in range(half_count)]
    fcs = [("fc", p) for p in range(piece_count)]
    early = len(downs) // 2
    order = pairs + downs[:early] + fcs + downs[early:]
    place = {item: i for i, item in enumerate(order)}

    def load_copy(item):
        i = place[item]
        slot = weights.at[i % slots]
        if item[0] == "pair":
            k, h = item[1], item[2]
            source = (gate_hbm, up_hbm)[item[3]]
            view = source.at[k * SLICE : (k + 1) * SLICE, h * SLICE : (h + 1) * SLICE]
        elif item[0] == "down":
            p, a = item[1], item[2]
            view = down_hbm.at[a * SLICE : (a + 1) * SLICE, p * SLICE : (p + 1) * SLICE]
        else:
            p = item[1]
            view = fc_hbm.at[:, p * SLICE : (p + 1) * SLICE]
            slot = weights.at[i % slots, 0:depth, :]
        return pltpu.make_async_copy(view, slot, load_sem.at[i])

    def start_load(i):
        if i < len(order):
            load_copy(order[i]).start()

    inputs = [
        pltpu.make_async_copy(source, target, input_sem.at[i])
        for i, (source, target) in enumerate(
            [
                (queries_hbm, queries),
                (tree_hbm, tree),
                (cache_hbm.at[0, 0], keys.at[0:cache_slots, :]),
                (residual_hbm, residual),
                (cache_hbm.at[0, 1], values.at[0:cache_slots, :]),
                (gain_hbm, gain),
                (router_hbm, router),
                (embed_hbm, embed),
            ]
        )
    ]
    for copy in inputs:
        copy.start()
    barrier = greet_all(n, me)

    row8 = lax.broadcasted_iota(jnp.int32, (padded, LANES), 0)
    col8 = lax.broadcasted_iota(jnp.int32, (padded, LANES), 1)
    node_ids = lax.broadcasted_iota(jnp.int32, (1, LANES), 1)
    reached = []
    related = jnp.zeros((padded, LANES), f32)
    for node in range(TREE_NODES):
        row = (node_ids == node).astype(f32)
        parent = parents[node]
        for earlier in range(node):
            row = row + jnp.where(parent == earlier, reached[earlier], 0.0)
        reached.append(row)
        related = related + jnp.where(row8 == node, row, 0.0)
    slot_ids = lax.broadcasted_iota(jnp.int32, (padded, cache_slots), 1)
    bias = jnp.concatenate(
        [
            jnp.where(slot_ids < lengths[0], 0.0, -1e30),
            jnp.where(related > 0.5, 0.0, -1e30),
        ],
        axis=1,
    )
    heads_each = QUERY_HEADS // KEY_VALUE_HEADS
    bias = jnp.concatenate([bias] * heads_each, axis=0)

    def named(choice, token):
        expert = routes[choice, token]
        rank = jnp.int32(0)
        for earlier in range(token):
            for other in range(2):
                rank = rank + jnp.where(routes[other, earlier] == expert, 1, 0)
        return expert, rank

    places = [[named(choice, token) for choice in range(2)] for token in range(TREE_NODES)]

    for copy in inputs[:3]:
        copy.wait()
    for i in range(slots):
        start_load(i)
    tree_rows[...] = jnp.zeros_like(tree_rows)
    for token in range(TREE_NODES):
        both = tree[token].astype(f32)
        tree_rows[0, token : token + 1, :] = both[0:1]
        tree_rows[1, token : token + 1, :] = both[1:2]
    tile = tree_rows.shape[1]
    blank = jnp.zeros((key_rows - cache_slots - tile, keys.shape[1]), bf16)
    keys[cache_slots : cache_slots + tile, :] = tree_rows[0].astype(bf16)
    keys[cache_slots + tile :, :] = blank
    values[cache_slots : cache_slots + tile, :] = tree_rows[1].astype(bf16)
    values[cache_slots + tile :, :] = blank
    spare = jnp.zeros((padded - TREE_NODES, HEAD_SIZE), f32)
    score_scale = HEAD_SIZE ** (-0.5)
    weights_of = []
    for g in range(KEY_VALUE_HEADS):
        parts = []
        for q in range(heads_each):
            head = g * heads_each + q
            parts.append(queries[:, head * HEAD_SIZE : (head + 1) * HEAD_SIZE].astype(f32))
            parts.append(spare)
        head_queries = jnp.concatenate(parts, axis=0).astype(bf16)
        scores = (
            lax.dot_general(
                head_queries,
                keys[:, g * HEAD_SIZE : (g + 1) * HEAD_SIZE],
                (((1,), (1,)), ((), ())),
                preferred_element_type=f32,
            )
            * score_scale
            + bias
        )
        peak = jnp.max(scores, axis=-1, keepdims=True)
        grown = jnp.exp(scores - peak)
        total = jnp.sum(grown, axis=-1, keepdims=True)
        weights_of.append((grown * (1.0 / total)).astype(bf16))
    for copy in inputs[3:5]:
        copy.wait()
    square = jnp.zeros((padded, HEAD_SIZE), f32)
    for g in range(KEY_VALUE_HEADS):
        context = jnp.dot(
            weights_of[g],
            values[:, g * HEAD_SIZE : (g + 1) * HEAD_SIZE],
            preferred_element_type=f32,
        )
        for q in range(heads_each):
            head = g * heads_each + q
            cols = slice(head * HEAD_SIZE, (head + 1) * HEAD_SIZE)
            state = context[q * padded : (q + 1) * padded] + jnp.concatenate(
                [residual[:, cols].astype(f32), spare], axis=0
            )
            hidden[:, cols] = state
            square = square + state * state
    for copy in inputs[5:]:
        copy.wait()
    level = lax.rsqrt(jnp.sum(square, axis=-1, keepdims=True) / model_width + EPSILON)

    slot_row = lax.broadcasted_iota(jnp.int32, (EXPERTS * padded, padded), 0)
    slot_col = lax.broadcasted_iota(jnp.int32, (EXPERTS * padded, padded), 1)
    placing = jnp.zeros((EXPERTS * padded, padded), f32)
    for token, choices in enumerate(places):
        for expert, rank in choices:
            placing = placing + jnp.where(
                (slot_row == expert * padded + rank) & (slot_col == token), 1.0, 0.0
            )
    placing = placing.astype(bf16)

    pl.semaphore_wait(barrier, n - 1)

    def to_plane(k, step):
        plane = lax.rem(mine + step, EXPERTS)
        return push(
            packed.at[k, plane],
            arrived.at[k, mine],
            out_sem.at[k, plane],
            in_sem.at[k, mine],
            plane * group + lane,
        )

    def from_plane(k, step):
        plane = lax.rem(mine + EXPERTS - step, EXPERTS)
        return push(
            packed.at[k, plane],
            arrived.at[k, plane],
            out_sem.at[k, plane],
            in_sem.at[k, plane],
            plane * group + lane,
        )

    for k in range(chunk_count):
        cols = slice(k * SLICE, (k + 1) * SLICE)
        gains = [gain[k * lines + t : k * lines + t + 1, :].astype(f32) for t in range(lines)]
        normal = (hidden[:, cols] * level * jnp.concatenate(gains, axis=1)).astype(bf16)
        normed[:, cols] = normal
        spread = jnp.dot(placing, normal, preferred_element_type=f32)
        for e in range(EXPERTS):
            packed[k, e] = spread[e * padded : e * padded + CAP].astype(bf16)
        for step in range(1, EXPERTS):
            to_plane(k, step).start()
        arrived[k, mine] = packed[k, mine]

    embed_row[...] = embed[...].astype(f32)

    def block_push(row, b, j):
        source = row.at[:, b * depth : (b + 1) * depth]
        return push(source, blocks.at[me], block_out_sem.at[j], block_in_sem.at[me], j)

    def send_block(row, b, j):
        @pl.when(me != j)
        def _():
            block_push(row, b, j).start()

        @pl.when(me == j)
        def _():
            blocks[j] = row[:, b * depth : (b + 1) * depth]

    def wait_block(row, b, j):
        @pl.when(me != j)
        def _():
            block_push(row, b, j).wait_send()

    for b in range(block_count):
        send_block(embed_row, b, block_count + b)

    logits = [jnp.zeros((padded, 1), f32) for _ in range(EXPERTS)]
    for k in range(chunk_count):
        cols = slice(k * SLICE, (k + 1) * SLICE)
        normal = normed[:, cols].astype(f32)
        for e in range(EXPERTS):
            logits[e] = logits[e] + jnp.sum(
                normal * router[e : e + 1, cols].astype(f32), axis=-1, keepdims=True
            )
    ids = [jnp.full((padded, 1), -1, jnp.int32) for _ in range(4)]
    token_row = row8[:, 0:1]
    for token, choices in enumerate(places):
        for choice, (expert, rank) in enumerate(choices):
            ids[choice] = jnp.where(token_row == token, expert, ids[choice])
            ids[2 + choice] = jnp.where(token_row == token, expert * CAP + rank, ids[2 + choice])
    first_logit = jnp.zeros((padded, 1), f32)
    second_logit = jnp.zeros((padded, 1), f32)
    for e in range(EXPERTS):
        first_logit = first_logit + jnp.where(ids[0] == e, logits[e], 0.0)
        second_logit = second_logit + jnp.where(ids[1] == e, logits[e], 0.0)
    first_share = jax.nn.sigmoid(first_logit - second_logit)
    share_col = col8[:, :share]
    weighted = jnp.where(share_col == ids[2], first_share, 0.0) + jnp.where(
        share_col == ids[3], 1.0 - first_share, 0.0
    )
    high = weighted.astype(bf16).astype(f32)
    middle = (weighted - high).astype(bf16).astype(f32)
    low = weighted - high - middle
    mixers = jnp.concatenate([high, middle, low], axis=0).astype(bf16)

    def lane_rows(k, which):
        return rows.at[k, pl.ds(pl.multiple_of(which * share, share), share), :]

    def row_push(k, which, sem, peer):
        block = lane_rows(k, which)
        return push(block, block, plane_out_sem.at[k, sem], plane_in_sem.at[k, sem], peer)

    chip_lane = (1 - across) * 2 + core
    core_lane = across * 2 + (1 - core)
    far_lane = (1 - across) * 2 + (1 - core)

    def gather_step(k):
        for step in range(1, EXPERTS):
            from_plane(k, step).wait_recv()
        rows[k, pl.ds(pl.multiple_of(lane * share, share), share), :] = jnp.concatenate(
            [arrived[k, s].astype(f32) for s in range(EXPERTS)], axis=0
        ).astype(bf16)
        row_push(k, lane, 0, chip_peer).start()
        row_push(k, lane, 1, core_peer).start()

    def forward_step(k):
        row_push(k, chip_lane, 0, chip_peer).wait_recv()
        row_push(k, chip_lane, 2, core_peer).start()

    def expert_step(k):
        row_push(k, core_lane, 1, core_peer).wait_recv()
        row_push(k, far_lane, 2, core_peer).wait_recv()
        for h in range(half_count):
            cols = slice(h * SLICE, (h + 1) * SLICE)
            sums = []
            for i, total in ((0, gate_sum), (1, up_sum)):
                item = ("pair", k, h, i)
                load_copy(item).wait()
                value = jnp.dot(
                    rows[k], weights[place[item] % slots], preferred_element_type=f32
                )
                if k > 0:
                    value = value + total[:, cols]
                if k < chunk_count - 1:
                    total[:, cols] = value
                sums.append(value)
                start_load(place[item] + slots)
            if k == chunk_count - 1:
                activation[h] = (jax.nn.silu(sums[0]) * sums[1]).astype(bf16)

    for t in range(chunk_count + 6):
        if t < chunk_count:
            gather_step(t)
        if 0 <= t - 2 < chunk_count:
            forward_step(t - 2)
        if 0 <= t - 3 < chunk_count:
            expert_step(t - 3)

    def core_push(p):
        return push(
            leaving.at[p], returned.at[p], core_out_sem.at[p], core_in_sem.at[p], core_peer
        )

    def chip_push(p):
        return push(
            chip_leaving.at[p],
            chip_returned.at[p],
            chip_out_sem.at[p],
            chip_in_sem.at[p],
            chip_peer,
        )

    def to_home(p, step):
        plane = lax.rem(mine + step, EXPERTS)
        return push(
            home_leaving.at[p, plane],
            home_returned.at[p, mine],
            home_out_sem.at[p, plane],
            home_in_sem.at[p, mine],
            plane * group + lane,
        )

    def from_expert(p, step):
        plane = lax.rem(mine + EXPERTS - step, EXPERTS)
        return push(
            home_leaving.at[p, plane],
            home_returned.at[p, plane],
            home_out_sem.at[p, plane],
            home_in_sem.at[p, plane],
            plane * group + lane,
        )

    def partial_step(p):
        partial = None
        for a in range(half_count):
            item = ("down", p, a)
            load_copy(item).wait()
            value = jnp.dot(
                activation[a], weights[place[item] % slots], preferred_element_type=f32
            )
            partial = value if partial is None else partial + value
            start_load(place[item] + slots)
        for member in range(group):
            block = partial[member * share : (member + 1) * share].astype(bf16)
            a, c = member // 2, member % 2

            @pl.when(core == c)
            def _():
                kept[p, a] = block

            @pl.when(core != c)
            def _():
                leaving[p, a] = block

        core_push(p).start()

    def core_step(p):
        core_push(p).wait_recv()
        far = 1 - across
        chip_leaving[p] = (kept[p, far].astype(f32) + returned[p, far].astype(f32)).astype(bf16)
        chip_push(p).start()
        chip_sum[p] = kept[p, across].astype(f32) + returned[p, across].astype(f32)

    def chip_step(p):
        chip_push(p).wait_recv()
        total = chip_sum[p] + chip_returned[p].astype(f32)
        for s in range(EXPERTS):
            home_leaving[p, s] = total[s * CAP : (s + 1) * CAP].astype(bf16)
        for step in range(1, EXPERTS):
            to_home(p, step).start()
        home_returned[p, mine] = home_leaving[p, mine]

    sent = [0]

    def home_step(p):
        for step in range(1, EXPERTS):
            from_expert(p, step).wait_recv()
        cols = slice(p * SLICE, (p + 1) * SLICE)
        block = jnp.concatenate(
            [home_returned[p, e].astype(f32) for e in range(EXPERTS)], axis=0
        ).astype(bf16)
        mixed = jnp.dot(mixers, block, preferred_element_type=f32)
        expert_sum = mixed[:padded] + mixed[padded : 2 * padded] + mixed[2 * padded :]
        result = (hidden[:, cols] + expert_sum).astype(bf16)
        layer_out[:, cols] = result[:TREE_NODES]
        picked[:, cols] = jnp.sum(
            jnp.where(token_row == accepted[0], result.astype(f32), 0.0), axis=0, keepdims=True
        )
        while sent[0] < block_count and (sent[0] + 1) * depth <= (p + 1) * SLICE:
            send_block(picked, sent[0], sent[0])
            sent[0] += 1

    def draft_push(q, peer, at):
        return push(
            draft_leaving.at[q, peer],
            draft_returned.at[q, at],
            draft_out_sem.at[q, peer],
            draft_in_sem.at[q, at],
            peer,
        )

    def draft_step():
        def take(k, carry):
            source = lax.rem(me + n - k, n)
            push(
                blocks.at[source],
                blocks.at[source],
                block_out_sem.at[source],
                block_in_sem.at[source],
                source,
            ).wait_recv()
            block_rows[pl.ds(source, 1), :] = blocks[source]
            return carry

        block_rows[pl.ds(me, 1), :] = blocks[me]
        lax.fori_loop(1, n, take, 0)
        draft_rows = block_rows[...].astype(bf16)
        for q in range(part_count):
            for p in range(q * piece_count // part_count, (q + 1) * piece_count // part_count):
                item = ("fc", p)
                load_copy(item).wait()
                partial = jnp.dot(
                    draft_rows, weights[place[item] % slots, 0:depth, :], preferred_element_type=f32
                )
                for t in range(lines):
                    draft_wide[pl.ds(p * lines + t, n, stride=line_count), :] = partial[
                        :, t * LANES : (t + 1) * LANES
                    ]
            each = line_count // part_count
            for source in range(n):
                start = source * line_count + q * each
                draft_leaving[q, source] = draft_wide[start : start + each, :].astype(bf16)

            def send_partial(k, carry):
                draft_push(q, lax.rem(me + k, n), me).start()
                return carry

            lax.fori_loop(1, n, send_partial, 0)
            draft_returned[q, me] = draft_leaving[q, me]

    for p in range(piece_count + 3):
        if p < piece_count:
            partial_step(p)
        if 0 <= p - 1 < piece_count:
            core_step(p - 1)
        if 0 <= p - 3 < piece_count:
            chip_step(p - 3)
        if 0 <= p - 5 < piece_count:
            home_step(p - 5)
    for p in range(max(0, piece_count - 2), piece_count - 1):
        home_step(p)
    ready = sent[0]
    soon = (me < ready) | (me >= block_count)

    @pl.when(soon)
    def _():
        draft_step()

    home_step(piece_count - 1)

    @pl.when(jnp.logical_not(soon))
    def _():
        draft_step()

    def drain(k, carry):
        peer = lax.rem(me + n - k, n)
        for q in range(part_count):
            draft_push(q, peer, peer).wait()
        return carry

    lax.fori_loop(1, n, drain, 0)
    each = line_count // part_count
    for q in range(part_count):
        total = draft_returned[q, 0].astype(f32)
        for source in range(1, n):
            total = total + draft_returned[q, source].astype(f32)
        draft_out[q * each : (q + 1) * each, :] = total

    for k in range(chunk_count):
        for step in range(1, EXPERTS):
            from_plane(k, step).wait_send()
        row_push(k, lane, 0, chip_peer).wait_send()
        row_push(k, lane, 1, core_peer).wait_send()
        row_push(k, chip_lane, 2, core_peer).wait_send()
    for p in range(piece_count):
        core_push(p).wait_send()
        chip_push(p).wait_send()
        for step in range(1, EXPERTS):
            from_expert(p, step).wait_send()
    for b in range(block_count):
        wait_block(picked, b, b)
        wait_block(embed_row, b, block_count + b)


def finish_kernel(layer, draft_lines, layer_out, draft_out):
    layer_out[...] = layer[...]
    for t in range(draft_lines.shape[0]):
        draft_out[:, t * LANES : (t + 1) * LANES] = draft_lines[t : t + 1, :].astype(jnp.bfloat16)


def fused(
    queries,
    tree_key_value,
    key_value_cache,
    lengths,
    parents,
    residual,
    ffn_gain,
    router,
    routes,
    gate_weight,
    up_weight,
    down_weight,
    accepted,
    next_embed,
    draft_fc,
    n,
):
    width, model_width = down_weight.shape
    depth = draft_fc.shape[0]
    group = n // EXPERTS
    share = EXPERTS * CAP
    slots = 26
    pieces = model_width // SLICE
    halves = width // SLICE
    parts = 3
    loads = 2 * pieces * halves + pieces * halves + pieces
    line_count = model_width // LANES
    kv_width = tree_key_value.shape[2]
    key_rows = key_value_cache.shape[2] + LANES
    anywhere = pl.BlockSpec(memory_space=pl.ANY)
    scalars = pl.BlockSpec(memory_space=pltpu.SMEM)
    whole = pl.BlockSpec(memory_space=pltpu.VMEM)
    bf16, f32 = jnp.bfloat16, jnp.float32
    dma = pltpu.SemaphoreType.DMA
    layer, draft_lines = pl.pallas_call(
        functools.partial(fused_kernel, n, slots),
        out_shape=(
            jax.ShapeDtypeStruct((TREE_NODES, model_width), bf16),
            jax.ShapeDtypeStruct((line_count, LANES), f32),
        ),
        in_specs=[scalars] * 4 + [anywhere] * 11,
        out_specs=(whole, whole),
        scratch_shapes=[
            pltpu.VMEM((slots, SLICE, SLICE), bf16),
            pltpu.VMEM((TREE_NODES, model_width), bf16),
            pltpu.VMEM((TREE_NODES, 2, kv_width), bf16),
            pltpu.VMEM((key_rows, kv_width), bf16),
            pltpu.VMEM((key_rows, kv_width), bf16),
            pltpu.VMEM((TREE_NODES, model_width), bf16),
            pltpu.VMEM((line_count, LANES), bf16),
            pltpu.VMEM((EXPERTS, model_width), bf16),
            pltpu.VMEM((1, model_width), bf16),
            pltpu.VMEM((2, 16, kv_width), f32),
            pltpu.VMEM((8, model_width), f32),
            pltpu.VMEM((8, model_width), bf16),
            pltpu.VMEM((pieces, EXPERTS, CAP, SLICE), bf16),
            pltpu.VMEM((pieces, EXPERTS, CAP, SLICE), bf16),
            pltpu.VMEM((pieces, group * share, SLICE), bf16),
            pltpu.VMEM((group * share, width), f32),
            pltpu.VMEM((group * share, width), f32),
            pltpu.VMEM((halves, group * share, SLICE), bf16),
            pltpu.VMEM((pieces, 2, share, SLICE), bf16),
            pltpu.VMEM((pieces, 2, share, SLICE), bf16),
            pltpu.VMEM((pieces, 2, share, SLICE), bf16),
            pltpu.VMEM((pieces, share, SLICE), f32),
            pltpu.VMEM((pieces, share, SLICE), bf16),
            pltpu.VMEM((pieces, share, SLICE), bf16),
            pltpu.VMEM((pieces, EXPERTS, CAP, SLICE), bf16),
            pltpu.VMEM((pieces, EXPERTS, CAP, SLICE), bf16),
            pltpu.VMEM((1, model_width), f32),
            pltpu.VMEM((1, model_width), f32),
            pltpu.VMEM((n, 1, depth), f32),
            pltpu.VMEM((n, depth), f32),
            pltpu.VMEM((n * line_count, LANES), f32),
            pltpu.VMEM((parts, n, line_count // parts, LANES), bf16),
            pltpu.VMEM((parts, n, line_count // parts, LANES), bf16),
            dma((loads,)),
            dma((8,)),
            dma((pieces, EXPERTS)),
            dma((pieces, EXPERTS)),
            dma((pieces, 3)),
            dma((pieces, 3)),
            dma((pieces,)),
            dma((pieces,)),
            dma((pieces,)),
            dma((pieces,)),
            dma((pieces, EXPERTS)),
            dma((pieces, EXPERTS)),
            dma((n,)),
            dma((n,)),
            dma((parts, n)),
            dma((parts, n)),
        ],
        compiler_params=pltpu.CompilerParams(
            collective_id=0, has_side_effects=True, vmem_limit_bytes=67_000_000
        ),
        name="fused",
    )(
        lengths,
        parents,
        routes.T,
        accepted,
        queries,
        tree_key_value,
        key_value_cache,
        residual,
        ffn_gain.reshape(line_count, LANES),
        router.T,
        next_embed,
        gate_weight,
        up_weight,
        down_weight,
        draft_fc,
    )
    return pl.pallas_call(
        finish_kernel,
        out_shape=(
            jax.ShapeDtypeStruct((TREE_NODES, model_width), bf16),
            jax.ShapeDtypeStruct((1, model_width), bf16),
        ),
        in_specs=[whole, whole],
        out_specs=(whole, whole),
        name="finish",
    )(layer, draft_lines)


def fits(lengths, gate_weight, draft_fc, n):
    model_width, width = gate_weight.shape
    depth = draft_fc.shape[0]
    return (
        lengths.shape[0] == 1
        and n == 4 * EXPERTS
        and width == 2 * SLICE
        and model_width == 6 * SLICE
        and depth % LANES == 0
        and depth <= SLICE
        and n * depth == 2 * model_width
    )


def per_device(
    queries,
    tree_key_value,
    key_value_cache,
    lengths,
    parents,
    residual,
    ffn_gain,
    router,
    routes,
    gate_weight,
    up_weight,
    down_weight,
    accepted,
    next_embed,
    draft_fc,
):
    devices = lax.axis_size("expert")
    if fits(lengths, gate_weight, draft_fc, devices):
        return fused(
            queries,
            tree_key_value,
            key_value_cache,
            lengths,
            parents,
            residual,
            ffn_gain,
            router,
            routes,
            gate_weight,
            up_weight,
            down_weight,
            accepted,
            next_embed,
            draft_fc,
            devices,
        )
    context = attention(queries, tree_key_value, key_value_cache, lengths, parents)
    hidden_state = residual.astype(jnp.float32) + context
    normed = (
        hidden_state
        * lax.rsqrt(jnp.mean(hidden_state * hidden_state, axis=-1, keepdims=True) + EPSILON)
        * ffn_gain.astype(jnp.float32)
    ).astype(jnp.bfloat16)
    tokens_here, model_width = normed.shape
    logits = jnp.dot(normed, router, preferred_element_type=jnp.float32)
    expert_ids = jnp.arange(EXPERTS, dtype=jnp.int32)
    first_hit = (routes[:, 0:1] == expert_ids[None, :]).astype(jnp.float32)
    second_hit = (routes[:, 1:2] == expert_ids[None, :]).astype(jnp.float32)
    first_logit = jnp.sum(logits * first_hit, axis=-1)
    second_logit = jnp.sum(logits * second_hit, axis=-1)
    first_share = jax.nn.sigmoid(first_logit - second_logit)
    mixing = first_share[:, None] * first_hit + (1.0 - first_share)[:, None] * second_hit
    hit_table = first_hit + second_hit
    slot_rank = jnp.cumsum(hit_table, axis=0) - 1.0
    slot_ids = jnp.arange(CAP, dtype=jnp.float32)
    placing = hit_table.T[:, None, :] * (slot_rank.T[:, None, :] == slot_ids[None, :, None]).astype(
        jnp.float32
    )
    packed = jnp.einsum(
        "ect,td->ecd", placing.astype(jnp.bfloat16), normed, preferred_element_type=jnp.float32
    ).astype(jnp.bfloat16)
    grouped = moe(packed, gate_weight, up_weight, down_weight, devices)
    weighted = placing * mixing.T[:, None, :]
    expert_sum = jnp.einsum("ect,ecd->td", weighted, grouped, precision=lax.Precision.HIGHEST)
    layer_out = (hidden_state + expert_sum).astype(jnp.bfloat16)
    request_total = lengths.shape[0]
    picker = (accepted[:, None] == jnp.arange(TREE_NODES, dtype=jnp.int32)[None, :]).astype(
        jnp.bfloat16
    )
    picked = jnp.einsum(
        "rt,rtd->rd",
        picker,
        layer_out.reshape(request_total, TREE_NODES, model_width),
        preferred_element_type=jnp.float32,
    ).astype(jnp.bfloat16)
    draft_in = jnp.concatenate([picked, next_embed], axis=1)
    depth = draft_fc.shape[0]
    blocks = draft_in.reshape(request_total, devices, depth).transpose(1, 0, 2)
    draft_out = draft(blocks.astype(jnp.float32), draft_fc).astype(jnp.bfloat16)
    return (layer_out, draft_out)


def solution(mesh):
    return jax.shard_map(
        per_device,
        mesh=mesh,
        in_specs=(
            P(("groups", "expert"), None),
            P(("groups", "expert"), None, None),
            P(("groups", "expert"), None, None, None),
            P(("groups", "expert")),
            P(("groups", "expert")),
            P(("groups", "expert"), None),
            P(),
            P(),
            P(("groups", "expert"), None),
            P(None, "expert"),
            P(None, "expert"),
            P("expert", None),
            P(("groups", "expert")),
            P(("groups", "expert"), None),
            P("expert", None),
        ),
        out_specs=(P(("groups", "expert"), None), P(("groups", "expert"), None)),
        check_vma=False,
    )
```

```python
import functools

import jax
import jax.numpy as jnp
from jax import lax
from jax.experimental import pallas as pl
from jax.experimental.pallas import tpu as pltpu
from jax.sharding import PartitionSpec as P

QUERY_HEADS = 48
KEY_VALUE_HEADS = 8
HEAD_SIZE = 128
EXPERTS = 4
TREE_NODES = 6
CACHE_SLOTS = 512
CAP = 4


EPSILON = 1e-05


def related_kernel(parents, out):
    node_ids = lax.broadcasted_iota(jnp.int32, (1, out.shape[2]), 1)
    for request in range(out.shape[0]):
        reached = []
        for node in range(TREE_NODES):
            row = (node_ids == node).astype(jnp.float32)
            parent = parents[request * TREE_NODES + node]
            for earlier in range(node):
                row = row + jnp.where(parent == earlier, reached[earlier], 0.0)
            reached.append(row)
            out[request, node : node + 1, :] = row


def ancestors(parent_ids):
    table = pl.pallas_call(
        related_kernel,
        out_shape=jax.ShapeDtypeStruct((parent_ids.shape[0] // TREE_NODES, TREE_NODES, 128), jnp.float32),
        in_specs=[pl.BlockSpec(memory_space=pltpu.SMEM)],
        out_specs=pl.BlockSpec(memory_space=pltpu.VMEM),
        name="related",
    )(parent_ids)
    return table[:, :, :TREE_NODES] > 0.5


def attention(queries, tree_key_value, key_value_cache, lengths, parents):
    request_total = lengths.shape[0]
    query_head_count = queries.reshape(
        request_total, TREE_NODES, KEY_VALUE_HEADS, QUERY_HEADS // KEY_VALUE_HEADS, HEAD_SIZE
    )
    cached_key_rows = key_value_cache[:, 0].reshape(
        request_total, CACHE_SLOTS, KEY_VALUE_HEADS, HEAD_SIZE
    )
    cached_value_rows = key_value_cache[:, 1].reshape(
        request_total, CACHE_SLOTS, KEY_VALUE_HEADS, HEAD_SIZE
    )
    tree_key_rows = tree_key_value[:, 0].reshape(
        request_total, TREE_NODES, KEY_VALUE_HEADS, HEAD_SIZE
    )
    tree_value_rows = tree_key_value[:, 1].reshape(
        request_total, TREE_NODES, KEY_VALUE_HEADS, HEAD_SIZE
    )
    score_scale = HEAD_SIZE ** (-0.5)
    cache_scores = (
        jnp.einsum(
            "rtgqd,rlgd->rgtql",
            query_head_count,
            cached_key_rows,
            preferred_element_type=jnp.float32,
        )
        * score_scale
    )
    tree_scores = (
        jnp.einsum(
            "rtgqd,rugd->rgtqu", query_head_count, tree_key_rows, preferred_element_type=jnp.float32
        )
        * score_scale
    )
    visible = jnp.arange(CACHE_SLOTS, dtype=jnp.int32)[None, :] < lengths[:, None]
    related = ancestors(parents)
    cache_scores = jnp.where(visible[:, None, None, None, :], cache_scores, -1e30)
    tree_scores = jnp.where(related[:, None, :, None, :], tree_scores, -1e30)
    row_peak = jnp.maximum(jnp.max(cache_scores, axis=-1), jnp.max(tree_scores, axis=-1))[..., None]
    cache_exp = jnp.exp(cache_scores - row_peak)
    tree_exp = jnp.exp(tree_scores - row_peak)
    denominator = (jnp.sum(cache_exp, axis=-1) + jnp.sum(tree_exp, axis=-1))[..., None]
    cache_weights = (cache_exp / denominator).astype(jnp.bfloat16)
    tree_weights = (tree_exp / denominator).astype(jnp.bfloat16)
    context = jnp.einsum(
        "rgtql,rlgd->rtgqd", cache_weights, cached_value_rows, preferred_element_type=jnp.float32
    ) + jnp.einsum(
        "rgtqu,rugd->rtgqd", tree_weights, tree_value_rows, preferred_element_type=jnp.float32
    )
    return context.reshape(request_total * TREE_NODES, QUERY_HEADS * HEAD_SIZE)


VMEM_LIMIT = 66_000_000


def greet(n, me):
    barrier = pltpu.get_barrier_semaphore()

    def hello(k, carry):
        pl.semaphore_signal(barrier, inc=1, device_id={"expert": lax.rem(me + k, n)})
        return carry

    lax.fori_loop(1, n, hello, 0)
    pl.semaphore_wait(barrier, n - 1)


def push(src, dst, send_sem, recv_sem, peer):
    return pltpu.make_async_remote_copy(
        src_ref=src,
        dst_ref=dst,
        send_sem=send_sem,
        recv_sem=recv_sem,
        device_id={"expert": peer},
        device_id_type=pl.DeviceIdType.MESH,
    )


def moe_kernel(
    n,
    group_size,
    pair_slots,
    down_slots,
    packed,
    gate_hbm,
    up_hbm,
    down_hbm,
    grouped,
    gate_buf,
    up_buf,
    down_buf,
    arrived,
    rows_wide,
    rows,
    activation,
    result,
    leaving,
    returned,
    pair_sem,
    down_sem,
    out_sem,
    in_sem,
    back_out_sem,
    back_in_sem,
    own_sem,
):
    me = lax.axis_index("expert")
    width = gate_hbm.shape[1]
    chunk = gate_buf.shape[2]
    pair_count = width // chunk
    piece = down_buf.shape[2]
    piece_count = down_hbm.shape[1] // piece

    def pair_copies(i):
        slot = lax.rem(i, pair_slots)
        cols = pl.ds(pl.multiple_of(i * chunk, chunk), chunk)
        return (
            pltpu.make_async_copy(gate_hbm.at[:, cols], gate_buf.at[slot], pair_sem.at[0, slot]),
            pltpu.make_async_copy(up_hbm.at[:, cols], up_buf.at[slot], pair_sem.at[1, slot]),
        )

    def down_copy(i):
        slot = lax.rem(i, down_slots)
        cols = pl.ds(pl.multiple_of(i * piece, piece), piece)
        return pltpu.make_async_copy(down_hbm.at[:, cols], down_buf.at[slot], down_sem.at[slot])

    def start_pair(i, carry):
        for copy in pair_copies(i):
            copy.start()
        return carry

    def start_down(i, carry):
        down_copy(i).start()
        return carry

    lax.fori_loop(0, pair_slots, start_pair, 0)
    greet(n, me)

    def dispatch(k, carry):
        peer = lax.rem(me + k, n)
        push(
            packed.at[peer // group_size], arrived.at[me], out_sem.at[peer], in_sem.at[me], peer
        ).start()
        return carry

    lax.fori_loop(1, n, dispatch, 0)
    own = pltpu.make_async_copy(packed.at[me // group_size], arrived.at[me], own_sem)
    own.start()
    lax.fori_loop(0, down_slots, start_down, 0)
    own.wait()

    def take(k, carry):
        source = lax.rem(me + n - k, n)
        push(
            packed.at[0], arrived.at[source], out_sem.at[source], in_sem.at[source], source
        ).wait_recv()
        return carry

    lax.fori_loop(1, n, take, 0)

    def both(pair):
        return pl.ds(pl.multiple_of(pair * 2 * CAP, 2 * CAP), 2 * CAP)

    def widen(pair, carry):
        rows_wide[both(pair), :] = jnp.concatenate(
            [arrived[2 * pair].astype(jnp.float32), arrived[2 * pair + 1].astype(jnp.float32)],
            axis=0,
        )
        return carry

    lax.fori_loop(0, n // 2, widen, 0)
    rows[...] = rows_wide[...].astype(jnp.bfloat16)

    def pair_step(i, carry):
        slot = lax.rem(i, pair_slots)
        for copy in pair_copies(i):
            copy.wait()
        gate_val = jnp.dot(rows[...], gate_buf[slot], preferred_element_type=jnp.float32)
        up_val = jnp.dot(rows[...], up_buf[slot], preferred_element_type=jnp.float32)
        cols = pl.ds(pl.multiple_of(i * chunk, chunk), chunk)
        activation[:, cols] = (jax.nn.silu(gate_val) * up_val).astype(jnp.bfloat16)

        @pl.when(i + pair_slots < pair_count)
        def _():
            start_pair(i + pair_slots, 0)

        return carry

    lax.fori_loop(0, pair_count, pair_step, 0)

    def down_step(i, carry):
        slot = lax.rem(i, down_slots)
        down_copy(i).wait()
        result[...] = jnp.dot(
            activation[...], down_buf[slot], preferred_element_type=jnp.float32
        )

        @pl.when(i + down_slots < piece_count)
        def _():
            start_down(i + down_slots, 0)

        def narrow(pair, inner):
            block = result[both(pair), :]
            leaving[2 * pair, i] = block[:CAP].astype(jnp.bfloat16)
            leaving[2 * pair + 1, i] = block[CAP:].astype(jnp.bfloat16)
            return inner

        lax.fori_loop(0, n // 2, narrow, 0)

        def send_back(k, inner):
            peer = lax.rem(me + k, n)
            push(
                leaving.at[peer, i],
                returned.at[me, i],
                back_out_sem.at[peer],
                back_in_sem.at[me],
                peer,
            ).start()
            return inner

        lax.fori_loop(1, n, send_back, 0)
        return carry

    lax.fori_loop(0, piece_count, down_step, 0)
    returned[me] = leaving[me]

    def drain(k, carry):
        peer = lax.rem(me + n - k, n)
        push(
            leaving.at[peer], returned.at[peer], back_out_sem.at[peer], back_in_sem.at[peer], peer
        ).wait()
        push(
            packed.at[0], arrived.at[peer], out_sem.at[peer], in_sem.at[peer], peer
        ).wait_send()
        return carry

    lax.fori_loop(1, n, drain, 0)

    def gather(expert, carry):
        for i in range(piece_count):

            def add(member, total):
                return total + returned[expert * group_size + member, i].astype(jnp.float32)

            grouped[expert, :, i * piece : (i + 1) * piece] = lax.fori_loop(
                0, group_size, add, jnp.zeros((CAP, piece), jnp.float32)
            )
        return carry

    lax.fori_loop(0, EXPERTS, gather, 0)


def moe(packed, gate_weight, up_weight, down_weight, n):
    model_width, width = gate_weight.shape
    row_count = n * CAP
    chunk = min(512, width)
    piece = model_width // 4
    pair_slots = min(3, width // chunk)
    down_slots = min(2, model_width // piece)
    anywhere = pl.BlockSpec(memory_space=pl.ANY)
    whole = pl.BlockSpec(memory_space=pltpu.VMEM)
    bf16, f32 = jnp.bfloat16, jnp.float32
    return pl.pallas_call(
        functools.partial(moe_kernel, n, n // EXPERTS, pair_slots, down_slots),
        out_shape=jax.ShapeDtypeStruct((EXPERTS, CAP, model_width), f32),
        in_specs=[whole, anywhere, anywhere, anywhere],
        out_specs=whole,
        scratch_shapes=[
            pltpu.VMEM((pair_slots, model_width, chunk), bf16),
            pltpu.VMEM((pair_slots, model_width, chunk), bf16),
            pltpu.VMEM((down_slots, width, piece), bf16),
            pltpu.VMEM((n, CAP, model_width), bf16),
            pltpu.VMEM((row_count, model_width), f32),
            pltpu.VMEM((row_count, model_width), bf16),
            pltpu.VMEM((row_count, width), bf16),
            pltpu.VMEM((row_count, piece), f32),
            pltpu.VMEM((n, model_width // piece, CAP, piece), bf16),
            pltpu.VMEM((n, model_width // piece, CAP, piece), bf16),
            pltpu.SemaphoreType.DMA((2, pair_slots)),
            pltpu.SemaphoreType.DMA((down_slots,)),
            pltpu.SemaphoreType.DMA((n,)),
            pltpu.SemaphoreType.DMA((n,)),
            pltpu.SemaphoreType.DMA((n,)),
            pltpu.SemaphoreType.DMA((n,)),
            pltpu.SemaphoreType.DMA,
        ],
        compiler_params=pltpu.CompilerParams(
            collective_id=0, has_side_effects=True, vmem_limit_bytes=VMEM_LIMIT
        ),
        name="moe",
    )(packed, gate_weight, up_weight, down_weight)


def draft_kernel(
    n,
    share,
    piece,
    blocks,
    fc_hbm,
    out,
    fc_buf,
    arrived,
    rows_wide,
    result,
    leaving,
    returned,
    fc_sem,
    out_sem,
    in_sem,
    back_out_sem,
    back_in_sem,
):
    me = lax.axis_index("expert")
    piece_count = fc_hbm.shape[1] // piece
    half = piece // 2

    def fc_copy(i):
        cols = pl.ds(pl.multiple_of(i * piece, piece), piece)
        return pltpu.make_async_copy(fc_hbm.at[:, cols], fc_buf.at[i], fc_sem.at[i])

    def start_fc(i, carry):
        fc_copy(i).start()
        return carry

    lax.fori_loop(0, piece_count, start_fc, 0)
    greet(n, me)

    def dispatch(k, carry):
        peer = lax.rem(me + k, n)
        push(blocks.at[peer], arrived.at[me], out_sem.at[peer], in_sem.at[me], peer).start()
        return carry

    lax.fori_loop(1, n, dispatch, 0)
    rows_wide[pl.ds(me * share, share), :] = blocks[me]

    def take(k, carry):
        source = lax.rem(me + n - k, n)
        push(
            blocks.at[source], arrived.at[source], out_sem.at[source], in_sem.at[source], source
        ).wait()
        rows_wide[pl.ds(source * share, share), :] = arrived[source]
        return carry

    lax.fori_loop(1, n, take, 0)

    def step(i, carry):
        fc_copy(i).wait()
        result[...] = jnp.dot(
            rows_wide[...].astype(jnp.bfloat16), fc_buf[i], preferred_element_type=jnp.float32
        )

        def split(source, inner):
            block = result[pl.ds(source * share, share), :]
            leaving[source, i] = jnp.concatenate(
                [block[:, :half], block[:, half:]], axis=0
            ).astype(jnp.bfloat16)
            return inner

        lax.fori_loop(0, n, split, 0)

        def send_back(k, inner):
            peer = lax.rem(me + k, n)
            push(
                leaving.at[peer, i],
                returned.at[me, i],
                back_out_sem.at[peer],
                back_in_sem.at[me],
                peer,
            ).start()
            return inner

        lax.fori_loop(1, n, send_back, 0)
        return carry

    lax.fori_loop(0, piece_count, step, 0)
    returned[me] = leaving[me]

    def drain(k, carry):
        peer = lax.rem(me + n - k, n)
        push(
            leaving.at[peer], returned.at[peer], back_out_sem.at[peer], back_in_sem.at[peer], peer
        ).wait()
        return carry

    lax.fori_loop(1, n, drain, 0)
    for i in range(piece_count):

        def add(source, total):
            return total + returned[source, i].astype(jnp.float32)

        total = lax.fori_loop(0, n, add, jnp.zeros((2 * share, half), jnp.float32))
        out[:, i * piece : i * piece + half] = total[:share]
        out[:, i * piece + half : (i + 1) * piece] = total[share:]


def draft(blocks, draft_fc):
    n, share, depth = blocks.shape
    model_width = draft_fc.shape[1]
    piece = model_width // 4
    pieces = model_width // piece
    whole = pl.BlockSpec(memory_space=pltpu.VMEM)
    f32 = jnp.float32
    return pl.pallas_call(
        functools.partial(draft_kernel, n, share, piece),
        out_shape=jax.ShapeDtypeStruct((share, model_width), f32),
        in_specs=[whole, pl.BlockSpec(memory_space=pl.ANY)],
        out_specs=whole,
        scratch_shapes=[
            pltpu.VMEM((pieces, depth, piece), jnp.bfloat16),
            pltpu.VMEM((n, share, depth), f32),
            pltpu.VMEM((n * share, depth), f32),
            pltpu.VMEM((n * share, piece), f32),
            pltpu.VMEM((n, pieces, 2 * share, piece // 2), jnp.bfloat16),
            pltpu.VMEM((n, pieces, 2 * share, piece // 2), jnp.bfloat16),
            pltpu.SemaphoreType.DMA((pieces,)),
            pltpu.SemaphoreType.DMA((n,)),
            pltpu.SemaphoreType.DMA((n,)),
            pltpu.SemaphoreType.DMA((n,)),
            pltpu.SemaphoreType.DMA((n,)),
        ],
        compiler_params=pltpu.CompilerParams(
            collective_id=1, has_side_effects=True, vmem_limit_bytes=VMEM_LIMIT
        ),
        name="draft",
    )(blocks, draft_fc)


SLICE = 1024
LANES = 128
UNIT = 256


def greet_all(n, me):
    barrier = pltpu.get_barrier_semaphore()

    def hello(k, carry):
        pl.semaphore_signal(barrier, inc=1, device_id={"expert": lax.rem(me + k, n)})
        return carry

    lax.fori_loop(1, n, hello, 0)
    return barrier


def fused_kernel(
    n,
    slots,
    lengths,
    parents,
    routes,
    accepted,
    queries_hbm,
    tree_hbm,
    cache_hbm,
    residual_hbm,
    gain_hbm,
    router_hbm,
    embed_hbm,
    gate_hbm,
    up_hbm,
    down_hbm,
    fc_hbm,
    layer_out,
    draft_out,
    weights,
    queries,
    tree,
    keys,
    values,
    residual,
    gain,
    router,
    embed,
    tree_rows,
    hidden,
    normed,
    packed,
    arrived,
    rows,
    gate_sum,
    up_sum,
    activation,
    kept,
    leaving,
    returned,
    chip_sum,
    chip_leaving,
    chip_returned,
    home_leaving,
    home_returned,
    pick_rows,
    pick_arrived,
    shares,
    share_leaving,
    share_rows,
    hidden_row,
    embed_row,
    blocks,
    block_rows,
    draft_sum,
    draft_wide,
    draft_leaving,
    draft_returned,
    load_sem,
    input_sem,
    out_sem,
    in_sem,
    plane_out_sem,
    plane_in_sem,
    core_out_sem,
    core_in_sem,
    chip_out_sem,
    chip_in_sem,
    home_out_sem,
    home_in_sem,
    pick_out_sem,
    pick_in_sem,
    share_out_sem,
    share_in_sem,
    block_out_sem,
    block_in_sem,
    draft_out_sem,
    draft_in_sem,
):
    bf16, f32 = jnp.bfloat16, jnp.float32
    me = lax.axis_index("expert")
    group = n // EXPERTS
    mine = me // group
    lane = lax.rem(me, group)
    core = lax.rem(lane, 2)
    across = lane // 2
    core_peer = mine * group + across * 2 + (1 - core)
    chip_peer = mine * group + (1 - across) * 2 + core
    model_width = down_hbm.shape[1]
    width = down_hbm.shape[0]
    depth = fc_hbm.shape[0]
    slice_count = model_width // SLICE
    half_count = width // SLICE
    half = SLICE // 2
    chunks = [(0, half), (half, half)] + [(k * SLICE, SLICE) for k in range(1, slice_count)]
    last = model_width - SLICE
    pieces = [(k * SLICE, SLICE) for k in range(slice_count - 1)]
    pieces += [(last, SLICE - UNIT), (model_width - UNIT, UNIT)]
    piece_count = len(pieces)
    unit_count = depth // UNIT
    block_count = model_width // depth
    padded = 8
    share = EXPERTS * CAP
    cache_slots = cache_hbm.shape[2]
    key_rows = keys.shape[0]
    line_count = model_width // LANES
    lines = SLICE // LANES
    part_count = draft_leaving.shape[0]

    pairs = [
        ("pair", k, h, i) for k in range(slice_count) for h in range(half_count) for i in range(2)
    ]
    downs = [("down", p, a) for p in range(piece_count) for a in range(half_count)]
    order = pairs + downs + [("fc", p) for p in range(slice_count)]
    place = {item: i for i, item in enumerate(order)}

    def load_copy(item):
        i = place[item]
        slot = weights.at[i % slots]
        if item[0] == "pair":
            k, h = item[1], item[2]
            source = (gate_hbm, up_hbm)[item[3]]
            view = source.at[k * SLICE : (k + 1) * SLICE, h * SLICE : (h + 1) * SLICE]
        elif item[0] == "down":
            a = item[2]
            start, size = pieces[item[1]]
            view = down_hbm.at[a * SLICE : (a + 1) * SLICE, start : start + size]
            slot = weights.at[i % slots, :, 0:size]
        else:
            p = item[1]
            view = fc_hbm.at[:, p * SLICE : (p + 1) * SLICE]
            slot = weights.at[i % slots, 0:depth, :]
        return pltpu.make_async_copy(view, slot, load_sem.at[i])

    def start_load(i):
        if i < len(order):
            load_copy(order[i]).start()

    inputs = [
        pltpu.make_async_copy(source, target, input_sem.at[i])
        for i, (source, target) in enumerate(
            [
                (queries_hbm, queries),
                (tree_hbm, tree),
                (cache_hbm.at[0, 0], keys.at[0:cache_slots, :]),
                (residual_hbm, residual),
                (cache_hbm.at[0, 1], values.at[0:cache_slots, :]),
                (gain_hbm, gain),
                (router_hbm, router),
                (embed_hbm, embed),
            ]
        )
    ]
    for copy in inputs:
        copy.start()
    barrier = greet_all(n, me)

    row8 = lax.broadcasted_iota(jnp.int32, (padded, LANES), 0)
    col8 = lax.broadcasted_iota(jnp.int32, (padded, LANES), 1)
    node_ids = lax.broadcasted_iota(jnp.int32, (1, LANES), 1)
    reached = []
    related = jnp.zeros((padded, LANES), f32)
    for node in range(TREE_NODES):
        row = (node_ids == node).astype(f32)
        parent = parents[node]
        for earlier in range(node):
            row = row + jnp.where(parent == earlier, reached[earlier], 0.0)
        reached.append(row)
        related = related + jnp.where(row8 == node, row, 0.0)
    slot_ids = lax.broadcasted_iota(jnp.int32, (padded, cache_slots), 1)
    bias = jnp.concatenate(
        [
            jnp.where(slot_ids < lengths[0], 0.0, -1e30),
            jnp.where(related > 0.5, 0.0, -1e30),
        ],
        axis=1,
    )
    heads_each = QUERY_HEADS // KEY_VALUE_HEADS
    bias = jnp.concatenate([bias] * heads_each, axis=0)

    def named(choice, token):
        expert = routes[choice, token]
        rank = jnp.int32(0)
        for earlier in range(token):
            for other in range(2):
                rank = rank + jnp.where(routes[other, earlier] == expert, 1, 0)
        return expert, rank

    places = [[named(choice, token) for choice in range(2)] for token in range(TREE_NODES)]

    for copy in inputs[:3]:
        copy.wait()
    for i in range(slots):
        start_load(i)
    tree_rows[...] = jnp.zeros_like(tree_rows)
    for token in range(TREE_NODES):
        both = tree[token].astype(f32)
        tree_rows[0, token : token + 1, :] = both[0:1]
        tree_rows[1, token : token + 1, :] = both[1:2]
    tile = tree_rows.shape[1]
    blank = jnp.zeros((key_rows - cache_slots - tile, keys.shape[1]), bf16)
    keys[cache_slots : cache_slots + tile, :] = tree_rows[0].astype(bf16)
    keys[cache_slots + tile :, :] = blank
    values[cache_slots : cache_slots + tile, :] = tree_rows[1].astype(bf16)
    values[cache_slots + tile :, :] = blank
    spare = jnp.zeros((padded - TREE_NODES, HEAD_SIZE), f32)
    score_scale = HEAD_SIZE ** (-0.5)
    weights_of = []
    for g in range(KEY_VALUE_HEADS):
        parts = []
        for q in range(heads_each):
            head = g * heads_each + q
            parts.append(queries[:, head * HEAD_SIZE : (head + 1) * HEAD_SIZE].astype(f32))
            parts.append(spare)
        head_queries = jnp.concatenate(parts, axis=0).astype(bf16)
        scores = (
            lax.dot_general(
                head_queries,
                keys[:, g * HEAD_SIZE : (g + 1) * HEAD_SIZE],
                (((1,), (1,)), ((), ())),
                preferred_element_type=f32,
            )
            * score_scale
            + bias
        )
        peak = jnp.max(scores, axis=-1, keepdims=True)
        grown = jnp.exp(scores - peak)
        total = jnp.sum(grown, axis=-1, keepdims=True)
        weights_of.append((grown * (1.0 / total)).astype(bf16))
    for copy in inputs[3:5]:
        copy.wait()
    square = jnp.zeros((padded, HEAD_SIZE), f32)
    for g in range(KEY_VALUE_HEADS):
        context = jnp.dot(
            weights_of[g],
            values[:, g * HEAD_SIZE : (g + 1) * HEAD_SIZE],
            preferred_element_type=f32,
        )
        for q in range(heads_each):
            head = g * heads_each + q
            cols = slice(head * HEAD_SIZE, (head + 1) * HEAD_SIZE)
            state = context[q * padded : (q + 1) * padded] + jnp.concatenate(
                [residual[:, cols].astype(f32), spare], axis=0
            )
            hidden[:, cols] = state
            square = square + state * state
    for copy in inputs[5:]:
        copy.wait()
    level = lax.rsqrt(jnp.sum(square, axis=-1, keepdims=True) / model_width + EPSILON)

    slot_row = lax.broadcasted_iota(jnp.int32, (EXPERTS * padded, padded), 0)
    slot_col = lax.broadcasted_iota(jnp.int32, (EXPERTS * padded, padded), 1)
    placing = jnp.zeros((EXPERTS * padded, padded), f32)
    for token, choices in enumerate(places):
        for expert, rank in choices:
            placing = placing + jnp.where(
                (slot_row == expert * padded + rank) & (slot_col == token), 1.0, 0.0
            )
    placing = placing.astype(bf16)

    def to_plane(c, step):
        plane = lax.rem(mine + step, EXPERTS)
        cols = pl.ds(chunks[c][0], chunks[c][1])
        return push(
            packed.at[plane, :, cols],
            arrived.at[mine, :, cols],
            out_sem.at[c, plane],
            in_sem.at[c, mine],
            plane * group + lane,
        )

    def from_plane(c, step):
        plane = lax.rem(mine + EXPERTS - step, EXPERTS)
        cols = pl.ds(chunks[c][0], chunks[c][1])
        return push(
            packed.at[plane, :, cols],
            arrived.at[plane, :, cols],
            out_sem.at[c, plane],
            in_sem.at[c, plane],
            plane * group + lane,
        )

    def pack_step(c):
        start, size = chunks[c]
        cols = slice(start, start + size)
        gains = [
            gain[t : t + 1, :].astype(f32)
            for t in range(start // LANES, (start + size) // LANES)
        ]
        normal = (hidden[:, cols] * level * jnp.concatenate(gains, axis=1)).astype(bf16)
        normed[:, cols] = normal
        spread = jnp.dot(placing, normal, preferred_element_type=f32)
        for e in range(EXPERTS):
            packed[e, :, cols] = spread[e * padded : e * padded + CAP].astype(bf16)
        arrived[mine, :, cols] = packed[mine, :, cols]

    pack_step(0)
    pl.semaphore_wait(barrier, n - 1)
    for c in range(len(chunks)):
        if c > 0:
            pack_step(c)
        for step in range(1, EXPERTS):
            to_plane(c, step).start()

    token_row = row8[:, 0:1]
    embed_row[...] = embed[...].astype(f32)
    for k in range(slice_count):
        cols = slice(k * SLICE, (k + 1) * SLICE)
        hidden_row[:, cols] = jnp.sum(
            jnp.where(token_row == accepted[0], hidden[:, cols], 0.0), axis=0, keepdims=True
        )

    def block_push(row, b, j):
        source = row.at[:, b * depth : (b + 1) * depth]
        return push(source, blocks.at[me], block_out_sem.at[j], block_in_sem.at[me], j)

    def send_block(row, b, j):
        @pl.when(me != j)
        def _():
            block_push(row, b, j).start()

        @pl.when(me == j)
        def _():
            blocks[j] = row[:, b * depth : (b + 1) * depth]

    def wait_block(row, b, j):
        @pl.when(me != j)
        def _():
            block_push(row, b, j).wait_send()

    for b in range(block_count):
        send_block(embed_row, b, block_count + b)
        send_block(hidden_row, b, b)

    logits = [jnp.zeros((padded, 1), f32) for _ in range(EXPERTS)]
    for k in range(slice_count):
        cols = slice(k * SLICE, (k + 1) * SLICE)
        normal = normed[:, cols].astype(f32)
        for e in range(EXPERTS):
            logits[e] = logits[e] + jnp.sum(
                normal * router[e : e + 1, cols].astype(f32), axis=-1, keepdims=True
            )
    ids = [jnp.full((padded, 1), -1, jnp.int32) for _ in range(4)]
    for token, choices in enumerate(places):
        for choice, (expert, rank) in enumerate(choices):
            ids[choice] = jnp.where(token_row == token, expert, ids[choice])
            ids[2 + choice] = jnp.where(token_row == token, expert * CAP + rank, ids[2 + choice])
    first_logit = jnp.zeros((padded, 1), f32)
    second_logit = jnp.zeros((padded, 1), f32)
    for e in range(EXPERTS):
        first_logit = first_logit + jnp.where(ids[0] == e, logits[e], 0.0)
        second_logit = second_logit + jnp.where(ids[1] == e, logits[e], 0.0)
    first_share = jax.nn.sigmoid(first_logit - second_logit)
    share_col = col8[:, :share]
    weighted = jnp.where(share_col == ids[2], first_share, 0.0) + jnp.where(
        share_col == ids[3], 1.0 - first_share, 0.0
    )

    def split(exact):
        high = exact.astype(bf16).astype(f32)
        middle = (exact - high).astype(bf16).astype(f32)
        low = exact - high - middle
        return jnp.concatenate([high, middle, low], axis=0).astype(bf16)

    mixers = split(weighted)

    def pick_push(step, back):
        plane = lax.rem(mine + (EXPERTS - step if back else step), EXPERTS)
        return push(
            pick_rows.at[plane],
            pick_arrived.at[plane if back else mine],
            pick_out_sem.at[plane],
            pick_in_sem.at[plane if back else mine],
            plane * group + lane,
        )

    for e in range(EXPERTS):
        chosen = jnp.zeros((padded, LANES), f32)
        for expert, position, portion in (
            (ids[0], ids[2], first_share),
            (ids[1], ids[3], 1.0 - first_share),
        ):
            here = (col8 == mine * CAP + position - expert * CAP) & (expert == e)
            chosen = chosen + jnp.where(here, portion, 0.0)
        pick_rows[e] = jnp.sum(
            jnp.where(token_row == accepted[0], chosen, 0.0), axis=0, keepdims=True
        )
    for step in range(1, EXPERTS):
        pick_push(step, False).start()
    pick_arrived[mine] = pick_rows[mine]

    def row_push(c, which, sem, peer):
        start, size = chunks[c]
        block = rows.at[pl.ds(pl.multiple_of(which * share, share), share), pl.ds(start, size)]
        return push(block, block, plane_out_sem.at[c, sem], plane_in_sem.at[c, sem], peer)

    chip_lane = (1 - across) * 2 + core
    core_lane = across * 2 + (1 - core)
    far_lane = (1 - across) * 2 + (1 - core)

    def gather_step(k):
        for step in range(1, EXPERTS):
            from_plane(k, step).wait_recv()
        start, size = chunks[k]
        cols = slice(start, start + size)
        rows[pl.ds(pl.multiple_of(lane * share, share), share), cols] = jnp.concatenate(
            [arrived[s, :, cols].astype(f32) for s in range(EXPERTS)], axis=0
        ).astype(bf16)
        row_push(k, lane, 0, chip_peer).start()
        row_push(k, lane, 1, core_peer).start()

    def forward_step(k):
        row_push(k, chip_lane, 0, chip_peer).wait_recv()
        row_push(k, chip_lane, 2, core_peer).start()

    def expert_step(c):
        row_push(c, core_lane, 1, core_peer).wait_recv()
        row_push(c, far_lane, 2, core_peer).wait_recv()
        start, size = chunks[c]
        k, first = start // SLICE, start % SLICE
        final = start + size == model_width
        for h in range(half_count):
            cols = slice(h * SLICE, (h + 1) * SLICE)
            sums = []
            for i, total in ((0, gate_sum), (1, up_sum)):
                item = ("pair", k, h, i)
                if first == 0:
                    load_copy(item).wait()
                value = jnp.dot(
                    rows[:, start : start + size],
                    weights[place[item] % slots, first : first + size, :],
                    preferred_element_type=f32,
                )
                if start > 0:
                    value = value + total[:, cols]
                if not final:
                    total[:, cols] = value
                sums.append(value)
                if first + size == SLICE:
                    start_load(place[item] + slots)
            if final:
                activation[h] = (jax.nn.silu(sums[0]) * sums[1]).astype(bf16)

    for t in range(len(chunks) + 3):
        if t < len(chunks):
            gather_step(t)
        if 0 <= t - 2 < len(chunks):
            forward_step(t - 2)
        if 0 <= t - 3 < len(chunks):
            expert_step(t - 3)

    def piece_cols(p):
        return pl.ds(pieces[p][0], pieces[p][1])

    def core_push(p):
        cols = piece_cols(p)
        return push(
            leaving.at[:, :, cols],
            returned.at[:, :, cols],
            core_out_sem.at[p],
            core_in_sem.at[p],
            core_peer,
        )

    def chip_push(p):
        cols = piece_cols(p)
        return push(
            chip_leaving.at[:, cols],
            chip_returned.at[:, cols],
            chip_out_sem.at[p],
            chip_in_sem.at[p],
            chip_peer,
        )

    def to_home(p, step):
        plane = lax.rem(mine + step, EXPERTS)
        return push(
            home_leaving.at[plane, :, piece_cols(p)],
            home_returned.at[mine, :, piece_cols(p)],
            home_out_sem.at[p, plane],
            home_in_sem.at[p, mine],
            plane * group + lane,
        )

    def from_expert(p, step):
        plane = lax.rem(mine + EXPERTS - step, EXPERTS)
        return push(
            home_leaving.at[plane, :, piece_cols(p)],
            home_returned.at[plane, :, piece_cols(p)],
            home_out_sem.at[p, plane],
            home_in_sem.at[p, plane],
            plane * group + lane,
        )

    def partial_step(p):
        start, size = pieces[p]
        cols = slice(start, start + size)
        partial = None
        for a in range(half_count):
            item = ("down", p, a)
            load_copy(item).wait()
            value = jnp.dot(
                activation[a], weights[place[item] % slots, :, 0:size], preferred_element_type=f32
            )
            partial = value if partial is None else partial + value
            start_load(place[item] + slots)
        for member in range(group):
            block = partial[member * share : (member + 1) * share].astype(bf16)
            a, c = member // 2, member % 2

            @pl.when(core == c)
            def _():
                kept[a, :, cols] = block

            @pl.when(core != c)
            def _():
                leaving[a, :, cols] = block

        core_push(p).start()

    def core_step(p):
        core_push(p).wait_recv()
        start, size = pieces[p]
        cols = slice(start, start + size)
        far = 1 - across
        chip_leaving[:, cols] = (
            kept[far, :, cols].astype(f32) + returned[far, :, cols].astype(f32)
        ).astype(bf16)
        chip_push(p).start()
        chip_sum[:, cols] = kept[across, :, cols].astype(f32) + returned[across, :, cols].astype(
            f32
        )

    def share_push(unit, b):
        part = unit % unit_count
        return push(
            share_leaving.at[unit],
            shares.at[me, part],
            share_out_sem.at[unit],
            share_in_sem.at[me, part],
            b,
        )

    def chip_step(p, pick_mixers):
        chip_push(p).wait_recv()
        start, size = pieces[p]
        cols = slice(start, start + size)
        total = chip_sum[:, cols] + chip_returned[:, cols].astype(f32)
        mixed = jnp.dot(pick_mixers, total.astype(bf16), preferred_element_type=f32)
        portion = mixed[:padded] + mixed[padded : 2 * padded] + mixed[2 * padded :]
        for unit in range(start // UNIT, (start + size) // UNIT):
            b = unit // unit_count
            first = unit * UNIT - start
            value = portion[:EXPERTS, first : first + UNIT].astype(bf16)

            @pl.when(me != b)
            def _():
                share_leaving[unit] = value
                share_push(unit, b).start()

            @pl.when(me == b)
            def _():
                shares[b, unit % unit_count] = value

        for s in range(EXPERTS):
            home_leaving[s, :, cols] = total[s * CAP : (s + 1) * CAP].astype(bf16)
        for step in range(1, EXPERTS):
            to_home(p, step).start()
        home_returned[mine, :, cols] = home_leaving[mine, :, cols]

    def home_step(p):
        for step in range(1, EXPERTS):
            from_expert(p, step).wait_recv()
        start, size = pieces[p]
        cols = slice(start, start + size)
        block = jnp.concatenate(
            [home_returned[e, :, cols].astype(f32) for e in range(EXPERTS)], axis=0
        ).astype(bf16)
        mixed = jnp.dot(mixers, block, preferred_element_type=f32)
        expert_sum = mixed[:padded] + mixed[padded : 2 * padded] + mixed[2 * padded :]
        result = (hidden[:, cols] + expert_sum).astype(bf16)
        layer_out[:, cols] = result[:TREE_NODES]

    def draft_push(q, peer, at):
        return push(
            draft_leaving.at[q, peer],
            draft_returned.at[q, at],
            draft_out_sem.at[q, peer],
            draft_in_sem.at[q, at],
            peer,
        )

    def row_of(device):
        return lax.rem(device, group) * EXPERTS + device // group

    def block_step():
        def take(k, carry):
            source = lax.rem(me + n - k, n)
            push(
                blocks.at[source],
                blocks.at[source],
                block_out_sem.at[source],
                block_in_sem.at[source],
                source,
            ).wait_recv()
            block_rows[pl.ds(row_of(source), 1), :] = blocks[source]
            return carry

        block_rows[pl.ds(row_of(me), 1), :] = blocks[me]
        lax.fori_loop(1, n, take, 0)
        share_rows[...] = jnp.zeros_like(share_rows)

    def share_step(first, past):
        @pl.when(me < block_count)
        def _():
            for part in range(first, past):

                def take(k, carry):
                    source = lax.rem(me + n - k, n)
                    push(
                        shares.at[source, part],
                        shares.at[source, part],
                        share_out_sem.at[part],
                        share_in_sem.at[source, part],
                        source,
                    ).wait_recv()
                    return carry

                lax.fori_loop(1, n, take, 0)
                sums = []
                for member in range(group):
                    total = shares[member, part].astype(f32)
                    for e in range(1, EXPERTS):
                        total = total + shares[e * group + member, part].astype(f32)
                    sums.append(total)
                share_rows[:, part * UNIT : (part + 1) * UNIT] = jnp.concatenate(sums, axis=0)

    def draft_step(first, past, final):
        share_step(first, past)
        deep = slice(first * UNIT, past * UNIT)
        draft_rows = (block_rows[:, deep] + share_rows[:, deep]).astype(bf16)
        per_part = slice_count // part_count
        for q in range(part_count):
            for p in range(q * per_part, (q + 1) * per_part):
                item = ("fc", p)
                if first == 0:
                    load_copy(item).wait()
                partial = jnp.dot(
                    draft_rows, weights[place[item] % slots, deep, :], preferred_element_type=f32
                )
                cols = slice(p * SLICE, (p + 1) * SLICE)
                if first > 0:
                    partial = partial + draft_sum[:, cols]
                if not final:
                    draft_sum[:, cols] = partial
                    continue
                for t in range(lines):
                    draft_wide[pl.ds(p * lines + t, n, stride=line_count), :] = partial[
                        :, t * LANES : (t + 1) * LANES
                    ]
            if not final:
                continue
            each = line_count // part_count
            for row in range(n):
                device = row % EXPERTS * group + row // EXPERTS
                start = row * line_count + q * each
                draft_leaving[q, device] = draft_wide[start : start + each, :].astype(bf16)

            def send_partial(k, carry):
                draft_push(q, lax.rem(me + k, n), me).start()
                return carry

            lax.fori_loop(1, n, send_partial, 0)
            draft_returned[q, me] = draft_leaving[q, me]

    for step in range(1, EXPERTS):
        pick_push(step, True).wait_recv()
    picks = jnp.concatenate(
        [pick_arrived[s][:, :share] for s in range(EXPERTS)]
        + [jnp.zeros((padded - EXPERTS, share), f32)],
        axis=0,
    )
    pick_mixers = split(picks)

    for p in range(piece_count + 3):
        if p < piece_count:
            partial_step(p)
        if 0 <= p - 1 < piece_count:
            core_step(p - 1)
        if p == piece_count:
            block_step()
        if 0 <= p - 3 < piece_count:
            chip_step(p - 3, pick_mixers)
    draft_step(0, unit_count - 1, False)
    draft_step(unit_count - 1, unit_count, True)
    for p in range(piece_count):
        home_step(p)

    for c in range(len(chunks)):
        for step in range(1, EXPERTS):
            from_plane(c, step).wait_send()
        row_push(c, lane, 0, chip_peer).wait_send()
        row_push(c, lane, 1, core_peer).wait_send()
        row_push(c, chip_lane, 2, core_peer).wait_send()
    for step in range(1, EXPERTS):
        pick_push(step, False).wait_send()
    for p in range(piece_count):
        core_push(p).wait_send()
        chip_push(p).wait_send()
        for step in range(1, EXPERTS):
            from_expert(p, step).wait_send()
    for b in range(block_count):
        wait_block(hidden_row, b, b)
        wait_block(embed_row, b, block_count + b)

        @pl.when(me != b)
        def _():
            for part in range(unit_count):
                share_push(b * unit_count + part, b).wait_send()

    def drain(k, carry):
        peer = lax.rem(me + n - k, n)
        for q in range(part_count):
            draft_push(q, peer, peer).wait()
        return carry

    lax.fori_loop(1, n, drain, 0)
    each = line_count // part_count
    for q in range(part_count):
        total = draft_returned[q, 0].astype(f32)
        for source in range(1, n):
            total = total + draft_returned[q, source].astype(f32)
        draft_out[q * each : (q + 1) * each, :] = total


def finish_kernel(layer, draft_lines, layer_out, draft_out):
    layer_out[...] = layer[...]
    for t in range(draft_lines.shape[0]):
        draft_out[:, t * LANES : (t + 1) * LANES] = draft_lines[t : t + 1, :].astype(jnp.bfloat16)


def fused(
    queries,
    tree_key_value,
    key_value_cache,
    lengths,
    parents,
    residual,
    ffn_gain,
    router,
    routes,
    gate_weight,
    up_weight,
    down_weight,
    accepted,
    next_embed,
    draft_fc,
    n,
):
    width, model_width = down_weight.shape
    depth = draft_fc.shape[0]
    group = n // EXPERTS
    share = EXPERTS * CAP
    slots = 26
    slices = model_width // SLICE
    halves = width // SLICE
    parts = 3
    pieces = slices + 1
    chunks = slices + 1
    units = depth // UNIT
    loads = 2 * slices * halves + pieces * halves + slices
    line_count = model_width // LANES
    kv_width = tree_key_value.shape[2]
    key_rows = key_value_cache.shape[2] + LANES
    anywhere = pl.BlockSpec(memory_space=pl.ANY)
    scalars = pl.BlockSpec(memory_space=pltpu.SMEM)
    whole = pl.BlockSpec(memory_space=pltpu.VMEM)
    bf16, f32 = jnp.bfloat16, jnp.float32
    dma = pltpu.SemaphoreType.DMA
    layer, draft_lines = pl.pallas_call(
        functools.partial(fused_kernel, n, slots),
        out_shape=(
            jax.ShapeDtypeStruct((TREE_NODES, model_width), bf16),
            jax.ShapeDtypeStruct((line_count, LANES), f32),
        ),
        in_specs=[scalars] * 4 + [anywhere] * 11,
        out_specs=(whole, whole),
        scratch_shapes=[
            pltpu.VMEM((slots, SLICE, SLICE), bf16),
            pltpu.VMEM((TREE_NODES, model_width), bf16),
            pltpu.VMEM((TREE_NODES, 2, kv_width), bf16),
            pltpu.VMEM((key_rows, kv_width), bf16),
            pltpu.VMEM((key_rows, kv_width), bf16),
            pltpu.VMEM((TREE_NODES, model_width), bf16),
            pltpu.VMEM((line_count, LANES), bf16),
            pltpu.VMEM((EXPERTS, model_width), bf16),
            pltpu.VMEM((1, model_width), bf16),
            pltpu.VMEM((2, 16, kv_width), f32),
            pltpu.VMEM((8, model_width), f32),
            pltpu.VMEM((8, model_width), bf16),
            pltpu.VMEM((EXPERTS, CAP, model_width), bf16),
            pltpu.VMEM((EXPERTS, CAP, model_width), bf16),
            pltpu.VMEM((group * share, model_width), bf16),
            pltpu.VMEM((group * share, width), f32),
            pltpu.VMEM((group * share, width), f32),
            pltpu.VMEM((halves, group * share, SLICE), bf16),
            pltpu.VMEM((2, share, model_width), bf16),
            pltpu.VMEM((2, share, model_width), bf16),
            pltpu.VMEM((2, share, model_width), bf16),
            pltpu.VMEM((share, model_width), f32),
            pltpu.VMEM((share, model_width), bf16),
            pltpu.VMEM((share, model_width), bf16),
            pltpu.VMEM((EXPERTS, CAP, model_width), bf16),
            pltpu.VMEM((EXPERTS, CAP, model_width), bf16),
            pltpu.VMEM((EXPERTS, 1, LANES), f32),
            pltpu.VMEM((EXPERTS, 1, LANES), f32),
            pltpu.VMEM((n, units, EXPERTS, UNIT), bf16),
            pltpu.VMEM((model_width // UNIT, EXPERTS, UNIT), bf16),
            pltpu.VMEM((n, depth), f32),
            pltpu.VMEM((1, model_width), f32),
            pltpu.VMEM((1, model_width), f32),
            pltpu.VMEM((n, 1, depth), f32),
            pltpu.VMEM((n, depth), f32),
            pltpu.VMEM((n, model_width), f32),
            pltpu.VMEM((n * line_count, LANES), f32),
            pltpu.VMEM((parts, n, line_count // parts, LANES), bf16),
            pltpu.VMEM((parts, n, line_count // parts, LANES), bf16),
            dma((loads,)),
            dma((8,)),
            dma((chunks, EXPERTS)),
            dma((chunks, EXPERTS)),
            dma((chunks, 3)),
            dma((chunks, 3)),
            dma((pieces,)),
            dma((pieces,)),
            dma((pieces,)),
            dma((pieces,)),
            dma((pieces, EXPERTS)),
            dma((pieces, EXPERTS)),
            dma((EXPERTS,)),
            dma((EXPERTS,)),
            dma((model_width // UNIT,)),
            dma((n, units)),
            dma((n,)),
            dma((n,)),
            dma((parts, n)),
            dma((parts, n)),
        ],
        compiler_params=pltpu.CompilerParams(
            collective_id=0, has_side_effects=True, vmem_limit_bytes=66_000_000
        ),
        name="fused",
    )(
        lengths,
        parents,
        routes.T,
        accepted,
        queries,
        tree_key_value,
        key_value_cache,
        residual,
        ffn_gain.reshape(line_count, LANES),
        router.T,
        next_embed,
        gate_weight,
        up_weight,
        down_weight,
        draft_fc,
    )
    return pl.pallas_call(
        finish_kernel,
        out_shape=(
            jax.ShapeDtypeStruct((TREE_NODES, model_width), bf16),
            jax.ShapeDtypeStruct((1, model_width), bf16),
        ),
        in_specs=[whole, whole],
        out_specs=(whole, whole),
        name="finish",
    )(layer, draft_lines)


def fits(lengths, gate_weight, draft_fc, n):
    model_width, width = gate_weight.shape
    depth = draft_fc.shape[0]
    return (
        lengths.shape[0] == 1
        and n == 4 * EXPERTS
        and width == 2 * SLICE
        and model_width == 6 * SLICE
        and depth % UNIT == 0
        and depth > UNIT
        and depth <= SLICE
        and n * depth == 2 * model_width
    )


def per_device(
    queries,
    tree_key_value,
    key_value_cache,
    lengths,
    parents,
    residual,
    ffn_gain,
    router,
    routes,
    gate_weight,
    up_weight,
    down_weight,
    accepted,
    next_embed,
    draft_fc,
):
    devices = lax.axis_size("expert")
    if fits(lengths, gate_weight, draft_fc, devices):
        return fused(
            queries,
            tree_key_value,
            key_value_cache,
            lengths,
            parents,
            residual,
            ffn_gain,
            router,
            routes,
            gate_weight,
            up_weight,
            down_weight,
            accepted,
            next_embed,
            draft_fc,
            devices,
        )
    context = attention(queries, tree_key_value, key_value_cache, lengths, parents)
    hidden_state = residual.astype(jnp.float32) + context
    normed = (
        hidden_state
        * lax.rsqrt(jnp.mean(hidden_state * hidden_state, axis=-1, keepdims=True) + EPSILON)
        * ffn_gain.astype(jnp.float32)
    ).astype(jnp.bfloat16)
    tokens_here, model_width = normed.shape
    logits = jnp.dot(normed, router, preferred_element_type=jnp.float32)
    expert_ids = jnp.arange(EXPERTS, dtype=jnp.int32)
    first_hit = (routes[:, 0:1] == expert_ids[None, :]).astype(jnp.float32)
    second_hit = (routes[:, 1:2] == expert_ids[None, :]).astype(jnp.float32)
    first_logit = jnp.sum(logits * first_hit, axis=-1)
    second_logit = jnp.sum(logits * second_hit, axis=-1)
    first_share = jax.nn.sigmoid(first_logit - second_logit)
    mixing = first_share[:, None] * first_hit + (1.0 - first_share)[:, None] * second_hit
    hit_table = first_hit + second_hit
    slot_rank = jnp.cumsum(hit_table, axis=0) - 1.0
    slot_ids = jnp.arange(CAP, dtype=jnp.float32)
    placing = hit_table.T[:, None, :] * (slot_rank.T[:, None, :] == slot_ids[None, :, None]).astype(
        jnp.float32
    )
    packed = jnp.einsum(
        "ect,td->ecd", placing.astype(jnp.bfloat16), normed, preferred_element_type=jnp.float32
    ).astype(jnp.bfloat16)
    grouped = moe(packed, gate_weight, up_weight, down_weight, devices)
    weighted = placing * mixing.T[:, None, :]
    expert_sum = jnp.einsum("ect,ecd->td", weighted, grouped, precision=lax.Precision.HIGHEST)
    layer_out = (hidden_state + expert_sum).astype(jnp.bfloat16)
    request_total = lengths.shape[0]
    picker = (accepted[:, None] == jnp.arange(TREE_NODES, dtype=jnp.int32)[None, :]).astype(
        jnp.bfloat16
    )
    picked = jnp.einsum(
        "rt,rtd->rd",
        picker,
        layer_out.reshape(request_total, TREE_NODES, model_width),
        preferred_element_type=jnp.float32,
    ).astype(jnp.bfloat16)
    draft_in = jnp.concatenate([picked, next_embed], axis=1)
    depth = draft_fc.shape[0]
    blocks = draft_in.reshape(request_total, devices, depth).transpose(1, 0, 2)
    draft_out = draft(blocks.astype(jnp.float32), draft_fc).astype(jnp.bfloat16)
    return (layer_out, draft_out)


def solution(mesh):
    return jax.shard_map(
        per_device,
        mesh=mesh,
        in_specs=(
            P(("groups", "expert"), None),
            P(("groups", "expert"), None, None),
            P(("groups", "expert"), None, None, None),
            P(("groups", "expert")),
            P(("groups", "expert")),
            P(("groups", "expert"), None),
            P(),
            P(),
            P(("groups", "expert"), None),
            P(None, "expert"),
            P(None, "expert"),
            P("expert", None),
            P(("groups", "expert")),
            P(("groups", "expert"), None),
            P("expert", None),
        ),
        out_specs=(P(("groups", "expert"), None), P(("groups", "expert"), None)),
        check_vma=False,
    )
```

```python
import functools

import jax
import jax.numpy as jnp
from jax import lax
from jax.experimental import pallas as pl
from jax.experimental.pallas import tpu as pltpu
from jax.sharding import PartitionSpec as P

QUERY_HEADS = 48
KEY_VALUE_HEADS = 8
HEAD_SIZE = 128
EXPERTS = 4
TREE_NODES = 6
CACHE_SLOTS = 512
CAP = 4


EPSILON = 1e-05


def related_kernel(parents, out):
    node_ids = lax.broadcasted_iota(jnp.int32, (1, out.shape[2]), 1)
    for request in range(out.shape[0]):
        reached = []
        for node in range(TREE_NODES):
            row = (node_ids == node).astype(jnp.float32)
            parent = parents[request * TREE_NODES + node]
            for earlier in range(node):
                row = row + jnp.where(parent == earlier, reached[earlier], 0.0)
            reached.append(row)
            out[request, node : node + 1, :] = row


def ancestors(parent_ids):
    table = pl.pallas_call(
        related_kernel,
        out_shape=jax.ShapeDtypeStruct((parent_ids.shape[0] // TREE_NODES, TREE_NODES, 128), jnp.float32),
        in_specs=[pl.BlockSpec(memory_space=pltpu.SMEM)],
        out_specs=pl.BlockSpec(memory_space=pltpu.VMEM),
        name="related",
    )(parent_ids)
    return table[:, :, :TREE_NODES] > 0.5


def attention(queries, tree_key_value, key_value_cache, lengths, parents):
    request_total = lengths.shape[0]
    query_head_count = queries.reshape(
        request_total, TREE_NODES, KEY_VALUE_HEADS, QUERY_HEADS // KEY_VALUE_HEADS, HEAD_SIZE
    )
    cached_key_rows = key_value_cache[:, 0].reshape(
        request_total, CACHE_SLOTS, KEY_VALUE_HEADS, HEAD_SIZE
    )
    cached_value_rows = key_value_cache[:, 1].reshape(
        request_total, CACHE_SLOTS, KEY_VALUE_HEADS, HEAD_SIZE
    )
    tree_key_rows = tree_key_value[:, 0].reshape(
        request_total, TREE_NODES, KEY_VALUE_HEADS, HEAD_SIZE
    )
    tree_value_rows = tree_key_value[:, 1].reshape(
        request_total, TREE_NODES, KEY_VALUE_HEADS, HEAD_SIZE
    )
    score_scale = HEAD_SIZE ** (-0.5)
    cache_scores = (
        jnp.einsum(
            "rtgqd,rlgd->rgtql",
            query_head_count,
            cached_key_rows,
            preferred_element_type=jnp.float32,
        )
        * score_scale
    )
    tree_scores = (
        jnp.einsum(
            "rtgqd,rugd->rgtqu", query_head_count, tree_key_rows, preferred_element_type=jnp.float32
        )
        * score_scale
    )
    visible = jnp.arange(CACHE_SLOTS, dtype=jnp.int32)[None, :] < lengths[:, None]
    related = ancestors(parents)
    cache_scores = jnp.where(visible[:, None, None, None, :], cache_scores, -1e30)
    tree_scores = jnp.where(related[:, None, :, None, :], tree_scores, -1e30)
    row_peak = jnp.maximum(jnp.max(cache_scores, axis=-1), jnp.max(tree_scores, axis=-1))[..., None]
    cache_exp = jnp.exp(cache_scores - row_peak)
    tree_exp = jnp.exp(tree_scores - row_peak)
    denominator = (jnp.sum(cache_exp, axis=-1) + jnp.sum(tree_exp, axis=-1))[..., None]
    cache_weights = (cache_exp / denominator).astype(jnp.bfloat16)
    tree_weights = (tree_exp / denominator).astype(jnp.bfloat16)
    context = jnp.einsum(
        "rgtql,rlgd->rtgqd", cache_weights, cached_value_rows, preferred_element_type=jnp.float32
    ) + jnp.einsum(
        "rgtqu,rugd->rtgqd", tree_weights, tree_value_rows, preferred_element_type=jnp.float32
    )
    return context.reshape(request_total * TREE_NODES, QUERY_HEADS * HEAD_SIZE)


VMEM_LIMIT = 66_000_000


def greet(n, me):
    barrier = pltpu.get_barrier_semaphore()

    def hello(k, carry):
        pl.semaphore_signal(barrier, inc=1, device_id={"expert": lax.rem(me + k, n)})
        return carry

    lax.fori_loop(1, n, hello, 0)
    pl.semaphore_wait(barrier, n - 1)


def push(src, dst, send_sem, recv_sem, peer):
    return pltpu.make_async_remote_copy(
        src_ref=src,
        dst_ref=dst,
        send_sem=send_sem,
        recv_sem=recv_sem,
        device_id={"expert": peer},
        device_id_type=pl.DeviceIdType.MESH,
    )


def moe_kernel(
    n,
    group_size,
    pair_slots,
    down_slots,
    packed,
    gate_hbm,
    up_hbm,
    down_hbm,
    grouped,
    gate_buf,
    up_buf,
    down_buf,
    arrived,
    rows_wide,
    rows,
    activation,
    result,
    leaving,
    returned,
    pair_sem,
    down_sem,
    out_sem,
    in_sem,
    back_out_sem,
    back_in_sem,
    own_sem,
):
    me = lax.axis_index("expert")
    width = gate_hbm.shape[1]
    chunk = gate_buf.shape[2]
    pair_count = width // chunk
    piece = down_buf.shape[2]
    piece_count = down_hbm.shape[1] // piece

    def pair_copies(i):
        slot = lax.rem(i, pair_slots)
        cols = pl.ds(pl.multiple_of(i * chunk, chunk), chunk)
        return (
            pltpu.make_async_copy(gate_hbm.at[:, cols], gate_buf.at[slot], pair_sem.at[0, slot]),
            pltpu.make_async_copy(up_hbm.at[:, cols], up_buf.at[slot], pair_sem.at[1, slot]),
        )

    def down_copy(i):
        slot = lax.rem(i, down_slots)
        cols = pl.ds(pl.multiple_of(i * piece, piece), piece)
        return pltpu.make_async_copy(down_hbm.at[:, cols], down_buf.at[slot], down_sem.at[slot])

    def start_pair(i, carry):
        for copy in pair_copies(i):
            copy.start()
        return carry

    def start_down(i, carry):
        down_copy(i).start()
        return carry

    lax.fori_loop(0, pair_slots, start_pair, 0)
    greet(n, me)

    def dispatch(k, carry):
        peer = lax.rem(me + k, n)
        push(
            packed.at[peer // group_size], arrived.at[me], out_sem.at[peer], in_sem.at[me], peer
        ).start()
        return carry

    lax.fori_loop(1, n, dispatch, 0)
    own = pltpu.make_async_copy(packed.at[me // group_size], arrived.at[me], own_sem)
    own.start()
    lax.fori_loop(0, down_slots, start_down, 0)
    own.wait()

    def take(k, carry):
        source = lax.rem(me + n - k, n)
        push(
            packed.at[0], arrived.at[source], out_sem.at[source], in_sem.at[source], source
        ).wait_recv()
        return carry

    lax.fori_loop(1, n, take, 0)

    def both(pair):
        return pl.ds(pl.multiple_of(pair * 2 * CAP, 2 * CAP), 2 * CAP)

    def widen(pair, carry):
        rows_wide[both(pair), :] = jnp.concatenate(
            [arrived[2 * pair].astype(jnp.float32), arrived[2 * pair + 1].astype(jnp.float32)],
            axis=0,
        )
        return carry

    lax.fori_loop(0, n // 2, widen, 0)
    rows[...] = rows_wide[...].astype(jnp.bfloat16)

    def pair_step(i, carry):
        slot = lax.rem(i, pair_slots)
        for copy in pair_copies(i):
            copy.wait()
        gate_val = jnp.dot(rows[...], gate_buf[slot], preferred_element_type=jnp.float32)
        up_val = jnp.dot(rows[...], up_buf[slot], preferred_element_type=jnp.float32)
        cols = pl.ds(pl.multiple_of(i * chunk, chunk), chunk)
        activation[:, cols] = (jax.nn.silu(gate_val) * up_val).astype(jnp.bfloat16)

        @pl.when(i + pair_slots < pair_count)
        def _():
            start_pair(i + pair_slots, 0)

        return carry

    lax.fori_loop(0, pair_count, pair_step, 0)

    def down_step(i, carry):
        slot = lax.rem(i, down_slots)
        down_copy(i).wait()
        result[...] = jnp.dot(
            activation[...], down_buf[slot], preferred_element_type=jnp.float32
        )

        @pl.when(i + down_slots < piece_count)
        def _():
            start_down(i + down_slots, 0)

        def narrow(pair, inner):
            block = result[both(pair), :]
            leaving[2 * pair, i] = block[:CAP].astype(jnp.bfloat16)
            leaving[2 * pair + 1, i] = block[CAP:].astype(jnp.bfloat16)
            return inner

        lax.fori_loop(0, n // 2, narrow, 0)

        def send_back(k, inner):
            peer = lax.rem(me + k, n)
            push(
                leaving.at[peer, i],
                returned.at[me, i],
                back_out_sem.at[peer],
                back_in_sem.at[me],
                peer,
            ).start()
            return inner

        lax.fori_loop(1, n, send_back, 0)
        return carry

    lax.fori_loop(0, piece_count, down_step, 0)
    returned[me] = leaving[me]

    def drain(k, carry):
        peer = lax.rem(me + n - k, n)
        push(
            leaving.at[peer], returned.at[peer], back_out_sem.at[peer], back_in_sem.at[peer], peer
        ).wait()
        push(
            packed.at[0], arrived.at[peer], out_sem.at[peer], in_sem.at[peer], peer
        ).wait_send()
        return carry

    lax.fori_loop(1, n, drain, 0)

    def gather(expert, carry):
        for i in range(piece_count):

            def add(member, total):
                return total + returned[expert * group_size + member, i].astype(jnp.float32)

            grouped[expert, :, i * piece : (i + 1) * piece] = lax.fori_loop(
                0, group_size, add, jnp.zeros((CAP, piece), jnp.float32)
            )
        return carry

    lax.fori_loop(0, EXPERTS, gather, 0)


def moe(packed, gate_weight, up_weight, down_weight, n):
    model_width, width = gate_weight.shape
    row_count = n * CAP
    chunk = min(512, width)
    piece = model_width // 4
    pair_slots = min(3, width // chunk)
    down_slots = min(2, model_width // piece)
    anywhere = pl.BlockSpec(memory_space=pl.ANY)
    whole = pl.BlockSpec(memory_space=pltpu.VMEM)
    bf16, f32 = jnp.bfloat16, jnp.float32
    return pl.pallas_call(
        functools.partial(moe_kernel, n, n // EXPERTS, pair_slots, down_slots),
        out_shape=jax.ShapeDtypeStruct((EXPERTS, CAP, model_width), f32),
        in_specs=[whole, anywhere, anywhere, anywhere],
        out_specs=whole,
        scratch_shapes=[
            pltpu.VMEM((pair_slots, model_width, chunk), bf16),
            pltpu.VMEM((pair_slots, model_width, chunk), bf16),
            pltpu.VMEM((down_slots, width, piece), bf16),
            pltpu.VMEM((n, CAP, model_width), bf16),
            pltpu.VMEM((row_count, model_width), f32),
            pltpu.VMEM((row_count, model_width), bf16),
            pltpu.VMEM((row_count, width), bf16),
            pltpu.VMEM((row_count, piece), f32),
            pltpu.VMEM((n, model_width // piece, CAP, piece), bf16),
            pltpu.VMEM((n, model_width // piece, CAP, piece), bf16),
            pltpu.SemaphoreType.DMA((2, pair_slots)),
            pltpu.SemaphoreType.DMA((down_slots,)),
            pltpu.SemaphoreType.DMA((n,)),
            pltpu.SemaphoreType.DMA((n,)),
            pltpu.SemaphoreType.DMA((n,)),
            pltpu.SemaphoreType.DMA((n,)),
            pltpu.SemaphoreType.DMA,
        ],
        compiler_params=pltpu.CompilerParams(
            collective_id=0, has_side_effects=True, vmem_limit_bytes=VMEM_LIMIT
        ),
        name="moe",
    )(packed, gate_weight, up_weight, down_weight)


def draft_kernel(
    n,
    share,
    piece,
    blocks,
    fc_hbm,
    out,
    fc_buf,
    arrived,
    rows_wide,
    result,
    leaving,
    returned,
    fc_sem,
    out_sem,
    in_sem,
    back_out_sem,
    back_in_sem,
):
    me = lax.axis_index("expert")
    piece_count = fc_hbm.shape[1] // piece
    half = piece // 2

    def fc_copy(i):
        cols = pl.ds(pl.multiple_of(i * piece, piece), piece)
        return pltpu.make_async_copy(fc_hbm.at[:, cols], fc_buf.at[i], fc_sem.at[i])

    def start_fc(i, carry):
        fc_copy(i).start()
        return carry

    lax.fori_loop(0, piece_count, start_fc, 0)
    greet(n, me)

    def dispatch(k, carry):
        peer = lax.rem(me + k, n)
        push(blocks.at[peer], arrived.at[me], out_sem.at[peer], in_sem.at[me], peer).start()
        return carry

    lax.fori_loop(1, n, dispatch, 0)
    rows_wide[pl.ds(me * share, share), :] = blocks[me]

    def take(k, carry):
        source = lax.rem(me + n - k, n)
        push(
            blocks.at[source], arrived.at[source], out_sem.at[source], in_sem.at[source], source
        ).wait()
        rows_wide[pl.ds(source * share, share), :] = arrived[source]
        return carry

    lax.fori_loop(1, n, take, 0)

    def step(i, carry):
        fc_copy(i).wait()
        result[...] = jnp.dot(
            rows_wide[...].astype(jnp.bfloat16), fc_buf[i], preferred_element_type=jnp.float32
        )

        def split(source, inner):
            block = result[pl.ds(source * share, share), :]
            leaving[source, i] = jnp.concatenate(
                [block[:, :half], block[:, half:]], axis=0
            ).astype(jnp.bfloat16)
            return inner

        lax.fori_loop(0, n, split, 0)

        def send_back(k, inner):
            peer = lax.rem(me + k, n)
            push(
                leaving.at[peer, i],
                returned.at[me, i],
                back_out_sem.at[peer],
                back_in_sem.at[me],
                peer,
            ).start()
            return inner

        lax.fori_loop(1, n, send_back, 0)
        return carry

    lax.fori_loop(0, piece_count, step, 0)
    returned[me] = leaving[me]

    def drain(k, carry):
        peer = lax.rem(me + n - k, n)
        push(
            leaving.at[peer], returned.at[peer], back_out_sem.at[peer], back_in_sem.at[peer], peer
        ).wait()
        return carry

    lax.fori_loop(1, n, drain, 0)
    for i in range(piece_count):

        def add(source, total):
            return total + returned[source, i].astype(jnp.float32)

        total = lax.fori_loop(0, n, add, jnp.zeros((2 * share, half), jnp.float32))
        out[:, i * piece : i * piece + half] = total[:share]
        out[:, i * piece + half : (i + 1) * piece] = total[share:]


def draft(blocks, draft_fc):
    n, share, depth = blocks.shape
    model_width = draft_fc.shape[1]
    piece = model_width // 4
    pieces = model_width // piece
    whole = pl.BlockSpec(memory_space=pltpu.VMEM)
    f32 = jnp.float32
    return pl.pallas_call(
        functools.partial(draft_kernel, n, share, piece),
        out_shape=jax.ShapeDtypeStruct((share, model_width), f32),
        in_specs=[whole, pl.BlockSpec(memory_space=pl.ANY)],
        out_specs=whole,
        scratch_shapes=[
            pltpu.VMEM((pieces, depth, piece), jnp.bfloat16),
            pltpu.VMEM((n, share, depth), f32),
            pltpu.VMEM((n * share, depth), f32),
            pltpu.VMEM((n * share, piece), f32),
            pltpu.VMEM((n, pieces, 2 * share, piece // 2), jnp.bfloat16),
            pltpu.VMEM((n, pieces, 2 * share, piece // 2), jnp.bfloat16),
            pltpu.SemaphoreType.DMA((pieces,)),
            pltpu.SemaphoreType.DMA((n,)),
            pltpu.SemaphoreType.DMA((n,)),
            pltpu.SemaphoreType.DMA((n,)),
            pltpu.SemaphoreType.DMA((n,)),
        ],
        compiler_params=pltpu.CompilerParams(
            collective_id=1, has_side_effects=True, vmem_limit_bytes=VMEM_LIMIT
        ),
        name="draft",
    )(blocks, draft_fc)


SLICE = 1024
LANES = 128
UNIT = 256


def greet_all(n, me):
    barrier = pltpu.get_barrier_semaphore()

    def hello(k, carry):
        pl.semaphore_signal(barrier, inc=1, device_id={"expert": lax.rem(me + k, n)})
        return carry

    lax.fori_loop(1, n, hello, 0)
    return barrier


def fused_kernel(
    n,
    slots,
    lengths_hbm,
    parents_hbm,
    routes_hbm,
    accepted_hbm,
    queries_hbm,
    tree_hbm,
    cache_hbm,
    residual_hbm,
    gain_hbm,
    router_hbm,
    embed_hbm,
    gate_hbm,
    up_hbm,
    down_hbm,
    fc_hbm,
    layer_out,
    draft_out,
    lengths,
    parents,
    routes,
    accepted,
    weights,
    queries,
    tree,
    keys,
    values,
    residual,
    gain,
    router,
    embed,
    tree_rows,
    hidden,
    normed,
    packed,
    arrived,
    rows,
    gate_sum,
    up_sum,
    activation,
    kept,
    leaving,
    returned,
    chip_sum,
    chip_leaving,
    chip_returned,
    home_leaving,
    home_returned,
    pick_rows,
    pick_arrived,
    shares,
    share_leaving,
    share_rows,
    hidden_row,
    embed_row,
    blocks,
    block_rows,
    draft_sum,
    draft_wide,
    draft_leaving,
    draft_returned,
    load_sem,
    input_sem,
    out_sem,
    in_sem,
    plane_out_sem,
    plane_in_sem,
    core_out_sem,
    core_in_sem,
    chip_out_sem,
    chip_in_sem,
    home_out_sem,
    home_in_sem,
    pick_out_sem,
    pick_in_sem,
    share_out_sem,
    share_in_sem,
    block_out_sem,
    block_in_sem,
    draft_out_sem,
    draft_in_sem,
):
    bf16, f32 = jnp.bfloat16, jnp.float32
    me = lax.axis_index("expert")
    group = n // EXPERTS
    mine = me // group
    lane = lax.rem(me, group)
    core = lax.rem(lane, 2)
    across = lane // 2
    core_peer = mine * group + across * 2 + (1 - core)
    chip_peer = mine * group + (1 - across) * 2 + core
    model_width = down_hbm.shape[1]
    width = down_hbm.shape[0]
    depth = fc_hbm.shape[0]
    slice_count = model_width // SLICE
    half_count = width // SLICE
    half = SLICE // 2
    chunks = [(0, half), (half, half)] + [(k * SLICE, SLICE) for k in range(1, slice_count)]
    last = model_width - SLICE
    pieces = [(k * SLICE, SLICE) for k in range(slice_count - 1)]
    pieces += [(last, SLICE - UNIT), (model_width - UNIT, UNIT)]
    piece_count = len(pieces)
    unit_count = depth // UNIT
    block_count = model_width // depth
    padded = 8
    share = EXPERTS * CAP
    cache_slots = cache_hbm.shape[2]
    key_rows = keys.shape[0]
    line_count = model_width // LANES
    lines = SLICE // LANES
    part_count = draft_leaving.shape[0]

    pairs = [
        ("pair", k, h, i) for k in range(slice_count) for h in range(half_count) for i in range(2)
    ]
    downs = [("down", p, a) for p in range(piece_count) for a in range(half_count)]
    order = pairs + downs + [("fc", p) for p in range(slice_count)]
    place = {item: i for i, item in enumerate(order)}
    sem_count = load_sem.shape[0]

    def load_group(item):
        if item[0] == "pair":
            return item[1]
        if item[0] == "down":
            return slice_count + item[1]
        return slice_count + piece_count

    def wait_loads(item):
        if item[0] == "pair":
            view = weights.at[0 : 2 * half_count]
        elif item[0] == "down":
            view = weights.at[0:half_count, :, 0 : pieces[item[1]][1]]
        else:
            view = weights.at[0:slice_count, 0:depth, :]
        pltpu.make_async_copy(view, view, load_sem.at[load_group(item) % sem_count]).wait()

    def load_copy(item):
        i = place[item]
        slot = weights.at[i % slots]
        if item[0] == "pair":
            k, h = item[1], item[2]
            source = (gate_hbm, up_hbm)[item[3]]
            view = source.at[k * SLICE : (k + 1) * SLICE, h * SLICE : (h + 1) * SLICE]
        elif item[0] == "down":
            a = item[2]
            start, size = pieces[item[1]]
            view = down_hbm.at[a * SLICE : (a + 1) * SLICE, start : start + size]
            slot = weights.at[i % slots, :, 0:size]
        else:
            p = item[1]
            view = fc_hbm.at[:, p * SLICE : (p + 1) * SLICE]
            slot = weights.at[i % slots, 0:depth, :]
        return pltpu.make_async_copy(view, slot, load_sem.at[load_group(item) % sem_count])

    def start_load(i):
        if i < len(order):
            load_copy(order[i]).start()

    inputs = [
        pltpu.make_async_copy(source, target, input_sem.at[i])
        for i, (source, target) in enumerate(
            [
                (queries_hbm, queries),
                (tree_hbm, tree),
                (cache_hbm.at[0, 0], keys.at[0:cache_slots, :]),
                (residual_hbm, residual),
                (cache_hbm.at[0, 1], values.at[0:cache_slots, :]),
                (gain_hbm, gain),
                (router_hbm, router),
                (embed_hbm, embed),
                (lengths_hbm, lengths),
                (parents_hbm, parents),
                (routes_hbm, routes),
                (accepted_hbm, accepted),
            ]
        )
    ]
    for copy in inputs[8:] + inputs[:8]:
        copy.start()
    barrier = greet_all(n, me)
    for copy in inputs[8:]:
        copy.wait()

    row8 = lax.broadcasted_iota(jnp.int32, (padded, LANES), 0)
    col8 = lax.broadcasted_iota(jnp.int32, (padded, LANES), 1)
    node_ids = lax.broadcasted_iota(jnp.int32, (1, LANES), 1)
    reached = []
    related = jnp.zeros((padded, LANES), f32)
    for node in range(TREE_NODES):
        row = (node_ids == node).astype(f32)
        parent = parents[node]
        for earlier in range(node):
            row = row + jnp.where(parent == earlier, reached[earlier], 0.0)
        reached.append(row)
        related = related + jnp.where(row8 == node, row, 0.0)
    slot_ids = lax.broadcasted_iota(jnp.int32, (padded, cache_slots), 1)
    bias = jnp.concatenate(
        [
            jnp.where(slot_ids < lengths[0], 0.0, -1e30),
            jnp.where(related > 0.5, 0.0, -1e30),
        ],
        axis=1,
    )
    heads_each = QUERY_HEADS // KEY_VALUE_HEADS
    bias = jnp.concatenate([bias] * heads_each, axis=0)

    def named(choice, token):
        expert = routes[choice, token]
        rank = jnp.int32(0)
        for earlier in range(token):
            for other in range(2):
                rank = rank + jnp.where(routes[other, earlier] == expert, 1, 0)
        return expert, rank

    places = [[named(choice, token) for choice in range(2)] for token in range(TREE_NODES)]

    for copy in inputs[:3]:
        copy.wait()
    for i in range(slots):
        start_load(i)
    tree_rows[...] = jnp.zeros_like(tree_rows)
    for token in range(TREE_NODES):
        both = tree[token].astype(f32)
        tree_rows[0, token : token + 1, :] = both[0:1]
        tree_rows[1, token : token + 1, :] = both[1:2]
    tile = tree_rows.shape[1]
    blank = jnp.zeros((key_rows - cache_slots - tile, keys.shape[1]), bf16)
    keys[cache_slots : cache_slots + tile, :] = tree_rows[0].astype(bf16)
    keys[cache_slots + tile :, :] = blank
    values[cache_slots : cache_slots + tile, :] = tree_rows[1].astype(bf16)
    values[cache_slots + tile :, :] = blank
    spare = jnp.zeros((padded - TREE_NODES, HEAD_SIZE), f32)
    score_scale = HEAD_SIZE ** (-0.5)
    weights_of = []
    for g in range(KEY_VALUE_HEADS):
        parts = []
        for q in range(heads_each):
            head = g * heads_each + q
            parts.append(queries[:, head * HEAD_SIZE : (head + 1) * HEAD_SIZE].astype(f32))
            parts.append(spare)
        head_queries = jnp.concatenate(parts, axis=0).astype(bf16)
        scores = (
            lax.dot_general(
                head_queries,
                keys[:, g * HEAD_SIZE : (g + 1) * HEAD_SIZE],
                (((1,), (1,)), ((), ())),
                preferred_element_type=f32,
            )
            * score_scale
            + bias
        )
        peak = jnp.max(scores, axis=-1, keepdims=True)
        grown = jnp.exp(scores - peak)
        total = jnp.sum(grown, axis=-1, keepdims=True)
        weights_of.append((grown * (1.0 / total)).astype(bf16))
    for copy in inputs[3:5]:
        copy.wait()
    square = jnp.zeros((padded, HEAD_SIZE), f32)
    for g in range(KEY_VALUE_HEADS):
        context = jnp.dot(
            weights_of[g],
            values[:, g * HEAD_SIZE : (g + 1) * HEAD_SIZE],
            preferred_element_type=f32,
        )
        for q in range(heads_each):
            head = g * heads_each + q
            cols = slice(head * HEAD_SIZE, (head + 1) * HEAD_SIZE)
            state = context[q * padded : (q + 1) * padded] + jnp.concatenate(
                [residual[:, cols].astype(f32), spare], axis=0
            )
            hidden[:, cols] = state
            square = square + state * state
    for copy in inputs[5:8]:
        copy.wait()
    level = lax.rsqrt(jnp.sum(square, axis=-1, keepdims=True) / model_width + EPSILON)

    slot_row = lax.broadcasted_iota(jnp.int32, (EXPERTS * padded, padded), 0)
    slot_col = lax.broadcasted_iota(jnp.int32, (EXPERTS * padded, padded), 1)
    placing = jnp.zeros((EXPERTS * padded, padded), f32)
    for token, choices in enumerate(places):
        for expert, rank in choices:
            placing = placing + jnp.where(
                (slot_row == expert * padded + rank) & (slot_col == token), 1.0, 0.0
            )
    placing = placing.astype(bf16)

    def to_plane(c, step):
        plane = lax.rem(mine + step, EXPERTS)
        cols = pl.ds(chunks[c][0], chunks[c][1])
        return push(
            packed.at[plane, :, cols],
            arrived.at[mine, :, cols],
            out_sem,
            in_sem.at[c],
            plane * group + lane,
        )

    def awaited(ref, sem):
        return push(ref, ref, sem, sem, core_peer)

    def pack_step(c):
        start, size = chunks[c]
        cols = slice(start, start + size)
        gains = [
            gain[t : t + 1, :].astype(f32)
            for t in range(start // LANES, (start + size) // LANES)
        ]
        normal = (hidden[:, cols] * level * jnp.concatenate(gains, axis=1)).astype(bf16)
        normed[:, cols] = normal
        spread = jnp.dot(placing, normal, preferred_element_type=f32)
        for e in range(EXPERTS):
            packed[e, :, cols] = spread[e * padded : e * padded + CAP].astype(bf16)
        arrived[mine, :, cols] = packed[mine, :, cols]

    pack_step(0)
    pl.semaphore_wait(barrier, n - 1)
    for c in range(len(chunks)):
        if c > 0:
            pack_step(c)
        for step in range(1, EXPERTS):
            to_plane(c, step).start()

    token_row = row8[:, 0:1]
    embed_row[...] = embed[...].astype(f32)
    for k in range(slice_count):
        cols = slice(k * SLICE, (k + 1) * SLICE)
        hidden_row[:, cols] = jnp.sum(
            jnp.where(token_row == accepted[0], hidden[:, cols], 0.0), axis=0, keepdims=True
        )

    def block_push(row, b, j):
        source = row.at[:, b * depth : (b + 1) * depth]
        return push(source, blocks.at[me], block_out_sem, block_in_sem, j)

    def send_block(row, b, j):
        @pl.when(me != j)
        def _():
            block_push(row, b, j).start()

        @pl.when(me == j)
        def _():
            blocks[j] = row[:, b * depth : (b + 1) * depth]

    for b in range(block_count):
        send_block(embed_row, b, block_count + b)
        send_block(hidden_row, b, b)

    logits = [jnp.zeros((padded, 1), f32) for _ in range(EXPERTS)]
    for k in range(slice_count):
        cols = slice(k * SLICE, (k + 1) * SLICE)
        normal = normed[:, cols].astype(f32)
        for e in range(EXPERTS):
            logits[e] = logits[e] + jnp.sum(
                normal * router[e : e + 1, cols].astype(f32), axis=-1, keepdims=True
            )
    ids = [jnp.full((padded, 1), -1, jnp.int32) for _ in range(4)]
    for token, choices in enumerate(places):
        for choice, (expert, rank) in enumerate(choices):
            ids[choice] = jnp.where(token_row == token, expert, ids[choice])
            ids[2 + choice] = jnp.where(token_row == token, expert * CAP + rank, ids[2 + choice])
    first_logit = jnp.zeros((padded, 1), f32)
    second_logit = jnp.zeros((padded, 1), f32)
    for e in range(EXPERTS):
        first_logit = first_logit + jnp.where(ids[0] == e, logits[e], 0.0)
        second_logit = second_logit + jnp.where(ids[1] == e, logits[e], 0.0)
    first_share = jax.nn.sigmoid(first_logit - second_logit)
    share_col = col8[:, :share]
    weighted = jnp.where(share_col == ids[2], first_share, 0.0) + jnp.where(
        share_col == ids[3], 1.0 - first_share, 0.0
    )

    def split(exact):
        high = exact.astype(bf16).astype(f32)
        middle = (exact - high).astype(bf16).astype(f32)
        low = exact - high - middle
        return jnp.concatenate([high, middle, low], axis=0).astype(bf16)

    mixers = split(weighted)

    def pick_push(step):
        plane = lax.rem(mine + step, EXPERTS)
        return push(
            pick_rows.at[plane],
            pick_arrived.at[mine],
            pick_out_sem,
            pick_in_sem,
            plane * group + lane,
        )

    for e in range(EXPERTS):
        chosen = jnp.zeros((padded, LANES), f32)
        for expert, position, portion in (
            (ids[0], ids[2], first_share),
            (ids[1], ids[3], 1.0 - first_share),
        ):
            here = (col8 == mine * CAP + position - expert * CAP) & (expert == e)
            chosen = chosen + jnp.where(here, portion, 0.0)
        pick_rows[e] = jnp.sum(
            jnp.where(token_row == accepted[0], chosen, 0.0), axis=0, keepdims=True
        )
    for step in range(1, EXPERTS):
        pick_push(step).start()
    pick_arrived[mine] = pick_rows[mine]

    def row_push(c, which, sem, peer):
        start, size = chunks[c]
        block = rows.at[pl.ds(pl.multiple_of(which * share, share), share), pl.ds(start, size)]
        return push(block, block, plane_out_sem, plane_in_sem.at[c, sem], peer)

    chip_lane = (1 - across) * 2 + core

    def gather_step(k):
        start, size = chunks[k]
        cols = slice(start, start + size)
        awaited(arrived.at[0 : EXPERTS - 1, :, pl.ds(start, size)], in_sem.at[k]).wait_recv()
        rows[pl.ds(pl.multiple_of(lane * share, share), share), cols] = jnp.concatenate(
            [arrived[s, :, cols].astype(f32) for s in range(EXPERTS)], axis=0
        ).astype(bf16)
        row_push(k, lane, 0, chip_peer).start()
        row_push(k, lane, 1, core_peer).start()

    def forward_step(k):
        row_push(k, chip_lane, 0, chip_peer).wait_recv()
        row_push(k, chip_lane, 1, core_peer).start()

    def expert_step(c):
        start, size = chunks[c]
        pair_rows = rows.at[0 : 2 * share, pl.ds(start, size)]
        awaited(pair_rows, plane_in_sem.at[c, 1]).wait_recv()
        k, first = start // SLICE, start % SLICE
        final = start + size == model_width
        if first == 0:
            wait_loads(("pair", k))
        for h in range(half_count):
            cols = slice(h * SLICE, (h + 1) * SLICE)
            sums = []
            for i, total in ((0, gate_sum), (1, up_sum)):
                item = ("pair", k, h, i)
                value = jnp.dot(
                    rows[:, start : start + size],
                    weights[place[item] % slots, first : first + size, :],
                    preferred_element_type=f32,
                )
                if start > 0:
                    value = value + total[:, cols]
                if not final:
                    total[:, cols] = value
                sums.append(value)
                if first + size == SLICE:
                    start_load(place[item] + slots)
            if final:
                activation[h] = (jax.nn.silu(sums[0]) * sums[1]).astype(bf16)

    for t in range(len(chunks) + 3):
        if t < len(chunks):
            gather_step(t)
        if 0 <= t - 2 < len(chunks):
            forward_step(t - 2)
        if 0 <= t - 3 < len(chunks):
            expert_step(t - 3)

    def piece_cols(p):
        return pl.ds(pieces[p][0], pieces[p][1])

    def core_push(p):
        cols = piece_cols(p)
        return push(
            leaving.at[:, :, cols],
            returned.at[:, :, cols],
            core_out_sem,
            core_in_sem.at[p],
            core_peer,
        )

    def chip_push(p):
        cols = piece_cols(p)
        return push(
            chip_leaving.at[:, cols],
            chip_returned.at[:, cols],
            chip_out_sem,
            chip_in_sem.at[p],
            chip_peer,
        )

    def to_home(p, step):
        plane = lax.rem(mine + step, EXPERTS)
        return push(
            home_leaving.at[plane, :, piece_cols(p)],
            home_returned.at[mine, :, piece_cols(p)],
            home_out_sem,
            home_in_sem,
            plane * group + lane,
        )

    def partial_step(p):
        start, size = pieces[p]
        cols = slice(start, start + size)
        partial = None
        wait_loads(("down", p))
        for a in range(half_count):
            item = ("down", p, a)
            value = jnp.dot(
                activation[a], weights[place[item] % slots, :, 0:size], preferred_element_type=f32
            )
            partial = value if partial is None else partial + value
            start_load(place[item] + slots)
        for member in range(group):
            block = partial[member * share : (member + 1) * share].astype(bf16)
            a, c = member // 2, member % 2

            @pl.when(core == c)
            def _():
                kept[a, :, cols] = block

            @pl.when(core != c)
            def _():
                leaving[a, :, cols] = block

        core_push(p).start()

    def core_step(p):
        core_push(p).wait_recv()
        start, size = pieces[p]
        cols = slice(start, start + size)
        far = 1 - across
        chip_leaving[:, cols] = (
            kept[far, :, cols].astype(f32) + returned[far, :, cols].astype(f32)
        ).astype(bf16)
        chip_push(p).start()
        chip_sum[:, cols] = kept[across, :, cols].astype(f32) + returned[across, :, cols].astype(
            f32
        )

    def share_push(unit, b):
        part = unit % unit_count
        return push(
            share_leaving.at[unit],
            shares.at[part, me],
            share_out_sem,
            share_in_sem.at[part // (unit_count - 1)],
            b,
        )

    def chip_step(p, pick_mixers):
        chip_push(p).wait_recv()
        start, size = pieces[p]
        cols = slice(start, start + size)
        total = chip_sum[:, cols] + chip_returned[:, cols].astype(f32)
        mixed = jnp.dot(pick_mixers, total.astype(bf16), preferred_element_type=f32)
        portion = mixed[:padded] + mixed[padded : 2 * padded] + mixed[2 * padded :]
        for unit in range(start // UNIT, (start + size) // UNIT):
            b = unit // unit_count
            first = unit * UNIT - start
            value = portion[:EXPERTS, first : first + UNIT].astype(bf16)

            @pl.when(me != b)
            def _():
                share_leaving[unit] = value
                share_push(unit, b).start()

            @pl.when(me == b)
            def _():
                shares[unit % unit_count, b] = value

        for s in range(EXPERTS):
            home_leaving[s, :, cols] = total[s * CAP : (s + 1) * CAP].astype(bf16)
        for step in range(1, EXPERTS):
            to_home(p, step).start()
        home_returned[mine, :, cols] = home_leaving[mine, :, cols]

    def home_step(p):
        start, size = pieces[p]
        cols = slice(start, start + size)
        block = jnp.concatenate(
            [home_returned[e, :, cols].astype(f32) for e in range(EXPERTS)], axis=0
        ).astype(bf16)
        mixed = jnp.dot(mixers, block, preferred_element_type=f32)
        expert_sum = mixed[:padded] + mixed[padded : 2 * padded] + mixed[2 * padded :]
        result = (hidden[:, cols] + expert_sum).astype(bf16)
        layer_out[:, cols] = result[:TREE_NODES]

    def draft_push(q, peer, at):
        return push(
            draft_leaving.at[q, peer],
            draft_returned.at[q, at],
            draft_out_sem,
            draft_in_sem,
            peer,
        )

    def row_of(device):
        return lax.rem(device, group) * EXPERTS + device // group

    def block_step():
        awaited(blocks.at[0 : n - 1], block_in_sem).wait_recv()

        def take(source, carry):
            block_rows[pl.ds(row_of(source), 1), :] = blocks[source]
            return carry

        lax.fori_loop(0, n, take, 0)
        share_rows[...] = jnp.zeros_like(share_rows)

    def share_step(first, past):
        @pl.when(me < block_count)
        def _():
            sem = share_in_sem.at[first // (unit_count - 1)]
            awaited(shares.at[first:past, 0 : n - 1], sem).wait_recv()
            for part in range(first, past):
                sums = []
                for member in range(group):
                    total = shares[part, member].astype(f32)
                    for e in range(1, EXPERTS):
                        total = total + shares[part, e * group + member].astype(f32)
                    sums.append(total)
                share_rows[:, part * UNIT : (part + 1) * UNIT] = jnp.concatenate(sums, axis=0)

    def draft_step(first, past, final):
        share_step(first, past)
        deep = slice(first * UNIT, past * UNIT)
        draft_rows = (block_rows[:, deep] + share_rows[:, deep]).astype(bf16)
        per_part = slice_count // part_count
        if first == 0:
            wait_loads(("fc",))
        for q in range(part_count):
            for p in range(q * per_part, (q + 1) * per_part):
                item = ("fc", p)
                partial = jnp.dot(
                    draft_rows, weights[place[item] % slots, deep, :], preferred_element_type=f32
                )
                cols = slice(p * SLICE, (p + 1) * SLICE)
                if first > 0:
                    partial = partial + draft_sum[:, cols]
                if not final:
                    draft_sum[:, cols] = partial
                    continue
                for t in range(lines):
                    draft_wide[pl.ds(p * lines + t, n, stride=line_count), :] = partial[
                        :, t * LANES : (t + 1) * LANES
                    ]
            if not final:
                continue
            each = line_count // part_count
            for row in range(n):
                device = row % EXPERTS * group + row // EXPERTS
                start = row * line_count + q * each
                draft_leaving[q, device] = draft_wide[start : start + each, :].astype(bf16)

            def send_partial(k, carry):
                draft_push(q, lax.rem(me + k, n), me).start()
                return carry

            lax.fori_loop(1, n, send_partial, 0)
            draft_returned[q, me] = draft_leaving[q, me]

    awaited(pick_arrived.at[0 : EXPERTS - 1], pick_in_sem).wait_recv()
    picks = jnp.concatenate(
        [pick_arrived[s][:, :share] for s in range(EXPERTS)]
        + [jnp.zeros((padded - EXPERTS, share), f32)],
        axis=0,
    )
    pick_mixers = split(picks)

    for p in range(piece_count + 3):
        if p < piece_count:
            partial_step(p)
        if 0 <= p - 1 < piece_count:
            core_step(p - 1)
        if p == piece_count:
            block_step()
        if 0 <= p - 3 < piece_count:
            chip_step(p - 3, pick_mixers)
    draft_step(0, unit_count - 1, False)
    draft_step(unit_count - 1, unit_count, True)
    awaited(home_returned.at[0 : EXPERTS - 1], home_in_sem).wait_recv()
    for p in range(piece_count):
        home_step(p)

    awaited(packed.at[0 : EXPERTS - 1], out_sem).wait_send()
    awaited(rows.at[0 : 3 * share, :], plane_out_sem).wait_send()
    awaited(pick_rows.at[0 : EXPERTS - 1], pick_out_sem).wait_send()
    awaited(leaving, core_out_sem).wait_send()
    awaited(chip_leaving, chip_out_sem).wait_send()
    awaited(home_leaving.at[0 : EXPERTS - 1], home_out_sem).wait_send()
    awaited(blocks.at[0 : n - 1], block_out_sem).wait_send()
    unit_total = share_leaving.shape[0]

    @pl.when(me < block_count)
    def _():
        awaited(share_leaving.at[0 : unit_total - unit_count], share_out_sem).wait_send()

    @pl.when(me >= block_count)
    def _():
        awaited(share_leaving, share_out_sem).wait_send()

    awaited(draft_leaving.at[:, 0 : n - 1], draft_out_sem).wait_send()
    awaited(draft_returned.at[:, 0 : n - 1], draft_in_sem).wait_recv()
    each = line_count // part_count
    for q in range(part_count):
        total = draft_returned[q, 0].astype(f32)
        for source in range(1, n):
            total = total + draft_returned[q, source].astype(f32)
        draft_out[q * each : (q + 1) * each, :] = total


def finish_kernel(layer, draft_lines, layer_out, draft_out):
    layer_out[...] = layer[...]
    for t in range(draft_lines.shape[0]):
        draft_out[:, t * LANES : (t + 1) * LANES] = draft_lines[t : t + 1, :].astype(jnp.bfloat16)


def fused(
    queries,
    tree_key_value,
    key_value_cache,
    lengths,
    parents,
    residual,
    ffn_gain,
    router,
    routes,
    gate_weight,
    up_weight,
    down_weight,
    accepted,
    next_embed,
    draft_fc,
    n,
):
    width, model_width = down_weight.shape
    depth = draft_fc.shape[0]
    group = n // EXPERTS
    share = EXPERTS * CAP
    slots = 24
    slices = model_width // SLICE
    halves = width // SLICE
    parts = 3
    pieces = slices + 1
    chunks = slices + 1
    units = depth // UNIT
    line_count = model_width // LANES
    kv_width = tree_key_value.shape[2]
    key_rows = key_value_cache.shape[2] + LANES
    anywhere = pl.BlockSpec(memory_space=pl.ANY)
    whole = pl.BlockSpec(memory_space=pltpu.VMEM)
    bf16, f32 = jnp.bfloat16, jnp.float32
    dma = pltpu.SemaphoreType.DMA
    layer, draft_lines = pl.pallas_call(
        functools.partial(fused_kernel, n, slots),
        out_shape=(
            jax.ShapeDtypeStruct((TREE_NODES, model_width), bf16),
            jax.ShapeDtypeStruct((line_count, LANES), f32),
        ),
        in_specs=[anywhere] * 15,
        out_specs=(whole, whole),
        scratch_shapes=[
            pltpu.SMEM(lengths.shape, jnp.int32),
            pltpu.SMEM(parents.shape, jnp.int32),
            pltpu.SMEM(routes.T.shape, jnp.int32),
            pltpu.SMEM(accepted.shape, jnp.int32),
            pltpu.VMEM((slots, SLICE, SLICE), bf16),
            pltpu.VMEM((TREE_NODES, model_width), bf16),
            pltpu.VMEM((TREE_NODES, 2, kv_width), bf16),
            pltpu.VMEM((key_rows, kv_width), bf16),
            pltpu.VMEM((key_rows, kv_width), bf16),
            pltpu.VMEM((TREE_NODES, model_width), bf16),
            pltpu.VMEM((line_count, LANES), bf16),
            pltpu.VMEM((EXPERTS, model_width), bf16),
            pltpu.VMEM((1, model_width), bf16),
            pltpu.VMEM((2, 16, kv_width), f32),
            pltpu.VMEM((8, model_width), f32),
            pltpu.VMEM((8, model_width), bf16),
            pltpu.VMEM((EXPERTS, CAP, model_width), bf16),
            pltpu.VMEM((EXPERTS, CAP, model_width), bf16),
            pltpu.VMEM((group * share, model_width), bf16),
            pltpu.VMEM((group * share, width), f32),
            pltpu.VMEM((group * share, width), f32),
            pltpu.VMEM((halves, group * share, SLICE), bf16),
            pltpu.VMEM((2, share, model_width), bf16),
            pltpu.VMEM((2, share, model_width), bf16),
            pltpu.VMEM((2, share, model_width), bf16),
            pltpu.VMEM((share, model_width), f32),
            pltpu.VMEM((share, model_width), bf16),
            pltpu.VMEM((share, model_width), bf16),
            pltpu.VMEM((EXPERTS, CAP, model_width), bf16),
            pltpu.VMEM((EXPERTS, CAP, model_width), bf16),
            pltpu.VMEM((EXPERTS, 1, LANES), f32),
            pltpu.VMEM((EXPERTS, 1, LANES), f32),
            pltpu.VMEM((units, n, EXPERTS, UNIT), bf16),
            pltpu.VMEM((model_width // UNIT, EXPERTS, UNIT), bf16),
            pltpu.VMEM((n, depth), f32),
            pltpu.VMEM((1, model_width), f32),
            pltpu.VMEM((1, model_width), f32),
            pltpu.VMEM((n, 1, depth), f32),
            pltpu.VMEM((n, depth), f32),
            pltpu.VMEM((n, model_width), f32),
            pltpu.VMEM((n * line_count, LANES), f32),
            pltpu.VMEM((parts, n, line_count // parts, LANES), bf16),
            pltpu.VMEM((parts, n, line_count // parts, LANES), bf16),
            dma((10,)),
            dma((12,)),
            dma,
            dma((chunks,)),
            dma,
            dma((chunks, 2)),
            dma,
            dma((pieces,)),
            dma,
            dma((pieces,)),
            dma,
            dma,
            dma,
            dma,
            dma,
            dma((2,)),
            dma,
            dma,
            dma,
            dma,
        ],
        compiler_params=pltpu.CompilerParams(
            collective_id=0, has_side_effects=True, vmem_limit_bytes=62_000_000
        ),
        name="fused",
    )(
        lengths,
        parents,
        routes.T,
        accepted,
        queries,
        tree_key_value,
        key_value_cache,
        residual,
        ffn_gain.reshape(line_count, LANES),
        router.T,
        next_embed,
        gate_weight,
        up_weight,
        down_weight,
        draft_fc,
    )
    return pl.pallas_call(
        finish_kernel,
        out_shape=(
            jax.ShapeDtypeStruct((TREE_NODES, model_width), bf16),
            jax.ShapeDtypeStruct((1, model_width), bf16),
        ),
        in_specs=[whole, whole],
        out_specs=(whole, whole),
        name="finish",
    )(layer, draft_lines)


def fits(lengths, gate_weight, draft_fc, n):
    model_width, width = gate_weight.shape
    depth = draft_fc.shape[0]
    return (
        lengths.shape[0] == 1
        and n == 4 * EXPERTS
        and width == 2 * SLICE
        and model_width == 6 * SLICE
        and depth % UNIT == 0
        and depth > UNIT
        and depth <= SLICE
        and n * depth == 2 * model_width
    )


def per_device(
    queries,
    tree_key_value,
    key_value_cache,
    lengths,
    parents,
    residual,
    ffn_gain,
    router,
    routes,
    gate_weight,
    up_weight,
    down_weight,
    accepted,
    next_embed,
    draft_fc,
):
    devices = lax.axis_size("expert")
    if fits(lengths, gate_weight, draft_fc, devices):
        return fused(
            queries,
            tree_key_value,
            key_value_cache,
            lengths,
            parents,
            residual,
            ffn_gain,
            router,
            routes,
            gate_weight,
            up_weight,
            down_weight,
            accepted,
            next_embed,
            draft_fc,
            devices,
        )
    context = attention(queries, tree_key_value, key_value_cache, lengths, parents)
    hidden_state = residual.astype(jnp.float32) + context
    normed = (
        hidden_state
        * lax.rsqrt(jnp.mean(hidden_state * hidden_state, axis=-1, keepdims=True) + EPSILON)
        * ffn_gain.astype(jnp.float32)
    ).astype(jnp.bfloat16)
    tokens_here, model_width = normed.shape
    logits = jnp.dot(normed, router, preferred_element_type=jnp.float32)
    expert_ids = jnp.arange(EXPERTS, dtype=jnp.int32)
    first_hit = (routes[:, 0:1] == expert_ids[None, :]).astype(jnp.float32)
    second_hit = (routes[:, 1:2] == expert_ids[None, :]).astype(jnp.float32)
    first_logit = jnp.sum(logits * first_hit, axis=-1)
    second_logit = jnp.sum(logits * second_hit, axis=-1)
    first_share = jax.nn.sigmoid(first_logit - second_logit)
    mixing = first_share[:, None] * first_hit + (1.0 - first_share)[:, None] * second_hit
    hit_table = first_hit + second_hit
    slot_rank = jnp.cumsum(hit_table, axis=0) - 1.0
    slot_ids = jnp.arange(CAP, dtype=jnp.float32)
    placing = hit_table.T[:, None, :] * (slot_rank.T[:, None, :] == slot_ids[None, :, None]).astype(
        jnp.float32
    )
    packed = jnp.einsum(
        "ect,td->ecd", placing.astype(jnp.bfloat16), normed, preferred_element_type=jnp.float32
    ).astype(jnp.bfloat16)
    grouped = moe(packed, gate_weight, up_weight, down_weight, devices)
    weighted = placing * mixing.T[:, None, :]
    expert_sum = jnp.einsum("ect,ecd->td", weighted, grouped, precision=lax.Precision.HIGHEST)
    layer_out = (hidden_state + expert_sum).astype(jnp.bfloat16)
    request_total = lengths.shape[0]
    picker = (accepted[:, None] == jnp.arange(TREE_NODES, dtype=jnp.int32)[None, :]).astype(
        jnp.bfloat16
    )
    picked = jnp.einsum(
        "rt,rtd->rd",
        picker,
        layer_out.reshape(request_total, TREE_NODES, model_width),
        preferred_element_type=jnp.float32,
    ).astype(jnp.bfloat16)
    draft_in = jnp.concatenate([picked, next_embed], axis=1)
    depth = draft_fc.shape[0]
    blocks = draft_in.reshape(request_total, devices, depth).transpose(1, 0, 2)
    draft_out = draft(blocks.astype(jnp.float32), draft_fc).astype(jnp.bfloat16)
    return (layer_out, draft_out)


def solution(mesh):
    return jax.shard_map(
        per_device,
        mesh=mesh,
        in_specs=(
            P(("groups", "expert"), None),
            P(("groups", "expert"), None, None),
            P(("groups", "expert"), None, None, None),
            P(("groups", "expert")),
            P(("groups", "expert")),
            P(("groups", "expert"), None),
            P(),
            P(),
            P(("groups", "expert"), None),
            P(None, "expert"),
            P(None, "expert"),
            P("expert", None),
            P(("groups", "expert")),
            P(("groups", "expert"), None),
            P("expert", None),
        ),
        out_specs=(P(("groups", "expert"), None), P(("groups", "expert"), None)),
        check_vma=False,
    )
```

```python
import functools

import jax
import jax.numpy as jnp
from jax import lax
from jax.experimental import pallas as pl
from jax.experimental.pallas import tpu as pltpu
from jax.sharding import PartitionSpec as P

QUERY_HEADS = 48
KEY_VALUE_HEADS = 8
HEAD_SIZE = 128
EXPERTS = 4
TREE_NODES = 6
CACHE_SLOTS = 512
CAP = 4


EPSILON = 1e-05


def related_kernel(parents, out):
    node_ids = lax.broadcasted_iota(jnp.int32, (1, out.shape[2]), 1)
    for request in range(out.shape[0]):
        reached = []
        for node in range(TREE_NODES):
            row = (node_ids == node).astype(jnp.float32)
            parent = parents[request * TREE_NODES + node]
            for earlier in range(node):
                row = row + jnp.where(parent == earlier, reached[earlier], 0.0)
            reached.append(row)
            out[request, node : node + 1, :] = row


def ancestors(parent_ids):
    table = pl.pallas_call(
        related_kernel,
        out_shape=jax.ShapeDtypeStruct((parent_ids.shape[0] // TREE_NODES, TREE_NODES, 128), jnp.float32),
        in_specs=[pl.BlockSpec(memory_space=pltpu.SMEM)],
        out_specs=pl.BlockSpec(memory_space=pltpu.VMEM),
        name="related",
    )(parent_ids)
    return table[:, :, :TREE_NODES] > 0.5


def attention(queries, tree_key_value, key_value_cache, lengths, parents):
    request_total = lengths.shape[0]
    query_head_count = queries.reshape(
        request_total, TREE_NODES, KEY_VALUE_HEADS, QUERY_HEADS // KEY_VALUE_HEADS, HEAD_SIZE
    )
    cached_key_rows = key_value_cache[:, 0].reshape(
        request_total, CACHE_SLOTS, KEY_VALUE_HEADS, HEAD_SIZE
    )
    cached_value_rows = key_value_cache[:, 1].reshape(
        request_total, CACHE_SLOTS, KEY_VALUE_HEADS, HEAD_SIZE
    )
    tree_key_rows = tree_key_value[:, 0].reshape(
        request_total, TREE_NODES, KEY_VALUE_HEADS, HEAD_SIZE
    )
    tree_value_rows = tree_key_value[:, 1].reshape(
        request_total, TREE_NODES, KEY_VALUE_HEADS, HEAD_SIZE
    )
    score_scale = HEAD_SIZE ** (-0.5)
    cache_scores = (
        jnp.einsum(
            "rtgqd,rlgd->rgtql",
            query_head_count,
            cached_key_rows,
            preferred_element_type=jnp.float32,
        )
        * score_scale
    )
    tree_scores = (
        jnp.einsum(
            "rtgqd,rugd->rgtqu", query_head_count, tree_key_rows, preferred_element_type=jnp.float32
        )
        * score_scale
    )
    visible = jnp.arange(CACHE_SLOTS, dtype=jnp.int32)[None, :] < lengths[:, None]
    related = ancestors(parents)
    cache_scores = jnp.where(visible[:, None, None, None, :], cache_scores, -1e30)
    tree_scores = jnp.where(related[:, None, :, None, :], tree_scores, -1e30)
    row_peak = jnp.maximum(jnp.max(cache_scores, axis=-1), jnp.max(tree_scores, axis=-1))[..., None]
    cache_exp = jnp.exp(cache_scores - row_peak)
    tree_exp = jnp.exp(tree_scores - row_peak)
    denominator = (jnp.sum(cache_exp, axis=-1) + jnp.sum(tree_exp, axis=-1))[..., None]
    cache_weights = (cache_exp / denominator).astype(jnp.bfloat16)
    tree_weights = (tree_exp / denominator).astype(jnp.bfloat16)
    context = jnp.einsum(
        "rgtql,rlgd->rtgqd", cache_weights, cached_value_rows, preferred_element_type=jnp.float32
    ) + jnp.einsum(
        "rgtqu,rugd->rtgqd", tree_weights, tree_value_rows, preferred_element_type=jnp.float32
    )
    return context.reshape(request_total * TREE_NODES, QUERY_HEADS * HEAD_SIZE)


VMEM_LIMIT = 66_000_000


def greet(n, me):
    barrier = pltpu.get_barrier_semaphore()

    def hello(k, carry):
        pl.semaphore_signal(barrier, inc=1, device_id={"expert": lax.rem(me + k, n)})
        return carry

    lax.fori_loop(1, n, hello, 0)
    pl.semaphore_wait(barrier, n - 1)


def push(src, dst, send_sem, recv_sem, peer):
    return pltpu.make_async_remote_copy(
        src_ref=src,
        dst_ref=dst,
        send_sem=send_sem,
        recv_sem=recv_sem,
        device_id={"expert": peer},
        device_id_type=pl.DeviceIdType.MESH,
    )


def moe_kernel(
    n,
    group_size,
    pair_slots,
    down_slots,
    packed,
    gate_hbm,
    up_hbm,
    down_hbm,
    grouped,
    gate_buf,
    up_buf,
    down_buf,
    arrived,
    rows_wide,
    rows,
    activation,
    result,
    leaving,
    returned,
    pair_sem,
    down_sem,
    out_sem,
    in_sem,
    back_out_sem,
    back_in_sem,
    own_sem,
):
    me = lax.axis_index("expert")
    width = gate_hbm.shape[1]
    chunk = gate_buf.shape[2]
    pair_count = width // chunk
    piece = down_buf.shape[2]
    piece_count = down_hbm.shape[1] // piece

    def pair_copies(i):
        slot = lax.rem(i, pair_slots)
        cols = pl.ds(pl.multiple_of(i * chunk, chunk), chunk)
        return (
            pltpu.make_async_copy(gate_hbm.at[:, cols], gate_buf.at[slot], pair_sem.at[0, slot]),
            pltpu.make_async_copy(up_hbm.at[:, cols], up_buf.at[slot], pair_sem.at[1, slot]),
        )

    def down_copy(i):
        slot = lax.rem(i, down_slots)
        cols = pl.ds(pl.multiple_of(i * piece, piece), piece)
        return pltpu.make_async_copy(down_hbm.at[:, cols], down_buf.at[slot], down_sem.at[slot])

    def start_pair(i, carry):
        for copy in pair_copies(i):
            copy.start()
        return carry

    def start_down(i, carry):
        down_copy(i).start()
        return carry

    lax.fori_loop(0, pair_slots, start_pair, 0)
    greet(n, me)

    def dispatch(k, carry):
        peer = lax.rem(me + k, n)
        push(
            packed.at[peer // group_size], arrived.at[me], out_sem.at[peer], in_sem.at[me], peer
        ).start()
        return carry

    lax.fori_loop(1, n, dispatch, 0)
    own = pltpu.make_async_copy(packed.at[me // group_size], arrived.at[me], own_sem)
    own.start()
    lax.fori_loop(0, down_slots, start_down, 0)
    own.wait()

    def take(k, carry):
        source = lax.rem(me + n - k, n)
        push(
            packed.at[0], arrived.at[source], out_sem.at[source], in_sem.at[source], source
        ).wait_recv()
        return carry

    lax.fori_loop(1, n, take, 0)

    def both(pair):
        return pl.ds(pl.multiple_of(pair * 2 * CAP, 2 * CAP), 2 * CAP)

    def widen(pair, carry):
        rows_wide[both(pair), :] = jnp.concatenate(
            [arrived[2 * pair].astype(jnp.float32), arrived[2 * pair + 1].astype(jnp.float32)],
            axis=0,
        )
        return carry

    lax.fori_loop(0, n // 2, widen, 0)
    rows[...] = rows_wide[...].astype(jnp.bfloat16)

    def pair_step(i, carry):
        slot = lax.rem(i, pair_slots)
        for copy in pair_copies(i):
            copy.wait()
        gate_val = jnp.dot(rows[...], gate_buf[slot], preferred_element_type=jnp.float32)
        up_val = jnp.dot(rows[...], up_buf[slot], preferred_element_type=jnp.float32)
        cols = pl.ds(pl.multiple_of(i * chunk, chunk), chunk)
        activation[:, cols] = (jax.nn.silu(gate_val) * up_val).astype(jnp.bfloat16)

        @pl.when(i + pair_slots < pair_count)
        def _():
            start_pair(i + pair_slots, 0)

        return carry

    lax.fori_loop(0, pair_count, pair_step, 0)

    def down_step(i, carry):
        slot = lax.rem(i, down_slots)
        down_copy(i).wait()
        result[...] = jnp.dot(
            activation[...], down_buf[slot], preferred_element_type=jnp.float32
        )

        @pl.when(i + down_slots < piece_count)
        def _():
            start_down(i + down_slots, 0)

        def narrow(pair, inner):
            block = result[both(pair), :]
            leaving[2 * pair, i] = block[:CAP].astype(jnp.bfloat16)
            leaving[2 * pair + 1, i] = block[CAP:].astype(jnp.bfloat16)
            return inner

        lax.fori_loop(0, n // 2, narrow, 0)

        def send_back(k, inner):
            peer = lax.rem(me + k, n)
            push(
                leaving.at[peer, i],
                returned.at[me, i],
                back_out_sem.at[peer],
                back_in_sem.at[me],
                peer,
            ).start()
            return inner

        lax.fori_loop(1, n, send_back, 0)
        return carry

    lax.fori_loop(0, piece_count, down_step, 0)
    returned[me] = leaving[me]

    def drain(k, carry):
        peer = lax.rem(me + n - k, n)
        push(
            leaving.at[peer], returned.at[peer], back_out_sem.at[peer], back_in_sem.at[peer], peer
        ).wait()
        push(
            packed.at[0], arrived.at[peer], out_sem.at[peer], in_sem.at[peer], peer
        ).wait_send()
        return carry

    lax.fori_loop(1, n, drain, 0)

    def gather(expert, carry):
        for i in range(piece_count):

            def add(member, total):
                return total + returned[expert * group_size + member, i].astype(jnp.float32)

            grouped[expert, :, i * piece : (i + 1) * piece] = lax.fori_loop(
                0, group_size, add, jnp.zeros((CAP, piece), jnp.float32)
            )
        return carry

    lax.fori_loop(0, EXPERTS, gather, 0)


def moe(packed, gate_weight, up_weight, down_weight, n):
    model_width, width = gate_weight.shape
    row_count = n * CAP
    chunk = min(512, width)
    piece = model_width // 4
    pair_slots = min(3, width // chunk)
    down_slots = min(2, model_width // piece)
    anywhere = pl.BlockSpec(memory_space=pl.ANY)
    whole = pl.BlockSpec(memory_space=pltpu.VMEM)
    bf16, f32 = jnp.bfloat16, jnp.float32
    return pl.pallas_call(
        functools.partial(moe_kernel, n, n // EXPERTS, pair_slots, down_slots),
        out_shape=jax.ShapeDtypeStruct((EXPERTS, CAP, model_width), f32),
        in_specs=[whole, anywhere, anywhere, anywhere],
        out_specs=whole,
        scratch_shapes=[
            pltpu.VMEM((pair_slots, model_width, chunk), bf16),
            pltpu.VMEM((pair_slots, model_width, chunk), bf16),
            pltpu.VMEM((down_slots, width, piece), bf16),
            pltpu.VMEM((n, CAP, model_width), bf16),
            pltpu.VMEM((row_count, model_width), f32),
            pltpu.VMEM((row_count, model_width), bf16),
            pltpu.VMEM((row_count, width), bf16),
            pltpu.VMEM((row_count, piece), f32),
            pltpu.VMEM((n, model_width // piece, CAP, piece), bf16),
            pltpu.VMEM((n, model_width // piece, CAP, piece), bf16),
            pltpu.SemaphoreType.DMA((2, pair_slots)),
            pltpu.SemaphoreType.DMA((down_slots,)),
            pltpu.SemaphoreType.DMA((n,)),
            pltpu.SemaphoreType.DMA((n,)),
            pltpu.SemaphoreType.DMA((n,)),
            pltpu.SemaphoreType.DMA((n,)),
            pltpu.SemaphoreType.DMA,
        ],
        compiler_params=pltpu.CompilerParams(
            collective_id=0, has_side_effects=True, vmem_limit_bytes=VMEM_LIMIT
        ),
        name="moe",
    )(packed, gate_weight, up_weight, down_weight)


def draft_kernel(
    n,
    share,
    piece,
    blocks,
    fc_hbm,
    out,
    fc_buf,
    arrived,
    rows_wide,
    result,
    leaving,
    returned,
    fc_sem,
    out_sem,
    in_sem,
    back_out_sem,
    back_in_sem,
):
    me = lax.axis_index("expert")
    piece_count = fc_hbm.shape[1] // piece
    half = piece // 2

    def fc_copy(i):
        cols = pl.ds(pl.multiple_of(i * piece, piece), piece)
        return pltpu.make_async_copy(fc_hbm.at[:, cols], fc_buf.at[i], fc_sem.at[i])

    def start_fc(i, carry):
        fc_copy(i).start()
        return carry

    lax.fori_loop(0, piece_count, start_fc, 0)
    greet(n, me)

    def dispatch(k, carry):
        peer = lax.rem(me + k, n)
        push(blocks.at[peer], arrived.at[me], out_sem.at[peer], in_sem.at[me], peer).start()
        return carry

    lax.fori_loop(1, n, dispatch, 0)
    rows_wide[pl.ds(me * share, share), :] = blocks[me]

    def take(k, carry):
        source = lax.rem(me + n - k, n)
        push(
            blocks.at[source], arrived.at[source], out_sem.at[source], in_sem.at[source], source
        ).wait()
        rows_wide[pl.ds(source * share, share), :] = arrived[source]
        return carry

    lax.fori_loop(1, n, take, 0)

    def step(i, carry):
        fc_copy(i).wait()
        result[...] = jnp.dot(
            rows_wide[...].astype(jnp.bfloat16), fc_buf[i], preferred_element_type=jnp.float32
        )

        def split(source, inner):
            block = result[pl.ds(source * share, share), :]
            leaving[source, i] = jnp.concatenate(
                [block[:, :half], block[:, half:]], axis=0
            ).astype(jnp.bfloat16)
            return inner

        lax.fori_loop(0, n, split, 0)

        def send_back(k, inner):
            peer = lax.rem(me + k, n)
            push(
                leaving.at[peer, i],
                returned.at[me, i],
                back_out_sem.at[peer],
                back_in_sem.at[me],
                peer,
            ).start()
            return inner

        lax.fori_loop(1, n, send_back, 0)
        return carry

    lax.fori_loop(0, piece_count, step, 0)
    returned[me] = leaving[me]

    def drain(k, carry):
        peer = lax.rem(me + n - k, n)
        push(
            leaving.at[peer], returned.at[peer], back_out_sem.at[peer], back_in_sem.at[peer], peer
        ).wait()
        return carry

    lax.fori_loop(1, n, drain, 0)
    for i in range(piece_count):

        def add(source, total):
            return total + returned[source, i].astype(jnp.float32)

        total = lax.fori_loop(0, n, add, jnp.zeros((2 * share, half), jnp.float32))
        out[:, i * piece : i * piece + half] = total[:share]
        out[:, i * piece + half : (i + 1) * piece] = total[share:]


def draft(blocks, draft_fc):
    n, share, depth = blocks.shape
    model_width = draft_fc.shape[1]
    piece = model_width // 4
    pieces = model_width // piece
    whole = pl.BlockSpec(memory_space=pltpu.VMEM)
    f32 = jnp.float32
    return pl.pallas_call(
        functools.partial(draft_kernel, n, share, piece),
        out_shape=jax.ShapeDtypeStruct((share, model_width), f32),
        in_specs=[whole, pl.BlockSpec(memory_space=pl.ANY)],
        out_specs=whole,
        scratch_shapes=[
            pltpu.VMEM((pieces, depth, piece), jnp.bfloat16),
            pltpu.VMEM((n, share, depth), f32),
            pltpu.VMEM((n * share, depth), f32),
            pltpu.VMEM((n * share, piece), f32),
            pltpu.VMEM((n, pieces, 2 * share, piece // 2), jnp.bfloat16),
            pltpu.VMEM((n, pieces, 2 * share, piece // 2), jnp.bfloat16),
            pltpu.SemaphoreType.DMA((pieces,)),
            pltpu.SemaphoreType.DMA((n,)),
            pltpu.SemaphoreType.DMA((n,)),
            pltpu.SemaphoreType.DMA((n,)),
            pltpu.SemaphoreType.DMA((n,)),
        ],
        compiler_params=pltpu.CompilerParams(
            collective_id=1, has_side_effects=True, vmem_limit_bytes=VMEM_LIMIT
        ),
        name="draft",
    )(blocks, draft_fc)


SLICE = 1024
LANES = 128
UNIT = 256


def greet_near(group, mine, lane):
    barrier = pltpu.get_barrier_semaphore()
    for step in range(1, EXPERTS):
        peer = lax.rem(mine + step, EXPERTS) * group + lane
        pl.semaphore_signal(barrier, inc=1, device_id={"expert": peer})
    for step in range(1, group):
        peer = mine * group + lax.rem(lane + step, group)
        pl.semaphore_signal(barrier, inc=1, device_id={"expert": peer})
    return barrier


def fused_kernel(
    n,
    slots,
    lengths_hbm,
    parents_hbm,
    routes_hbm,
    accepted_hbm,
    queries_hbm,
    tree_hbm,
    cache_hbm,
    residual_hbm,
    gain_hbm,
    router_hbm,
    embed_hbm,
    gate_hbm,
    up_hbm,
    down_hbm,
    fc_hbm,
    layer_out,
    draft_out,
    lengths,
    parents,
    routes,
    accepted,
    weights,
    queries,
    tree,
    keys,
    values,
    residual,
    gain,
    router,
    embed,
    tree_rows,
    hidden,
    normed,
    packed,
    arrived,
    rows,
    gate_sum,
    up_sum,
    activation,
    kept,
    leaving,
    returned,
    chip_sum,
    chip_leaving,
    chip_returned,
    direct_leaving,
    direct_returned,
    home_leaving,
    home_returned,
    pick_rows,
    pick_arrived,
    shares,
    share_leaving,
    share_rows,
    hidden_row,
    embed_row,
    blocks,
    block_rows,
    draft_sum,
    draft_wide,
    draft_leaving,
    draft_returned,
    load_sem,
    input_sem,
    out_sem,
    in_sem,
    plane_out_sem,
    plane_in_sem,
    core_out_sem,
    core_in_sem,
    chip_out_sem,
    chip_in_sem,
    direct_out_sem,
    direct_in_sem,
    home_out_sem,
    home_in_sem,
    pick_out_sem,
    pick_in_sem,
    share_out_sem,
    share_in_sem,
    block_out_sem,
    block_in_sem,
    draft_out_sem,
    draft_in_sem,
):
    bf16, f32 = jnp.bfloat16, jnp.float32
    me = lax.axis_index("expert")
    group = n // EXPERTS
    mine = me // group
    lane = lax.rem(me, group)
    core = lax.rem(lane, 2)
    across = lane // 2
    core_peer = mine * group + across * 2 + (1 - core)
    chip_peer = mine * group + (1 - across) * 2 + core
    model_width = down_hbm.shape[1]
    width = down_hbm.shape[0]
    depth = fc_hbm.shape[0]
    slice_count = model_width // SLICE
    half_count = width // SLICE
    half = SLICE // 2
    chunks = [(0, half), (half, half)] + [(k * SLICE, SLICE) for k in range(1, slice_count)]
    last = model_width - SLICE
    pieces = [(k * SLICE, SLICE) for k in range(slice_count - 1)]
    pieces += [(last, SLICE - UNIT), (model_width - UNIT, UNIT)]
    piece_count = len(pieces)
    unit_count = depth // UNIT
    block_count = model_width // depth
    padded = 8
    share = EXPERTS * CAP
    cache_slots = cache_hbm.shape[2]
    key_rows = keys.shape[0]
    line_count = model_width // LANES
    lines = SLICE // LANES
    part_count = draft_leaving.shape[0]

    pairs = [
        ("pair", k, h, i) for k in range(slice_count) for h in range(half_count) for i in range(2)
    ]
    downs = [("down", p, a) for p in range(piece_count) for a in range(half_count)]
    order = pairs + downs + [("fc", p) for p in range(slice_count)]
    place = {item: i for i, item in enumerate(order)}
    sem_count = load_sem.shape[0]

    def load_group(item):
        if item[0] == "pair":
            return item[1]
        if item[0] == "down":
            return slice_count + item[1]
        return slice_count + piece_count

    def wait_loads(item):
        if item[0] == "pair":
            view = weights.at[0 : 2 * half_count]
        elif item[0] == "down":
            view = weights.at[0:half_count, :, 0 : pieces[item[1]][1]]
        else:
            view = weights.at[0:slice_count, 0:depth, :]
        pltpu.make_async_copy(view, view, load_sem.at[load_group(item) % sem_count]).wait()

    def load_copy(item):
        i = place[item]
        slot = weights.at[i % slots]
        if item[0] == "pair":
            k, h = item[1], item[2]
            source = (gate_hbm, up_hbm)[item[3]]
            view = source.at[k * SLICE : (k + 1) * SLICE, h * SLICE : (h + 1) * SLICE]
        elif item[0] == "down":
            a = item[2]
            start, size = pieces[item[1]]
            view = down_hbm.at[a * SLICE : (a + 1) * SLICE, start : start + size]
            slot = weights.at[i % slots, :, 0:size]
        else:
            p = item[1]
            view = fc_hbm.at[:, p * SLICE : (p + 1) * SLICE]
            slot = weights.at[i % slots, 0:depth, :]
        return pltpu.make_async_copy(view, slot, load_sem.at[load_group(item) % sem_count])

    def start_load(i):
        if i < len(order):
            load_copy(order[i]).start()

    inputs = [
        pltpu.make_async_copy(source, target, input_sem.at[i])
        for i, (source, target) in enumerate(
            [
                (queries_hbm, queries),
                (tree_hbm, tree),
                (cache_hbm.at[0, 0], keys.at[0:cache_slots, :]),
                (residual_hbm, residual),
                (cache_hbm.at[0, 1], values.at[0:cache_slots, :]),
                (gain_hbm, gain),
                (router_hbm, router),
                (embed_hbm, embed),
                (lengths_hbm, lengths),
                (parents_hbm, parents),
                (routes_hbm, routes),
                (accepted_hbm, accepted),
            ]
        )
    ]
    for copy in inputs[8:] + inputs[:8]:
        copy.start()
    barrier = greet_near(group, mine, lane)
    for copy in inputs[8:]:
        copy.wait()

    row8 = lax.broadcasted_iota(jnp.int32, (padded, LANES), 0)
    col8 = lax.broadcasted_iota(jnp.int32, (padded, LANES), 1)
    node_ids = lax.broadcasted_iota(jnp.int32, (1, LANES), 1)
    reached = []
    related = jnp.zeros((padded, LANES), f32)
    for node in range(TREE_NODES):
        row = (node_ids == node).astype(f32)
        parent = parents[node]
        for earlier in range(node):
            row = row + jnp.where(parent == earlier, reached[earlier], 0.0)
        reached.append(row)
        related = related + jnp.where(row8 == node, row, 0.0)
    slot_ids = lax.broadcasted_iota(jnp.int32, (padded, cache_slots), 1)
    bias = jnp.concatenate(
        [
            jnp.where(slot_ids < lengths[0], 0.0, -1e30),
            jnp.where(related > 0.5, 0.0, -1e30),
        ],
        axis=1,
    )
    heads_each = QUERY_HEADS // KEY_VALUE_HEADS
    bias = jnp.concatenate([bias] * heads_each, axis=0)

    def named(choice, token):
        expert = routes[choice, token]
        rank = jnp.int32(0)
        for earlier in range(token):
            for other in range(2):
                rank = rank + jnp.where(routes[other, earlier] == expert, 1, 0)
        return expert, rank

    places = [[named(choice, token) for choice in range(2)] for token in range(TREE_NODES)]

    for copy in inputs[:3]:
        copy.wait()
    for i in range(slots):
        start_load(i)
    tree_rows[...] = jnp.zeros_like(tree_rows)
    for token in range(TREE_NODES):
        both = tree[token].astype(f32)
        tree_rows[0, token : token + 1, :] = both[0:1]
        tree_rows[1, token : token + 1, :] = both[1:2]
    tile = tree_rows.shape[1]
    blank = jnp.zeros((key_rows - cache_slots - tile, keys.shape[1]), bf16)
    keys[cache_slots : cache_slots + tile, :] = tree_rows[0].astype(bf16)
    keys[cache_slots + tile :, :] = blank
    values[cache_slots : cache_slots + tile, :] = tree_rows[1].astype(bf16)
    values[cache_slots + tile :, :] = blank
    spare = jnp.zeros((padded - TREE_NODES, HEAD_SIZE), f32)
    score_scale = HEAD_SIZE ** (-0.5)
    weights_of = []
    for g in range(KEY_VALUE_HEADS):
        parts = []
        for q in range(heads_each):
            head = g * heads_each + q
            parts.append(queries[:, head * HEAD_SIZE : (head + 1) * HEAD_SIZE].astype(f32))
            parts.append(spare)
        head_queries = jnp.concatenate(parts, axis=0).astype(bf16)
        scores = (
            lax.dot_general(
                head_queries,
                keys[:, g * HEAD_SIZE : (g + 1) * HEAD_SIZE],
                (((1,), (1,)), ((), ())),
                preferred_element_type=f32,
            )
            * score_scale
            + bias
        )
        peak = jnp.max(scores, axis=-1, keepdims=True)
        grown = jnp.exp(scores - peak)
        total = jnp.sum(grown, axis=-1, keepdims=True)
        weights_of.append((grown * (1.0 / total)).astype(bf16))
    for copy in inputs[3:5]:
        copy.wait()
    square = jnp.zeros((padded, HEAD_SIZE), f32)
    for g in range(KEY_VALUE_HEADS):
        context = jnp.dot(
            weights_of[g],
            values[:, g * HEAD_SIZE : (g + 1) * HEAD_SIZE],
            preferred_element_type=f32,
        )
        for q in range(heads_each):
            head = g * heads_each + q
            cols = slice(head * HEAD_SIZE, (head + 1) * HEAD_SIZE)
            state = context[q * padded : (q + 1) * padded] + jnp.concatenate(
                [residual[:, cols].astype(f32), spare], axis=0
            )
            hidden[:, cols] = state
            square = square + state * state
    for copy in inputs[5:8]:
        copy.wait()
    level = lax.rsqrt(jnp.sum(square, axis=-1, keepdims=True) / model_width + EPSILON)

    slot_row = lax.broadcasted_iota(jnp.int32, (EXPERTS * padded, padded), 0)
    slot_col = lax.broadcasted_iota(jnp.int32, (EXPERTS * padded, padded), 1)
    placing = jnp.zeros((EXPERTS * padded, padded), f32)
    for token, choices in enumerate(places):
        for expert, rank in choices:
            placing = placing + jnp.where(
                (slot_row == expert * padded + rank) & (slot_col == token), 1.0, 0.0
            )
    placing = placing.astype(bf16)

    def to_plane(c, step):
        plane = lax.rem(mine + step, EXPERTS)
        cols = pl.ds(chunks[c][0], chunks[c][1])
        return push(
            packed.at[plane, :, cols],
            arrived.at[mine, :, cols],
            out_sem,
            in_sem.at[c],
            plane * group + lane,
        )

    def awaited(ref, sem):
        return push(ref, ref, sem, sem, core_peer)

    def pack_step(c):
        start, size = chunks[c]
        cols = slice(start, start + size)
        gains = [
            gain[t : t + 1, :].astype(f32)
            for t in range(start // LANES, (start + size) // LANES)
        ]
        normal = (hidden[:, cols] * level * jnp.concatenate(gains, axis=1)).astype(bf16)
        normed[:, cols] = normal
        spread = jnp.dot(placing, normal, preferred_element_type=f32)
        for e in range(EXPERTS):
            packed[e, :, cols] = spread[e * padded : e * padded + CAP].astype(bf16)
        arrived[mine, :, cols] = packed[mine, :, cols]

    pack_step(0)
    pl.semaphore_wait(barrier, EXPERTS + group - 2)
    for c in range(len(chunks)):
        if c > 0:
            pack_step(c)
        for step in range(1, EXPERTS):
            to_plane(c, step).start()

    token_row = row8[:, 0:1]
    embed_row[...] = embed[...].astype(f32)
    for k in range(slice_count):
        cols = slice(k * SLICE, (k + 1) * SLICE)
        hidden_row[:, cols] = jnp.sum(
            jnp.where(token_row == accepted[0], hidden[:, cols], 0.0), axis=0, keepdims=True
        )

    def block_push(row, b, j):
        source = row.at[:, b * depth : (b + 1) * depth]
        return push(source, blocks.at[me], block_out_sem, block_in_sem, j)

    def send_block(row, b, j):
        @pl.when(me != j)
        def _():
            block_push(row, b, j).start()

        @pl.when(me == j)
        def _():
            blocks[j] = row[:, b * depth : (b + 1) * depth]

    logits = [jnp.zeros((padded, 1), f32) for _ in range(EXPERTS)]
    for k in range(slice_count):
        cols = slice(k * SLICE, (k + 1) * SLICE)
        normal = normed[:, cols].astype(f32)
        for e in range(EXPERTS):
            logits[e] = logits[e] + jnp.sum(
                normal * router[e : e + 1, cols].astype(f32), axis=-1, keepdims=True
            )
    ids = [jnp.full((padded, 1), -1, jnp.int32) for _ in range(4)]
    for token, choices in enumerate(places):
        for choice, (expert, rank) in enumerate(choices):
            ids[choice] = jnp.where(token_row == token, expert, ids[choice])
            ids[2 + choice] = jnp.where(token_row == token, expert * CAP + rank, ids[2 + choice])
    first_logit = jnp.zeros((padded, 1), f32)
    second_logit = jnp.zeros((padded, 1), f32)
    for e in range(EXPERTS):
        first_logit = first_logit + jnp.where(ids[0] == e, logits[e], 0.0)
        second_logit = second_logit + jnp.where(ids[1] == e, logits[e], 0.0)
    first_share = jax.nn.sigmoid(first_logit - second_logit)
    share_col = col8[:, :share]
    weighted = jnp.where(share_col == ids[2], first_share, 0.0) + jnp.where(
        share_col == ids[3], 1.0 - first_share, 0.0
    )

    def split(exact):
        high = exact.astype(bf16).astype(f32)
        middle = (exact - high).astype(bf16).astype(f32)
        low = exact - high - middle
        return jnp.concatenate([high, middle, low], axis=0).astype(bf16)

    mixers = split(weighted)

    def pick_push(step):
        plane = lax.rem(mine + step, EXPERTS)
        return push(
            pick_rows.at[plane],
            pick_arrived.at[mine],
            pick_out_sem,
            pick_in_sem,
            plane * group + lane,
        )

    for e in range(EXPERTS):
        chosen = jnp.zeros((padded, LANES), f32)
        for expert, position, portion in (
            (ids[0], ids[2], first_share),
            (ids[1], ids[3], 1.0 - first_share),
        ):
            here = (col8 == mine * CAP + position - expert * CAP) & (expert == e)
            chosen = chosen + jnp.where(here, portion, 0.0)
        pick_rows[e] = jnp.sum(
            jnp.where(token_row == accepted[0], chosen, 0.0), axis=0, keepdims=True
        )
    def send_early():
        for step in range(1, EXPERTS):
            pick_push(step).start()
        for b in range(block_count):
            send_block(embed_row, b, block_count + b)
            send_block(hidden_row, b, b)

    pick_arrived[mine] = pick_rows[mine]

    def row_push(c, which, sem, peer):
        start, size = chunks[c]
        block = rows.at[pl.ds(pl.multiple_of(which * share, share), share), pl.ds(start, size)]
        return push(block, block, plane_out_sem, plane_in_sem.at[c, sem], peer)

    chip_lane = (1 - across) * 2 + core

    def gather_step(k):
        start, size = chunks[k]
        cols = slice(start, start + size)
        awaited(arrived.at[0 : EXPERTS - 1, :, pl.ds(start, size)], in_sem.at[k]).wait_recv()
        rows[pl.ds(pl.multiple_of(lane * share, share), share), cols] = jnp.concatenate(
            [arrived[s, :, cols].astype(f32) for s in range(EXPERTS)], axis=0
        ).astype(bf16)
        row_push(k, lane, 0, chip_peer).start()
        row_push(k, lane, 1, core_peer).start()

    def forward_step(k):
        row_push(k, chip_lane, 0, chip_peer).wait_recv()
        row_push(k, chip_lane, 1, core_peer).start()

    def expert_step(c):
        start, size = chunks[c]
        pair_rows = rows.at[0 : 2 * share, pl.ds(start, size)]
        awaited(pair_rows, plane_in_sem.at[c, 1]).wait_recv()
        k, first = start // SLICE, start % SLICE
        final = start + size == model_width
        if first == 0:
            wait_loads(("pair", k))
        for h in range(half_count):
            cols = slice(h * SLICE, (h + 1) * SLICE)
            sums = []
            for i, total in ((0, gate_sum), (1, up_sum)):
                item = ("pair", k, h, i)
                value = jnp.dot(
                    rows[:, start : start + size],
                    weights[place[item] % slots, first : first + size, :],
                    preferred_element_type=f32,
                )
                if start > 0:
                    value = value + total[:, cols]
                if not final:
                    total[:, cols] = value
                sums.append(value)
                if first + size == SLICE:
                    start_load(place[item] + slots)
            if final:
                activation[h] = (jax.nn.silu(sums[0]) * sums[1]).astype(bf16)

    for t in range(len(chunks) + 3):
        if t < len(chunks):
            gather_step(t)
        if t == 2:
            send_early()
        if 0 <= t - 2 < len(chunks):
            forward_step(t - 2)
        if 0 <= t - 3 < len(chunks):
            expert_step(t - 3)

    def piece_cols(p):
        return pl.ds(pieces[p][0], pieces[p][1])

    def core_push(p):
        cols = piece_cols(p)
        return push(
            leaving.at[:, :, cols],
            returned.at[:, :, cols],
            core_out_sem,
            core_in_sem.at[p],
            core_peer,
        )

    def chip_push(p):
        cols = piece_cols(p)
        return push(
            chip_leaving.at[:, cols],
            chip_returned.at[:, cols],
            chip_out_sem,
            chip_in_sem.at[p],
            chip_peer,
        )

    def to_home(p, step):
        plane = lax.rem(mine + step, EXPERTS)
        return push(
            home_leaving.at[plane, :, piece_cols(p)],
            home_returned.at[mine, :, piece_cols(p)],
            home_out_sem,
            home_in_sem,
            plane * group + lane,
        )

    def partial_step(p):
        start, size = pieces[p]
        cols = slice(start, start + size)
        partial = None
        wait_loads(("down", p))
        for a in range(half_count):
            item = ("down", p, a)
            value = jnp.dot(
                activation[a], weights[place[item] % slots, :, 0:size], preferred_element_type=f32
            )
            partial = value if partial is None else partial + value
            start_load(place[item] + slots)
        if p == piece_count - 1:
            for member in range(group):
                direct_leaving[member] = partial[member * share : (member + 1) * share].astype(
                    bf16
                )
            for step in range(1, group):
                peer = lax.rem(lane + step, group)
                push(
                    direct_leaving.at[peer],
                    direct_returned.at[lane],
                    direct_out_sem,
                    direct_in_sem,
                    mine * group + peer,
                ).start()
            direct_returned[lane] = direct_leaving[lane]
            return
        for member in range(group):
            block = partial[member * share : (member + 1) * share].astype(bf16)
            a, c = member // 2, member % 2

            @pl.when(core == c)
            def _():
                kept[a, :, cols] = block

            @pl.when(core != c)
            def _():
                leaving[a, :, cols] = block

        core_push(p).start()

    def core_step(p):
        core_push(p).wait_recv()
        start, size = pieces[p]
        cols = slice(start, start + size)
        far = 1 - across
        chip_leaving[:, cols] = (
            kept[far, :, cols].astype(f32) + returned[far, :, cols].astype(f32)
        ).astype(bf16)
        chip_push(p).start()
        chip_sum[:, cols] = kept[across, :, cols].astype(f32) + returned[across, :, cols].astype(
            f32
        )

    def share_push(unit, b):
        part = unit % unit_count
        return push(
            share_leaving.at[unit],
            shares.at[part, me],
            share_out_sem,
            share_in_sem.at[part // (unit_count - 1)],
            b,
        )

    def chip_step(p, pick_mixers):
        start, size = pieces[p]
        cols = slice(start, start + size)
        if p < piece_count - 1:
            chip_push(p).wait_recv()
            total = chip_sum[:, cols] + chip_returned[:, cols].astype(f32)
        else:
            awaited(direct_returned.at[0 : group - 1], direct_in_sem).wait_recv()
            total = direct_returned[0].astype(f32)
            for member in range(1, group):
                total = total + direct_returned[member].astype(f32)
        mixed = jnp.dot(pick_mixers, total.astype(bf16), preferred_element_type=f32)
        portion = mixed[:padded] + mixed[padded : 2 * padded] + mixed[2 * padded :]
        for unit in range(start // UNIT, (start + size) // UNIT):
            b = unit // unit_count
            first = unit * UNIT - start
            value = portion[:EXPERTS, first : first + UNIT].astype(bf16)

            @pl.when(me != b)
            def _():
                share_leaving[unit] = value
                share_push(unit, b).start()

            @pl.when(me == b)
            def _():
                shares[unit % unit_count, b] = value

        for s in range(EXPERTS):
            home_leaving[s, :, cols] = total[s * CAP : (s + 1) * CAP].astype(bf16)
        for step in range(1, EXPERTS):
            to_home(p, step).start()
        home_returned[mine, :, cols] = home_leaving[mine, :, cols]

    def home_step(p):
        start, size = pieces[p]
        cols = slice(start, start + size)
        block = jnp.concatenate(
            [home_returned[e, :, cols].astype(f32) for e in range(EXPERTS)], axis=0
        ).astype(bf16)
        mixed = jnp.dot(mixers, block, preferred_element_type=f32)
        expert_sum = mixed[:padded] + mixed[padded : 2 * padded] + mixed[2 * padded :]
        result = (hidden[:, cols] + expert_sum).astype(bf16)
        layer_out[:, cols] = result[:TREE_NODES]

    def draft_push(q, peer, at):
        return push(
            draft_leaving.at[q, peer],
            draft_returned.at[q, at],
            draft_out_sem,
            draft_in_sem,
            peer,
        )

    def row_of(device):
        return lax.rem(device, group) * EXPERTS + device // group

    def block_step():
        awaited(blocks.at[0 : n - 1], block_in_sem).wait_recv()

        def take(source, carry):
            block_rows[pl.ds(row_of(source), 1), :] = blocks[source]
            return carry

        lax.fori_loop(0, n, take, 0)
        share_rows[...] = jnp.zeros_like(share_rows)

    def share_step(first, past):
        @pl.when(me < block_count)
        def _():
            sem = share_in_sem.at[first // (unit_count - 1)]
            awaited(shares.at[first:past, 0 : n - 1], sem).wait_recv()
            for part in range(first, past):
                sums = []
                for member in range(group):
                    total = shares[part, member].astype(f32)
                    for e in range(1, EXPERTS):
                        total = total + shares[part, e * group + member].astype(f32)
                    sums.append(total)
                share_rows[:, part * UNIT : (part + 1) * UNIT] = jnp.concatenate(sums, axis=0)

    def draft_step(first, past, final):
        share_step(first, past)
        deep = slice(first * UNIT, past * UNIT)
        draft_rows = (block_rows[:, deep] + share_rows[:, deep]).astype(bf16)
        per_part = slice_count // part_count
        if first == 0:
            wait_loads(("fc",))
        for q in range(part_count):
            for p in range(q * per_part, (q + 1) * per_part):
                item = ("fc", p)
                partial = jnp.dot(
                    draft_rows, weights[place[item] % slots, deep, :], preferred_element_type=f32
                )
                cols = slice(p * SLICE, (p + 1) * SLICE)
                if first > 0:
                    partial = partial + draft_sum[:, cols]
                if not final:
                    draft_sum[:, cols] = partial
                    continue
                for t in range(lines):
                    draft_wide[pl.ds(p * lines + t, n, stride=line_count), :] = partial[
                        :, t * LANES : (t + 1) * LANES
                    ]
            if not final:
                continue
            each = line_count // part_count
            for row in range(n):
                device = row % EXPERTS * group + row // EXPERTS
                start = row * line_count + q * each
                draft_leaving[q, device] = draft_wide[start : start + each, :].astype(bf16)

            def send_partial(k, carry):
                draft_push(q, lax.rem(me + k, n), me).start()
                return carry

            lax.fori_loop(1, n, send_partial, 0)
            draft_returned[q, me] = draft_leaving[q, me]

    awaited(pick_arrived.at[0 : EXPERTS - 1], pick_in_sem).wait_recv()
    picks = jnp.concatenate(
        [pick_arrived[s][:, :share] for s in range(EXPERTS)]
        + [jnp.zeros((padded - EXPERTS, share), f32)],
        axis=0,
    )
    pick_mixers = split(picks)

    for p in range(piece_count):
        partial_step(p)
        if p > 0:
            core_step(p - 1)
        if p > 3:
            chip_step(p - 4, pick_mixers)
    block_step()
    for p in range(piece_count - 4, piece_count):
        chip_step(p, pick_mixers)
    draft_step(0, unit_count - 1, False)
    draft_step(unit_count - 1, unit_count, True)
    awaited(home_returned.at[0 : EXPERTS - 1], home_in_sem).wait_recv()
    for p in range(piece_count):
        home_step(p)

    awaited(packed.at[0 : EXPERTS - 1], out_sem).wait_send()
    awaited(rows.at[0 : 3 * share, :], plane_out_sem).wait_send()
    awaited(pick_rows.at[0 : EXPERTS - 1], pick_out_sem).wait_send()
    paired = model_width - UNIT
    awaited(leaving.at[:, :, 0:paired], core_out_sem).wait_send()
    awaited(chip_leaving.at[:, 0:paired], chip_out_sem).wait_send()
    awaited(direct_leaving.at[0 : group - 1], direct_out_sem).wait_send()
    awaited(home_leaving.at[0 : EXPERTS - 1], home_out_sem).wait_send()
    awaited(blocks.at[0 : n - 1], block_out_sem).wait_send()
    unit_total = share_leaving.shape[0]

    @pl.when(me < block_count)
    def _():
        awaited(share_leaving.at[0 : unit_total - unit_count], share_out_sem).wait_send()

    @pl.when(me >= block_count)
    def _():
        awaited(share_leaving, share_out_sem).wait_send()

    awaited(draft_leaving.at[:, 0 : n - 1], draft_out_sem).wait_send()
    awaited(draft_returned.at[:, 0 : n - 1], draft_in_sem).wait_recv()
    each = line_count // part_count
    for q in range(part_count):
        total = draft_returned[q, 0].astype(f32)
        for source in range(1, n):
            total = total + draft_returned[q, source].astype(f32)
        draft_out[q * each : (q + 1) * each, :] = total


def finish_kernel(layer, draft_lines, layer_out, draft_out):
    layer_out[...] = layer[...]
    for t in range(draft_lines.shape[0]):
        draft_out[:, t * LANES : (t + 1) * LANES] = draft_lines[t : t + 1, :].astype(jnp.bfloat16)


def fused(
    queries,
    tree_key_value,
    key_value_cache,
    lengths,
    parents,
    residual,
    ffn_gain,
    router,
    routes,
    gate_weight,
    up_weight,
    down_weight,
    accepted,
    next_embed,
    draft_fc,
    n,
):
    width, model_width = down_weight.shape
    depth = draft_fc.shape[0]
    group = n // EXPERTS
    share = EXPERTS * CAP
    slots = 24
    slices = model_width // SLICE
    halves = width // SLICE
    parts = 3
    pieces = slices + 1
    chunks = slices + 1
    units = depth // UNIT
    line_count = model_width // LANES
    kv_width = tree_key_value.shape[2]
    key_rows = key_value_cache.shape[2] + LANES
    in_hbm = pl.BlockSpec(memory_space=pltpu.HBM)
    whole = pl.BlockSpec(memory_space=pltpu.VMEM)
    bf16, f32 = jnp.bfloat16, jnp.float32
    dma = pltpu.SemaphoreType.DMA
    pinned = pltpu.with_memory_space_constraint
    layer, draft_lines = pl.pallas_call(
        functools.partial(fused_kernel, n, slots),
        out_shape=(
            pltpu.VMEM((TREE_NODES, model_width), bf16),
            pltpu.VMEM((line_count, LANES), f32),
        ),
        in_specs=[in_hbm] * 15,
        out_specs=(whole, whole),
        scratch_shapes=[
            pltpu.SMEM(lengths.shape, jnp.int32),
            pltpu.SMEM(parents.shape, jnp.int32),
            pltpu.SMEM(routes.T.shape, jnp.int32),
            pltpu.SMEM(accepted.shape, jnp.int32),
            pltpu.VMEM((slots, SLICE, SLICE), bf16),
            pltpu.VMEM((TREE_NODES, model_width), bf16),
            pltpu.VMEM((TREE_NODES, 2, kv_width), bf16),
            pltpu.VMEM((key_rows, kv_width), bf16),
            pltpu.VMEM((key_rows, kv_width), bf16),
            pltpu.VMEM((TREE_NODES, model_width), bf16),
            pltpu.VMEM((line_count, LANES), bf16),
            pltpu.VMEM((EXPERTS, model_width), bf16),
            pltpu.VMEM((1, model_width), bf16),
            pltpu.VMEM((2, 16, kv_width), f32),
            pltpu.VMEM((8, model_width), f32),
            pltpu.VMEM((8, model_width), bf16),
            pltpu.VMEM((EXPERTS, CAP, model_width), bf16),
            pltpu.VMEM((EXPERTS, CAP, model_width), bf16),
            pltpu.VMEM((group * share, model_width), bf16),
            pltpu.VMEM((group * share, width), f32),
            pltpu.VMEM((group * share, width), f32),
            pltpu.VMEM((halves, group * share, SLICE), bf16),
            pltpu.VMEM((2, share, model_width), bf16),
            pltpu.VMEM((2, share, model_width), bf16),
            pltpu.VMEM((2, share, model_width), bf16),
            pltpu.VMEM((share, model_width), f32),
            pltpu.VMEM((share, model_width), bf16),
            pltpu.VMEM((share, model_width), bf16),
            pltpu.VMEM((group, share, UNIT), bf16),
            pltpu.VMEM((group, share, UNIT), bf16),
            pltpu.VMEM((EXPERTS, CAP, model_width), bf16),
            pltpu.VMEM((EXPERTS, CAP, model_width), bf16),
            pltpu.VMEM((EXPERTS, 1, LANES), f32),
            pltpu.VMEM((EXPERTS, 1, LANES), f32),
            pltpu.VMEM((units, n, EXPERTS, UNIT), bf16),
            pltpu.VMEM((model_width // UNIT, EXPERTS, UNIT), bf16),
            pltpu.VMEM((n, depth), f32),
            pltpu.VMEM((1, model_width), f32),
            pltpu.VMEM((1, model_width), f32),
            pltpu.VMEM((n, 1, depth), f32),
            pltpu.VMEM((n, depth), f32),
            pltpu.VMEM((n, model_width), f32),
            pltpu.VMEM((n * line_count, LANES), f32),
            pltpu.VMEM((parts, n, line_count // parts, LANES), bf16),
            pltpu.VMEM((parts, n, line_count // parts, LANES), bf16),
            dma((10,)),
            dma((12,)),
            dma,
            dma((chunks,)),
            dma,
            dma((chunks, 2)),
            dma,
            dma((pieces,)),
            dma,
            dma((pieces,)),
            dma,
            dma,
            dma,
            dma,
            dma,
            dma,
            dma,
            dma((2,)),
            dma,
            dma,
            dma,
            dma,
        ],
        compiler_params=pltpu.CompilerParams(
            collective_id=0, has_side_effects=True, vmem_limit_bytes=62_000_000
        ),
        name="fused",
    )(
        lengths,
        parents,
        routes.T,
        accepted,
        queries,
        tree_key_value,
        key_value_cache,
        residual,
        ffn_gain.reshape(line_count, LANES),
        router.T,
        next_embed,
        gate_weight,
        up_weight,
        down_weight,
        draft_fc,
    )
    return pl.pallas_call(
        finish_kernel,
        out_shape=(
            jax.ShapeDtypeStruct((TREE_NODES, model_width), bf16),
            jax.ShapeDtypeStruct((1, model_width), bf16),
        ),
        in_specs=[whole, whole],
        out_specs=(whole, whole),
        name="finish",
    )(pinned(layer, pltpu.VMEM), pinned(draft_lines, pltpu.VMEM))


def fits(lengths, gate_weight, draft_fc, n):
    model_width, width = gate_weight.shape
    depth = draft_fc.shape[0]
    return (
        lengths.shape[0] == 1
        and n == 4 * EXPERTS
        and width == 2 * SLICE
        and model_width == 6 * SLICE
        and depth % UNIT == 0
        and depth > UNIT
        and depth <= SLICE
        and n * depth == 2 * model_width
    )


def per_device(
    queries,
    tree_key_value,
    key_value_cache,
    lengths,
    parents,
    residual,
    ffn_gain,
    router,
    routes,
    gate_weight,
    up_weight,
    down_weight,
    accepted,
    next_embed,
    draft_fc,
):
    devices = lax.axis_size("expert")
    if fits(lengths, gate_weight, draft_fc, devices):
        return fused(
            queries,
            tree_key_value,
            key_value_cache,
            lengths,
            parents,
            residual,
            ffn_gain,
            router,
            routes,
            gate_weight,
            up_weight,
            down_weight,
            accepted,
            next_embed,
            draft_fc,
            devices,
        )
    context = attention(queries, tree_key_value, key_value_cache, lengths, parents)
    hidden_state = residual.astype(jnp.float32) + context
    normed = (
        hidden_state
        * lax.rsqrt(jnp.mean(hidden_state * hidden_state, axis=-1, keepdims=True) + EPSILON)
        * ffn_gain.astype(jnp.float32)
    ).astype(jnp.bfloat16)
    tokens_here, model_width = normed.shape
    logits = jnp.dot(normed, router, preferred_element_type=jnp.float32)
    expert_ids = jnp.arange(EXPERTS, dtype=jnp.int32)
    first_hit = (routes[:, 0:1] == expert_ids[None, :]).astype(jnp.float32)
    second_hit = (routes[:, 1:2] == expert_ids[None, :]).astype(jnp.float32)
    first_logit = jnp.sum(logits * first_hit, axis=-1)
    second_logit = jnp.sum(logits * second_hit, axis=-1)
    first_share = jax.nn.sigmoid(first_logit - second_logit)
    mixing = first_share[:, None] * first_hit + (1.0 - first_share)[:, None] * second_hit
    hit_table = first_hit + second_hit
    slot_rank = jnp.cumsum(hit_table, axis=0) - 1.0
    slot_ids = jnp.arange(CAP, dtype=jnp.float32)
    placing = hit_table.T[:, None, :] * (slot_rank.T[:, None, :] == slot_ids[None, :, None]).astype(
        jnp.float32
    )
    packed = jnp.einsum(
        "ect,td->ecd", placing.astype(jnp.bfloat16), normed, preferred_element_type=jnp.float32
    ).astype(jnp.bfloat16)
    grouped = moe(packed, gate_weight, up_weight, down_weight, devices)
    weighted = placing * mixing.T[:, None, :]
    expert_sum = jnp.einsum("ect,ecd->td", weighted, grouped, precision=lax.Precision.HIGHEST)
    layer_out = (hidden_state + expert_sum).astype(jnp.bfloat16)
    request_total = lengths.shape[0]
    picker = (accepted[:, None] == jnp.arange(TREE_NODES, dtype=jnp.int32)[None, :]).astype(
        jnp.bfloat16
    )
    picked = jnp.einsum(
        "rt,rtd->rd",
        picker,
        layer_out.reshape(request_total, TREE_NODES, model_width),
        preferred_element_type=jnp.float32,
    ).astype(jnp.bfloat16)
    draft_in = jnp.concatenate([picked, next_embed], axis=1)
    depth = draft_fc.shape[0]
    blocks = draft_in.reshape(request_total, devices, depth).transpose(1, 0, 2)
    draft_out = draft(blocks.astype(jnp.float32), draft_fc).astype(jnp.bfloat16)
    return (layer_out, draft_out)


def solution(mesh):
    return jax.shard_map(
        per_device,
        mesh=mesh,
        in_specs=(
            P(("groups", "expert"), None),
            P(("groups", "expert"), None, None),
            P(("groups", "expert"), None, None, None),
            P(("groups", "expert")),
            P(("groups", "expert")),
            P(("groups", "expert"), None),
            P(),
            P(),
            P(("groups", "expert"), None),
            P(None, "expert"),
            P(None, "expert"),
            P("expert", None),
            P(("groups", "expert")),
            P(("groups", "expert"), None),
            P("expert", None),
        ),
        out_specs=(P(("groups", "expert"), None), P(("groups", "expert"), None)),
        check_vma=False,
    )
```

```python
import functools

import jax
import jax.numpy as jnp
from jax import lax
from jax.experimental import pallas as pl
from jax.experimental.pallas import tpu as pltpu
from jax.sharding import PartitionSpec as P

QUERY_HEADS = 48
KEY_VALUE_HEADS = 8
HEAD_SIZE = 128
EXPERTS = 4
TREE_NODES = 6
CACHE_SLOTS = 512
CAP = 4


EPSILON = 1e-05


def related_kernel(parents, out):
    node_ids = lax.broadcasted_iota(jnp.int32, (1, out.shape[2]), 1)
    for request in range(out.shape[0]):
        reached = []
        for node in range(TREE_NODES):
            row = (node_ids == node).astype(jnp.float32)
            parent = parents[request * TREE_NODES + node]
            for earlier in range(node):
                row = row + jnp.where(parent == earlier, reached[earlier], 0.0)
            reached.append(row)
            out[request, node : node + 1, :] = row


def ancestors(parent_ids):
    table = pl.pallas_call(
        related_kernel,
        out_shape=jax.ShapeDtypeStruct((parent_ids.shape[0] // TREE_NODES, TREE_NODES, 128), jnp.float32),
        in_specs=[pl.BlockSpec(memory_space=pltpu.SMEM)],
        out_specs=pl.BlockSpec(memory_space=pltpu.VMEM),
        name="related",
    )(parent_ids)
    return table[:, :, :TREE_NODES] > 0.5


def attention(queries, tree_key_value, key_value_cache, lengths, parents):
    request_total = lengths.shape[0]
    query_head_count = queries.reshape(
        request_total, TREE_NODES, KEY_VALUE_HEADS, QUERY_HEADS // KEY_VALUE_HEADS, HEAD_SIZE
    )
    cached_key_rows = key_value_cache[:, 0].reshape(
        request_total, CACHE_SLOTS, KEY_VALUE_HEADS, HEAD_SIZE
    )
    cached_value_rows = key_value_cache[:, 1].reshape(
        request_total, CACHE_SLOTS, KEY_VALUE_HEADS, HEAD_SIZE
    )
    tree_key_rows = tree_key_value[:, 0].reshape(
        request_total, TREE_NODES, KEY_VALUE_HEADS, HEAD_SIZE
    )
    tree_value_rows = tree_key_value[:, 1].reshape(
        request_total, TREE_NODES, KEY_VALUE_HEADS, HEAD_SIZE
    )
    score_scale = HEAD_SIZE ** (-0.5)
    cache_scores = (
        jnp.einsum(
            "rtgqd,rlgd->rgtql",
            query_head_count,
            cached_key_rows,
            preferred_element_type=jnp.float32,
        )
        * score_scale
    )
    tree_scores = (
        jnp.einsum(
            "rtgqd,rugd->rgtqu", query_head_count, tree_key_rows, preferred_element_type=jnp.float32
        )
        * score_scale
    )
    visible = jnp.arange(CACHE_SLOTS, dtype=jnp.int32)[None, :] < lengths[:, None]
    related = ancestors(parents)
    cache_scores = jnp.where(visible[:, None, None, None, :], cache_scores, -1e30)
    tree_scores = jnp.where(related[:, None, :, None, :], tree_scores, -1e30)
    row_peak = jnp.maximum(jnp.max(cache_scores, axis=-1), jnp.max(tree_scores, axis=-1))[..., None]
    cache_exp = jnp.exp(cache_scores - row_peak)
    tree_exp = jnp.exp(tree_scores - row_peak)
    denominator = (jnp.sum(cache_exp, axis=-1) + jnp.sum(tree_exp, axis=-1))[..., None]
    cache_weights = (cache_exp / denominator).astype(jnp.bfloat16)
    tree_weights = (tree_exp / denominator).astype(jnp.bfloat16)
    context = jnp.einsum(
        "rgtql,rlgd->rtgqd", cache_weights, cached_value_rows, preferred_element_type=jnp.float32
    ) + jnp.einsum(
        "rgtqu,rugd->rtgqd", tree_weights, tree_value_rows, preferred_element_type=jnp.float32
    )
    return context.reshape(request_total * TREE_NODES, QUERY_HEADS * HEAD_SIZE)


VMEM_LIMIT = 66_000_000


def greet(n, me):
    barrier = pltpu.get_barrier_semaphore()

    def hello(k, carry):
        pl.semaphore_signal(barrier, inc=1, device_id={"expert": lax.rem(me + k, n)})
        return carry

    lax.fori_loop(1, n, hello, 0)
    pl.semaphore_wait(barrier, n - 1)


def push(src, dst, send_sem, recv_sem, peer):
    return pltpu.make_async_remote_copy(
        src_ref=src,
        dst_ref=dst,
        send_sem=send_sem,
        recv_sem=recv_sem,
        device_id={"expert": peer},
        device_id_type=pl.DeviceIdType.MESH,
    )


def moe_kernel(
    n,
    group_size,
    pair_slots,
    down_slots,
    packed,
    gate_hbm,
    up_hbm,
    down_hbm,
    grouped,
    gate_buf,
    up_buf,
    down_buf,
    arrived,
    rows_wide,
    rows,
    activation,
    result,
    leaving,
    returned,
    pair_sem,
    down_sem,
    out_sem,
    in_sem,
    back_out_sem,
    back_in_sem,
    own_sem,
):
    me = lax.axis_index("expert")
    width = gate_hbm.shape[1]
    chunk = gate_buf.shape[2]
    pair_count = width // chunk
    piece = down_buf.shape[2]
    piece_count = down_hbm.shape[1] // piece

    def pair_copies(i):
        slot = lax.rem(i, pair_slots)
        cols = pl.ds(pl.multiple_of(i * chunk, chunk), chunk)
        return (
            pltpu.make_async_copy(gate_hbm.at[:, cols], gate_buf.at[slot], pair_sem.at[0, slot]),
            pltpu.make_async_copy(up_hbm.at[:, cols], up_buf.at[slot], pair_sem.at[1, slot]),
        )

    def down_copy(i):
        slot = lax.rem(i, down_slots)
        cols = pl.ds(pl.multiple_of(i * piece, piece), piece)
        return pltpu.make_async_copy(down_hbm.at[:, cols], down_buf.at[slot], down_sem.at[slot])

    def start_pair(i, carry):
        for copy in pair_copies(i):
            copy.start()
        return carry

    def start_down(i, carry):
        down_copy(i).start()
        return carry

    lax.fori_loop(0, pair_slots, start_pair, 0)
    greet(n, me)

    def dispatch(k, carry):
        peer = lax.rem(me + k, n)
        push(
            packed.at[peer // group_size], arrived.at[me], out_sem.at[peer], in_sem.at[me], peer
        ).start()
        return carry

    lax.fori_loop(1, n, dispatch, 0)
    own = pltpu.make_async_copy(packed.at[me // group_size], arrived.at[me], own_sem)
    own.start()
    lax.fori_loop(0, down_slots, start_down, 0)
    own.wait()

    def take(k, carry):
        source = lax.rem(me + n - k, n)
        push(
            packed.at[0], arrived.at[source], out_sem.at[source], in_sem.at[source], source
        ).wait_recv()
        return carry

    lax.fori_loop(1, n, take, 0)

    def both(pair):
        return pl.ds(pl.multiple_of(pair * 2 * CAP, 2 * CAP), 2 * CAP)

    def widen(pair, carry):
        rows_wide[both(pair), :] = jnp.concatenate(
            [arrived[2 * pair].astype(jnp.float32), arrived[2 * pair + 1].astype(jnp.float32)],
            axis=0,
        )
        return carry

    lax.fori_loop(0, n // 2, widen, 0)
    rows[...] = rows_wide[...].astype(jnp.bfloat16)

    def pair_step(i, carry):
        slot = lax.rem(i, pair_slots)
        for copy in pair_copies(i):
            copy.wait()
        gate_val = jnp.dot(rows[...], gate_buf[slot], preferred_element_type=jnp.float32)
        up_val = jnp.dot(rows[...], up_buf[slot], preferred_element_type=jnp.float32)
        cols = pl.ds(pl.multiple_of(i * chunk, chunk), chunk)
        activation[:, cols] = (jax.nn.silu(gate_val) * up_val).astype(jnp.bfloat16)

        @pl.when(i + pair_slots < pair_count)
        def _():
            start_pair(i + pair_slots, 0)

        return carry

    lax.fori_loop(0, pair_count, pair_step, 0)

    def down_step(i, carry):
        slot = lax.rem(i, down_slots)
        down_copy(i).wait()
        result[...] = jnp.dot(
            activation[...], down_buf[slot], preferred_element_type=jnp.float32
        )

        @pl.when(i + down_slots < piece_count)
        def _():
            start_down(i + down_slots, 0)

        def narrow(pair, inner):
            block = result[both(pair), :]
            leaving[2 * pair, i] = block[:CAP].astype(jnp.bfloat16)
            leaving[2 * pair + 1, i] = block[CAP:].astype(jnp.bfloat16)
            return inner

        lax.fori_loop(0, n // 2, narrow, 0)

        def send_back(k, inner):
            peer = lax.rem(me + k, n)
            push(
                leaving.at[peer, i],
                returned.at[me, i],
                back_out_sem.at[peer],
                back_in_sem.at[me],
                peer,
            ).start()
            return inner

        lax.fori_loop(1, n, send_back, 0)
        return carry

    lax.fori_loop(0, piece_count, down_step, 0)
    returned[me] = leaving[me]

    def drain(k, carry):
        peer = lax.rem(me + n - k, n)
        push(
            leaving.at[peer], returned.at[peer], back_out_sem.at[peer], back_in_sem.at[peer], peer
        ).wait()
        push(
            packed.at[0], arrived.at[peer], out_sem.at[peer], in_sem.at[peer], peer
        ).wait_send()
        return carry

    lax.fori_loop(1, n, drain, 0)

    def gather(expert, carry):
        for i in range(piece_count):

            def add(member, total):
                return total + returned[expert * group_size + member, i].astype(jnp.float32)

            grouped[expert, :, i * piece : (i + 1) * piece] = lax.fori_loop(
                0, group_size, add, jnp.zeros((CAP, piece), jnp.float32)
            )
        return carry

    lax.fori_loop(0, EXPERTS, gather, 0)


def moe(packed, gate_weight, up_weight, down_weight, n):
    model_width, width = gate_weight.shape
    row_count = n * CAP
    chunk = min(512, width)
    piece = model_width // 4
    pair_slots = min(3, width // chunk)
    down_slots = min(2, model_width // piece)
    anywhere = pl.BlockSpec(memory_space=pl.ANY)
    whole = pl.BlockSpec(memory_space=pltpu.VMEM)
    bf16, f32 = jnp.bfloat16, jnp.float32
    return pl.pallas_call(
        functools.partial(moe_kernel, n, n // EXPERTS, pair_slots, down_slots),
        out_shape=jax.ShapeDtypeStruct((EXPERTS, CAP, model_width), f32),
        in_specs=[whole, anywhere, anywhere, anywhere],
        out_specs=whole,
        scratch_shapes=[
            pltpu.VMEM((pair_slots, model_width, chunk), bf16),
            pltpu.VMEM((pair_slots, model_width, chunk), bf16),
            pltpu.VMEM((down_slots, width, piece), bf16),
            pltpu.VMEM((n, CAP, model_width), bf16),
            pltpu.VMEM((row_count, model_width), f32),
            pltpu.VMEM((row_count, model_width), bf16),
            pltpu.VMEM((row_count, width), bf16),
            pltpu.VMEM((row_count, piece), f32),
            pltpu.VMEM((n, model_width // piece, CAP, piece), bf16),
            pltpu.VMEM((n, model_width // piece, CAP, piece), bf16),
            pltpu.SemaphoreType.DMA((2, pair_slots)),
            pltpu.SemaphoreType.DMA((down_slots,)),
            pltpu.SemaphoreType.DMA((n,)),
            pltpu.SemaphoreType.DMA((n,)),
            pltpu.SemaphoreType.DMA((n,)),
            pltpu.SemaphoreType.DMA((n,)),
            pltpu.SemaphoreType.DMA,
        ],
        compiler_params=pltpu.CompilerParams(
            collective_id=0, has_side_effects=True, vmem_limit_bytes=VMEM_LIMIT
        ),
        name="moe",
    )(packed, gate_weight, up_weight, down_weight)


def draft_kernel(
    n,
    share,
    piece,
    blocks,
    fc_hbm,
    out,
    fc_buf,
    arrived,
    rows_wide,
    result,
    leaving,
    returned,
    fc_sem,
    out_sem,
    in_sem,
    back_out_sem,
    back_in_sem,
):
    me = lax.axis_index("expert")
    piece_count = fc_hbm.shape[1] // piece
    half = piece // 2

    def fc_copy(i):
        cols = pl.ds(pl.multiple_of(i * piece, piece), piece)
        return pltpu.make_async_copy(fc_hbm.at[:, cols], fc_buf.at[i], fc_sem.at[i])

    def start_fc(i, carry):
        fc_copy(i).start()
        return carry

    lax.fori_loop(0, piece_count, start_fc, 0)
    greet(n, me)

    def dispatch(k, carry):
        peer = lax.rem(me + k, n)
        push(blocks.at[peer], arrived.at[me], out_sem.at[peer], in_sem.at[me], peer).start()
        return carry

    lax.fori_loop(1, n, dispatch, 0)
    rows_wide[pl.ds(me * share, share), :] = blocks[me]

    def take(k, carry):
        source = lax.rem(me + n - k, n)
        push(
            blocks.at[source], arrived.at[source], out_sem.at[source], in_sem.at[source], source
        ).wait()
        rows_wide[pl.ds(source * share, share), :] = arrived[source]
        return carry

    lax.fori_loop(1, n, take, 0)

    def step(i, carry):
        fc_copy(i).wait()
        result[...] = jnp.dot(
            rows_wide[...].astype(jnp.bfloat16), fc_buf[i], preferred_element_type=jnp.float32
        )

        def split(source, inner):
            block = result[pl.ds(source * share, share), :]
            leaving[source, i] = jnp.concatenate(
                [block[:, :half], block[:, half:]], axis=0
            ).astype(jnp.bfloat16)
            return inner

        lax.fori_loop(0, n, split, 0)

        def send_back(k, inner):
            peer = lax.rem(me + k, n)
            push(
                leaving.at[peer, i],
                returned.at[me, i],
                back_out_sem.at[peer],
                back_in_sem.at[me],
                peer,
            ).start()
            return inner

        lax.fori_loop(1, n, send_back, 0)
        return carry

    lax.fori_loop(0, piece_count, step, 0)
    returned[me] = leaving[me]

    def drain(k, carry):
        peer = lax.rem(me + n - k, n)
        push(
            leaving.at[peer], returned.at[peer], back_out_sem.at[peer], back_in_sem.at[peer], peer
        ).wait()
        return carry

    lax.fori_loop(1, n, drain, 0)
    for i in range(piece_count):

        def add(source, total):
            return total + returned[source, i].astype(jnp.float32)

        total = lax.fori_loop(0, n, add, jnp.zeros((2 * share, half), jnp.float32))
        out[:, i * piece : i * piece + half] = total[:share]
        out[:, i * piece + half : (i + 1) * piece] = total[share:]


def draft(blocks, draft_fc):
    n, share, depth = blocks.shape
    model_width = draft_fc.shape[1]
    piece = model_width // 4
    pieces = model_width // piece
    whole = pl.BlockSpec(memory_space=pltpu.VMEM)
    f32 = jnp.float32
    return pl.pallas_call(
        functools.partial(draft_kernel, n, share, piece),
        out_shape=jax.ShapeDtypeStruct((share, model_width), f32),
        in_specs=[whole, pl.BlockSpec(memory_space=pl.ANY)],
        out_specs=whole,
        scratch_shapes=[
            pltpu.VMEM((pieces, depth, piece), jnp.bfloat16),
            pltpu.VMEM((n, share, depth), f32),
            pltpu.VMEM((n * share, depth), f32),
            pltpu.VMEM((n * share, piece), f32),
            pltpu.VMEM((n, pieces, 2 * share, piece // 2), jnp.bfloat16),
            pltpu.VMEM((n, pieces, 2 * share, piece // 2), jnp.bfloat16),
            pltpu.SemaphoreType.DMA((pieces,)),
            pltpu.SemaphoreType.DMA((n,)),
            pltpu.SemaphoreType.DMA((n,)),
            pltpu.SemaphoreType.DMA((n,)),
            pltpu.SemaphoreType.DMA((n,)),
        ],
        compiler_params=pltpu.CompilerParams(
            collective_id=1, has_side_effects=True, vmem_limit_bytes=VMEM_LIMIT
        ),
        name="draft",
    )(blocks, draft_fc)


SLICE = 1024
LANES = 128
UNIT = 256


def greet_near(group, mine, lane):
    barrier = pltpu.get_barrier_semaphore()
    for step in range(1, EXPERTS):
        peer = lax.rem(mine + step, EXPERTS) * group + lane
        pl.semaphore_signal(barrier, inc=1, device_id={"expert": peer})
    for step in range(1, group):
        peer = mine * group + lax.rem(lane + step, group)
        pl.semaphore_signal(barrier, inc=1, device_id={"expert": peer})
    return barrier


def fused_kernel(
    n,
    slots,
    lengths_hbm,
    parents_hbm,
    routes_hbm,
    accepted_hbm,
    queries_hbm,
    tree_hbm,
    cache_hbm,
    residual_hbm,
    gain_hbm,
    router_hbm,
    embed_hbm,
    gate_hbm,
    up_hbm,
    down_hbm,
    fc_hbm,
    layer_out,
    draft_out,
    lengths,
    parents,
    routes,
    accepted,
    weights,
    queries,
    tree,
    keys,
    values,
    residual,
    gain,
    router,
    embed,
    tree_rows,
    hidden,
    normed,
    packed,
    arrived,
    rows,
    gate_sum,
    up_sum,
    activation,
    leaving,
    returned,
    chip_sum,
    chip_leaving,
    chip_returned,
    home_leaving,
    home_returned,
    pick_rows,
    pick_arrived,
    shares,
    share_leaving,
    late_shares,
    late_leaving,
    share_rows,
    hidden_row,
    embed_row,
    blocks,
    block_rows,
    draft_sum,
    draft_wide,
    pair_leaving,
    pair_returned,
    draft_leaving,
    draft_returned,
    load_sem,
    input_sem,
    out_sem,
    in_sem,
    plane_out_sem,
    plane_in_sem,
    core_out_sem,
    core_in_sem,
    chip_out_sem,
    chip_in_sem,
    home_out_sem,
    home_in_sem,
    pick_out_sem,
    pick_in_sem,
    share_out_sem,
    late_out_sem,
    share_in_sem,
    block_out_sem,
    block_in_sem,
    pair_out_sem,
    pair_in_sem,
    draft_out_sem,
    draft_in_sem,
):
    bf16, f32 = jnp.bfloat16, jnp.float32
    me = lax.axis_index("expert")
    group = n // EXPERTS
    mine = me // group
    lane = lax.rem(me, group)
    core = lax.rem(lane, 2)
    across = lane // 2
    core_peer = mine * group + across * 2 + (1 - core)
    chip_peer = mine * group + (1 - across) * 2 + core
    model_width = down_hbm.shape[1]
    width = down_hbm.shape[0]
    depth = fc_hbm.shape[0]
    slice_count = model_width // SLICE
    half_count = width // SLICE
    half = SLICE // 2
    chunks = [(0, half), (half, half)] + [(k * SLICE, SLICE) for k in range(1, slice_count)]
    last = model_width - SLICE
    pieces = [(k * SLICE, SLICE) for k in range(slice_count - 1)]
    pieces += [(last, SLICE - UNIT), (model_width - UNIT, UNIT)]
    piece_count = len(pieces)
    unit_count = depth // UNIT
    block_count = model_width // depth
    late_block = block_count // 2
    late_unit = late_block * unit_count
    padded = 8
    share = EXPERTS * CAP
    cache_slots = cache_hbm.shape[2]
    key_rows = keys.shape[0]
    line_count = model_width // LANES
    lines = SLICE // LANES
    part_count = draft_leaving.shape[0]
    each = line_count // part_count

    pairs = [
        ("pair", k, h, i) for k in range(slice_count) for h in range(half_count) for i in range(2)
    ]
    downs = [("down", p, a) for p in range(piece_count) for a in range(half_count)]
    order = pairs + downs + [("fc", p) for p in range(slice_count)]
    place = {item: i for i, item in enumerate(order)}
    sem_count = load_sem.shape[0]

    def load_group(item):
        if item[0] == "pair":
            return item[1]
        if item[0] == "down":
            return slice_count + item[1]
        return slice_count + piece_count

    def wait_loads(item):
        if item[0] == "pair":
            view = weights.at[0 : 2 * half_count]
        elif item[0] == "down":
            view = weights.at[0:half_count, :, 0 : pieces[item[1]][1]]
        else:
            view = weights.at[0:slice_count, 0:depth, :]
        pltpu.make_async_copy(view, view, load_sem.at[load_group(item) % sem_count]).wait()

    def load_copy(item):
        i = place[item]
        slot = weights.at[i % slots]
        if item[0] == "pair":
            k, h = item[1], item[2]
            source = (gate_hbm, up_hbm)[item[3]]
            view = source.at[k * SLICE : (k + 1) * SLICE, h * SLICE : (h + 1) * SLICE]
        elif item[0] == "down":
            a = item[2]
            start, size = pieces[item[1]]
            view = down_hbm.at[a * SLICE : (a + 1) * SLICE, start : start + size]
            slot = weights.at[i % slots, :, 0:size]
        else:
            p = item[1]
            view = fc_hbm.at[:, p * SLICE : (p + 1) * SLICE]
            slot = weights.at[i % slots, 0:depth, :]
        return pltpu.make_async_copy(view, slot, load_sem.at[load_group(item) % sem_count])

    def start_load(i):
        if i < len(order):
            load_copy(order[i]).start()

    inputs = [
        pltpu.make_async_copy(source, target, input_sem.at[i])
        for i, (source, target) in enumerate(
            [
                (queries_hbm, queries),
                (tree_hbm, tree),
                (cache_hbm.at[0, 0], keys.at[0:cache_slots, :]),
                (residual_hbm, residual),
                (cache_hbm.at[0, 1], values.at[0:cache_slots, :]),
                (gain_hbm, gain),
                (router_hbm, router),
                (embed_hbm, embed),
                (lengths_hbm, lengths),
                (parents_hbm, parents),
                (routes_hbm, routes),
                (accepted_hbm, accepted),
            ]
        )
    ]
    for copy in inputs[8:] + inputs[:8]:
        copy.start()
    barrier = greet_near(group, mine, lane)
    for copy in inputs[8:]:
        copy.wait()

    row8 = lax.broadcasted_iota(jnp.int32, (padded, LANES), 0)
    col8 = lax.broadcasted_iota(jnp.int32, (padded, LANES), 1)
    node_ids = lax.broadcasted_iota(jnp.int32, (1, LANES), 1)
    reached = []
    related = jnp.zeros((padded, LANES), f32)
    for node in range(TREE_NODES):
        row = (node_ids == node).astype(f32)
        parent = parents[node]
        for earlier in range(node):
            row = row + jnp.where(parent == earlier, reached[earlier], 0.0)
        reached.append(row)
        related = related + jnp.where(row8 == node, row, 0.0)
    slot_ids = lax.broadcasted_iota(jnp.int32, (padded, cache_slots), 1)
    bias = jnp.concatenate(
        [
            jnp.where(slot_ids < lengths[0, 0], 0.0, -1e30),
            jnp.where(related > 0.5, 0.0, -1e30),
        ],
        axis=1,
    )
    heads_each = QUERY_HEADS // KEY_VALUE_HEADS
    bias = jnp.concatenate([bias] * heads_each, axis=0)

    def named(choice, token):
        expert = routes[choice, token]
        rank = jnp.int32(0)
        for earlier in range(token):
            for other in range(2):
                rank = rank + jnp.where(routes[other, earlier] == expert, 1, 0)
        return expert, rank

    places = [[named(choice, token) for choice in range(2)] for token in range(TREE_NODES)]

    for copy in inputs[:3]:
        copy.wait()
    for i in range(slots):
        start_load(i)
    tree_rows[...] = jnp.zeros_like(tree_rows)
    for token in range(TREE_NODES):
        both = tree[token].astype(f32)
        tree_rows[0, token : token + 1, :] = both[0:1]
        tree_rows[1, token : token + 1, :] = both[1:2]
    tile = tree_rows.shape[1]
    blank = jnp.zeros((key_rows - cache_slots - tile, keys.shape[1]), bf16)
    keys[cache_slots : cache_slots + tile, :] = tree_rows[0].astype(bf16)
    keys[cache_slots + tile :, :] = blank
    values[cache_slots : cache_slots + tile, :] = tree_rows[1].astype(bf16)
    values[cache_slots + tile :, :] = blank
    spare = jnp.zeros((padded - TREE_NODES, HEAD_SIZE), f32)
    score_scale = HEAD_SIZE ** (-0.5)
    weights_of = []
    for g in range(KEY_VALUE_HEADS):
        parts = []
        for q in range(heads_each):
            head = g * heads_each + q
            parts.append(queries[:, head * HEAD_SIZE : (head + 1) * HEAD_SIZE].astype(f32))
            parts.append(spare)
        head_queries = jnp.concatenate(parts, axis=0).astype(bf16)
        scores = (
            lax.dot_general(
                head_queries,
                keys[:, g * HEAD_SIZE : (g + 1) * HEAD_SIZE],
                (((1,), (1,)), ((), ())),
                preferred_element_type=f32,
            )
            * score_scale
            + bias
        )
        peak = jnp.max(scores, axis=-1, keepdims=True)
        grown = jnp.exp(scores - peak)
        total = jnp.sum(grown, axis=-1, keepdims=True)
        weights_of.append((grown * (1.0 / total)).astype(bf16))
    for copy in inputs[3:5]:
        copy.wait()
    square = jnp.zeros((padded, HEAD_SIZE), f32)
    for g in range(KEY_VALUE_HEADS):
        context = jnp.dot(
            weights_of[g],
            values[:, g * HEAD_SIZE : (g + 1) * HEAD_SIZE],
            preferred_element_type=f32,
        )
        for q in range(heads_each):
            head = g * heads_each + q
            cols = slice(head * HEAD_SIZE, (head + 1) * HEAD_SIZE)
            state = context[q * padded : (q + 1) * padded] + jnp.concatenate(
                [residual[:, cols].astype(f32), spare], axis=0
            )
            hidden[:, cols] = state
            square = square + state * state
    for copy in inputs[5:8]:
        copy.wait()
    level = lax.rsqrt(jnp.sum(square, axis=-1, keepdims=True) / model_width + EPSILON)

    slot_row = lax.broadcasted_iota(jnp.int32, (EXPERTS * padded, padded), 0)
    slot_col = lax.broadcasted_iota(jnp.int32, (EXPERTS * padded, padded), 1)
    placing = jnp.zeros((EXPERTS * padded, padded), f32)
    for token, choices in enumerate(places):
        for expert, rank in choices:
            placing = placing + jnp.where(
                (slot_row == expert * padded + rank) & (slot_col == token), 1.0, 0.0
            )
    placing = placing.astype(bf16)

    def to_plane(c, step):
        plane = lax.rem(mine + step, EXPERTS)
        cols = pl.ds(chunks[c][0], chunks[c][1])
        return push(
            packed.at[plane, :, cols],
            arrived.at[mine, :, cols],
            out_sem,
            in_sem.at[c],
            plane * group + lane,
        )

    def awaited(ref, sem):
        return push(ref, ref, sem, sem, core_peer)

    def pack_step(c):
        start, size = chunks[c]
        cols = slice(start, start + size)
        gains = [
            gain[t : t + 1, :].astype(f32)
            for t in range(start // LANES, (start + size) // LANES)
        ]
        normal = (hidden[:, cols] * level * jnp.concatenate(gains, axis=1)).astype(bf16)
        normed[:, cols] = normal
        spread = jnp.dot(placing, normal, preferred_element_type=f32)
        for e in range(EXPERTS):
            packed[e, :, cols] = spread[e * padded : e * padded + CAP].astype(bf16)
        arrived[mine, :, cols] = packed[mine, :, cols]

    pack_step(0)
    pl.semaphore_wait(barrier, EXPERTS + group - 2)
    for c in range(len(chunks)):
        if c > 0:
            pack_step(c)
        for step in range(1, EXPERTS):
            to_plane(c, step).start()

    token_row = row8[:, 0:1]
    embed_row[...] = embed[...].astype(f32)
    for k in range(slice_count):
        cols = slice(k * SLICE, (k + 1) * SLICE)
        hidden_row[:, cols] = jnp.sum(
            jnp.where(token_row == accepted[0, 0], hidden[:, cols], 0.0), axis=0, keepdims=True
        )

    def block_push(row, b, j):
        source = row.at[:, b * depth : (b + 1) * depth]
        return push(source, blocks.at[me], block_out_sem, block_in_sem, j)

    def send_block(row, b, j):
        @pl.when(me != j)
        def _():
            block_push(row, b, j).start()

        @pl.when(me == j)
        def _():
            blocks[j] = row[:, b * depth : (b + 1) * depth]

    logits = [jnp.zeros((padded, 1), f32) for _ in range(EXPERTS)]
    for k in range(slice_count):
        cols = slice(k * SLICE, (k + 1) * SLICE)
        normal = normed[:, cols].astype(f32)
        for e in range(EXPERTS):
            logits[e] = logits[e] + jnp.sum(
                normal * router[e : e + 1, cols].astype(f32), axis=-1, keepdims=True
            )
    ids = [jnp.full((padded, 1), -1, jnp.int32) for _ in range(4)]
    for token, choices in enumerate(places):
        for choice, (expert, rank) in enumerate(choices):
            ids[choice] = jnp.where(token_row == token, expert, ids[choice])
            ids[2 + choice] = jnp.where(token_row == token, expert * CAP + rank, ids[2 + choice])
    first_logit = jnp.zeros((padded, 1), f32)
    second_logit = jnp.zeros((padded, 1), f32)
    for e in range(EXPERTS):
        first_logit = first_logit + jnp.where(ids[0] == e, logits[e], 0.0)
        second_logit = second_logit + jnp.where(ids[1] == e, logits[e], 0.0)
    first_share = jax.nn.sigmoid(first_logit - second_logit)
    share_col = col8[:, :share]
    weighted = jnp.where(share_col == ids[2], first_share, 0.0) + jnp.where(
        share_col == ids[3], 1.0 - first_share, 0.0
    )

    def split(exact):
        high = exact.astype(bf16).astype(f32)
        middle = (exact - high).astype(bf16).astype(f32)
        low = exact - high - middle
        return jnp.concatenate([high, middle, low], axis=0).astype(bf16)

    mixers = split(weighted)

    def pick_push(step, turn):
        plane = lax.rem(mine + step, EXPERTS)
        column = lax.rem(across + turn, 2)
        return push(
            pick_rows.at[plane],
            pick_arrived.at[across * EXPERTS + mine],
            pick_out_sem,
            pick_in_sem,
            plane * group + column * 2 + core,
        )

    for e in range(EXPERTS):
        chosen = jnp.zeros((padded, LANES), f32)
        for expert, position, portion in (
            (ids[0], ids[2], first_share),
            (ids[1], ids[3], 1.0 - first_share),
        ):
            here = (col8 == mine * CAP + position - expert * CAP) & (expert == e)
            chosen = chosen + jnp.where(here, portion, 0.0)
        pick_rows[e] = jnp.sum(
            jnp.where(token_row == accepted[0, 0], chosen, 0.0), axis=0, keepdims=True
        )
    def send_early():
        for step in range(EXPERTS):
            for turn in range(2):
                if step + turn > 0:
                    pick_push(step, turn).start()
        for b in range(block_count):
            send_block(embed_row, b, block_count + b)
            send_block(hidden_row, b, b)

    pick_arrived[across * EXPERTS + mine] = pick_rows[mine]

    def row_push(c, which, sem, peer):
        start, size = chunks[c]
        block = rows.at[pl.ds(pl.multiple_of(which * share, share), share), pl.ds(start, size)]
        return push(block, block, plane_out_sem, plane_in_sem.at[c, sem], peer)

    chip_lane = (1 - across) * 2 + core

    def gather_step(k):
        start, size = chunks[k]
        cols = slice(start, start + size)
        awaited(arrived.at[0 : EXPERTS - 1, :, pl.ds(start, size)], in_sem.at[k]).wait_recv()
        rows[pl.ds(pl.multiple_of(lane * share, share), share), cols] = jnp.concatenate(
            [arrived[s, :, cols].astype(f32) for s in range(EXPERTS)], axis=0
        ).astype(bf16)
        row_push(k, lane, 0, chip_peer).start()
        row_push(k, lane, 1, core_peer).start()

    def forward_step(k):
        row_push(k, chip_lane, 0, chip_peer).wait_recv()
        row_push(k, chip_lane, 1, core_peer).start()

    def expert_step(c):
        start, size = chunks[c]
        pair_rows = rows.at[0 : 2 * share, pl.ds(start, size)]
        awaited(pair_rows, plane_in_sem.at[c, 1]).wait_recv()
        k, first = start // SLICE, start % SLICE
        final = start + size == model_width
        if first == 0:
            wait_loads(("pair", k))
        for h in range(half_count):
            cols = slice(h * SLICE, (h + 1) * SLICE)
            sums = []
            for i, total in ((0, gate_sum), (1, up_sum)):
                item = ("pair", k, h, i)
                value = jnp.dot(
                    rows[:, start : start + size],
                    weights[place[item] % slots, first : first + size, :],
                    preferred_element_type=f32,
                )
                if start > 0:
                    value = value + total[:, cols]
                if not final:
                    total[:, cols] = value
                sums.append(value)
                if first + size == SLICE:
                    start_load(place[item] + slots)
            if final:
                activation[h] = (jax.nn.silu(sums[0]) * sums[1]).astype(bf16)

    for t in range(len(chunks) + 3):
        if t < len(chunks):
            gather_step(t)
        if t == 2:
            send_early()
        if 0 <= t - 2 < len(chunks):
            forward_step(t - 2)
        if 0 <= t - 3 < len(chunks):
            expert_step(t - 3)

    def piece_cols(p):
        return pl.ds(pieces[p][0], pieces[p][1])

    def core_push(p):
        cols = piece_cols(p)
        return push(
            leaving.at[1 - core, :, :, cols],
            returned.at[:, :, cols],
            core_out_sem,
            core_in_sem.at[p],
            core_peer,
        )

    def chip_push(p):
        cols = piece_cols(p)
        return push(
            chip_leaving.at[:, cols],
            chip_returned.at[:, cols],
            chip_out_sem,
            chip_in_sem.at[p],
            chip_peer,
        )

    def to_home(p, step):
        plane = lax.rem(mine + step, EXPERTS)
        return push(
            home_leaving.at[plane, :, piece_cols(p)],
            home_returned.at[mine, :, piece_cols(p)],
            home_out_sem,
            home_in_sem,
            plane * group + lane,
        )

    def partial_step(p):
        start, size = pieces[p]
        cols = slice(start, start + size)
        partial = None
        wait_loads(("down", p))
        for a in range(half_count):
            item = ("down", p, a)
            value = jnp.dot(
                activation[a], weights[place[item] % slots, :, 0:size], preferred_element_type=f32
            )
            partial = value if partial is None else partial + value
            start_load(place[item] + slots)
        for member in range(group):
            block = partial[member * share : (member + 1) * share].astype(bf16)
            leaving[member % 2, member // 2, :, cols] = block

        core_push(p).start()

    def core_step(p):
        core_push(p).wait_recv()
        start, size = pieces[p]
        cols = slice(start, start + size)
        far = 1 - across
        chip_leaving[:, cols] = (
            leaving[core, far, :, cols].astype(f32) + returned[far, :, cols].astype(f32)
        ).astype(bf16)
        chip_push(p).start()
        chip_sum[:, cols] = leaving[core, across, :, cols].astype(f32) + returned[across, :, cols].astype(
            f32
        )
        if start < late_unit * UNIT:
            return
        portions = [
            portion_of(
                both_mixers[column],
                leaving[core, column, :, cols].astype(f32) + returned[column, :, cols].astype(f32),
            )
            for column in range(2)
        ]
        send_shares(start, size, jnp.concatenate(portions, axis=0))

    def portion_of(pick_mixers, total):
        mixed = jnp.dot(pick_mixers, total.astype(bf16), preferred_element_type=f32)
        portion = mixed[:padded] + mixed[padded : 2 * padded] + mixed[2 * padded :]
        return portion[:EXPERTS]

    def send_shares(start, size, portion):
        for unit in range(start // UNIT, (start + size) // UNIT):
            b, part = unit // unit_count, unit % unit_count
            first = unit * UNIT - start
            value = portion[:, first : first + UNIT].astype(bf16)
            if unit < late_unit:
                source, target, sem = share_leaving.at[unit], shares, share_out_sem
            else:
                source, target, sem = late_leaving.at[unit - late_unit], late_shares, late_out_sem

            source[...] = value

            @pl.when(me != b)
            def _():
                push(
                    source,
                    target.at[part, me],
                    sem,
                    share_in_sem.at[part // (unit_count - 1)],
                    b,
                ).start()

            @pl.when(me == b)
            def _():
                target[part, b] = value

    held_back = 3

    def leave_step(p):
        for step in range(1, EXPERTS):
            to_home(p, step).start()

    def chip_step(p):
        start, size = pieces[p]
        cols = slice(start, start + size)
        chip_push(p).wait_recv()
        total = chip_sum[:, cols] + chip_returned[:, cols].astype(f32)
        if start < late_unit * UNIT:
            send_shares(start, size, portion_of(own_mixers, total))
        for s in range(EXPERTS):
            home_leaving[s, :, cols] = total[s * CAP : (s + 1) * CAP].astype(bf16)
        home_returned[mine, :, cols] = home_leaving[mine, :, cols]
        if p >= held_back:
            leave_step(p)

    def home_step(p):
        start, size = pieces[p]
        cols = slice(start, start + size)
        block = jnp.concatenate(
            [home_returned[e, :, cols].astype(f32) for e in range(EXPERTS)], axis=0
        ).astype(bf16)
        mixed = jnp.dot(mixers, block, preferred_element_type=f32)
        expert_sum = mixed[:padded] + mixed[padded : 2 * padded] + mixed[2 * padded :]
        result = (hidden[:, cols] + expert_sum).astype(bf16)
        layer_out[:, cols] = result[:TREE_NODES]

    pair_rows_count = n // 2
    own_place = across * EXPERTS + mine

    def pair_push(q):
        return push(
            pair_leaving.at[q], pair_returned.at[q], pair_out_sem, pair_in_sem.at[q], core_peer
        )

    def draft_push(q, row):
        peer = lax.rem(row, EXPERTS) * group + row // EXPERTS * 2 + core
        return push(
            draft_leaving.at[q, row],
            draft_returned.at[q, me // 2],
            draft_out_sem,
            draft_in_sem,
            peer,
        )

    def row_of(device):
        column = lax.rem(device, group) // 2
        return lax.rem(device, 2) * pair_rows_count + column * EXPERTS + device // group

    def block_step():
        awaited(blocks.at[0 : n - 1], block_in_sem).wait_recv()

        def take(source, carry):
            block_rows[pl.ds(row_of(source), 1), :] = blocks[source]
            return carry

        lax.fori_loop(0, n, take, 0)
        share_rows[...] = jnp.zeros_like(share_rows)

    def share_step(first, past):
        sem = share_in_sem.at[first // (unit_count - 1)]

        @pl.when((me >= late_block) & (me < block_count))
        def _():
            awaited(late_shares.at[first:past, 0 : n - 1], sem).wait_recv()
            for part in range(first, past):
                totals = []
                for c in range(2):
                    total = late_shares[part, c].astype(f32)
                    for member in range(c + 2, n, 2):
                        total = total + late_shares[part, member].astype(f32)
                    totals.append(total)
                sums = [
                    totals[c][column * EXPERTS : (column + 1) * EXPERTS]
                    for c in range(2)
                    for column in range(2)
                ]
                share_rows[:, part * UNIT : (part + 1) * UNIT] = jnp.concatenate(sums, axis=0)

        @pl.when(me < late_block)
        def _():
            awaited(shares.at[first:past, 0 : n - 1], sem).wait_recv()
            for part in range(first, past):
                sums = []
                for member in (0, 2, 1, 3):
                    total = shares[part, member].astype(f32)
                    for e in range(1, EXPERTS):
                        total = total + shares[part, e * group + member].astype(f32)
                    sums.append(total)
                share_rows[:, part * UNIT : (part + 1) * UNIT] = jnp.concatenate(sums, axis=0)

    def draft_step(first, past, final):
        share_step(first, past)
        deep = slice(first * UNIT, past * UNIT)
        draft_rows = (block_rows[:, deep] + share_rows[:, deep]).astype(bf16)
        per_part = slice_count // part_count
        if first == 0:
            wait_loads(("fc",))
        for q in range(part_count):
            for p in range(q * per_part, (q + 1) * per_part):
                item = ("fc", p)
                partial = jnp.dot(
                    draft_rows, weights[place[item] % slots, deep, :], preferred_element_type=f32
                )
                cols = slice(p * SLICE, (p + 1) * SLICE)
                if first > 0:
                    partial = partial + draft_sum[:, cols]
                if not final:
                    draft_sum[:, cols] = partial
                    continue
                for t in range(lines):
                    draft_wide[pl.ds(p * lines + t, n, stride=line_count), :] = partial[
                        :, t * LANES : (t + 1) * LANES
                    ]
            if not final:
                continue
            for i in range(pair_rows_count):
                start = ((1 - core) * pair_rows_count + i) * line_count + q * each
                pair_leaving[q, i] = draft_wide[
                    pl.ds(pl.multiple_of(start, each), each), :
                ].astype(bf16)
            pair_push(q).start()

    def pair_step(q):
        pair_push(q).wait_recv()
        for i in range(pair_rows_count):
            start = (core * pair_rows_count + i) * line_count + q * each
            total = draft_wide[pl.ds(pl.multiple_of(start, each), each), :] + pair_returned[
                q, i
            ].astype(f32)
            draft_leaving[q, i] = total.astype(bf16)

        def send_partial(k, carry):
            draft_push(q, lax.rem(own_place + k, pair_rows_count)).start()
            return carry

        lax.fori_loop(1, pair_rows_count, send_partial, 0)
        draft_returned[q, me // 2] = draft_leaving[q, own_place]

    pick_total = pick_arrived.shape[0]
    awaited(pick_arrived.at[0 : pick_total - 1], pick_in_sem).wait_recv()

    def mixers_of(column):
        picks = [pick_arrived[column * EXPERTS + s][:, :share] for s in range(EXPERTS)]
        picks.append(jnp.zeros((padded - EXPERTS, share), f32))
        return split(jnp.concatenate(picks, axis=0))

    own_mixers = mixers_of(across)
    both_mixers = [mixers_of(column) for column in range(2)]

    for p in range(piece_count):
        partial_step(p)
        if p > 0:
            core_step(p - 1)
        if p >= 4:
            chip_step(p - 4)
    core_step(piece_count - 1)
    for p in range(held_back):
        leave_step(p)
    block_step()
    for p in range(piece_count - 4, piece_count):
        chip_step(p)
    draft_step(0, unit_count - 1, False)
    draft_step(unit_count - 1, unit_count, True)
    for q in range(part_count):
        pair_step(q)
    awaited(home_returned.at[0 : EXPERTS - 1], home_in_sem).wait_recv()
    for p in range(piece_count):
        home_step(p)

    awaited(packed.at[0 : EXPERTS - 1], out_sem).wait_send()
    awaited(rows.at[0 : 3 * share, :], plane_out_sem).wait_send()
    awaited(pick_arrived.at[0 : pick_total - 1], pick_out_sem).wait_send()
    awaited(leaving.at[0], core_out_sem).wait_send()
    awaited(chip_leaving, chip_out_sem).wait_send()
    awaited(home_leaving.at[0 : EXPERTS - 1], home_out_sem).wait_send()
    awaited(blocks.at[0 : n - 1], block_out_sem).wait_send()
    for low, past, buffer, sem in (
        (0, late_block, share_leaving, share_out_sem),
        (late_block, block_count, late_leaving, late_out_sem),
    ):
        total = buffer.shape[0]
        owner = (me >= low) & (me < past)

        @pl.when(owner)
        def _():
            awaited(buffer.at[0 : total - unit_count], sem).wait_send()

        @pl.when(jnp.logical_not(owner))
        def _():
            awaited(buffer, sem).wait_send()

    awaited(pair_leaving, pair_out_sem).wait_send()
    awaited(draft_leaving.at[:, 0 : pair_rows_count - 1], draft_out_sem).wait_send()
    awaited(draft_returned.at[:, 0 : pair_rows_count - 1], draft_in_sem).wait_recv()
    for q in range(part_count):
        total = draft_returned[q, 0].astype(f32)
        for source in range(1, pair_rows_count):
            total = total + draft_returned[q, source].astype(f32)
        draft_out[q * each : (q + 1) * each, :] = total


def finish_kernel(layer, draft_lines, layer_out, draft_out):
    layer_out[...] = layer[...]
    for t in range(draft_lines.shape[0]):
        draft_out[:, t * LANES : (t + 1) * LANES] = draft_lines[t : t + 1, :].astype(jnp.bfloat16)


def fused(
    queries,
    tree_key_value,
    key_value_cache,
    lengths,
    parents,
    residual,
    ffn_gain,
    router,
    routes,
    gate_weight,
    up_weight,
    down_weight,
    accepted,
    next_embed,
    draft_fc,
    n,
):
    width, model_width = down_weight.shape
    depth = draft_fc.shape[0]
    group = n // EXPERTS
    share = EXPERTS * CAP
    slots = 24
    slices = model_width // SLICE
    halves = width // SLICE
    parts = 3
    pieces = slices + 1
    chunks = slices + 1
    units = depth // UNIT
    line_count = model_width // LANES
    kv_width = tree_key_value.shape[2]
    key_rows = key_value_cache.shape[2] + LANES
    in_hbm = pl.BlockSpec(memory_space=pltpu.HBM)
    whole = pl.BlockSpec(memory_space=pltpu.VMEM)
    bf16, f32 = jnp.bfloat16, jnp.float32
    dma = pltpu.SemaphoreType.DMA
    pinned = pltpu.with_memory_space_constraint
    layer, draft_lines = pl.pallas_call(
        functools.partial(fused_kernel, n, slots),
        out_shape=(
            pltpu.VMEM((TREE_NODES, model_width), bf16),
            pltpu.VMEM((line_count, LANES), f32),
        ),
        in_specs=[in_hbm] * 15,
        out_specs=(whole, whole),
        scratch_shapes=[
            pltpu.SMEM((1, 1), jnp.int32),
            pltpu.SMEM(parents.shape, jnp.int32),
            pltpu.SMEM(routes.T.shape, jnp.int32),
            pltpu.SMEM((1, 1), jnp.int32),
            pltpu.VMEM((slots, SLICE, SLICE), bf16),
            pltpu.VMEM((TREE_NODES, model_width), bf16),
            pltpu.VMEM((TREE_NODES, 2, kv_width), bf16),
            pltpu.VMEM((key_rows, kv_width), bf16),
            pltpu.VMEM((key_rows, kv_width), bf16),
            pltpu.VMEM((TREE_NODES, model_width), bf16),
            pltpu.VMEM((line_count, LANES), bf16),
            pltpu.VMEM((EXPERTS, model_width), bf16),
            pltpu.VMEM((1, model_width), bf16),
            pltpu.VMEM((2, 16, kv_width), f32),
            pltpu.VMEM((8, model_width), f32),
            pltpu.VMEM((8, model_width), bf16),
            pltpu.VMEM((EXPERTS, CAP, model_width), bf16),
            pltpu.VMEM((EXPERTS, CAP, model_width), bf16),
            pltpu.VMEM((group * share, model_width), bf16),
            pltpu.VMEM((group * share, width), f32),
            pltpu.VMEM((group * share, width), f32),
            pltpu.VMEM((halves, group * share, SLICE), bf16),
            pltpu.VMEM((2, 2, share, model_width), bf16),
            pltpu.VMEM((2, share, model_width), bf16),
            pltpu.VMEM((share, model_width), f32),
            pltpu.VMEM((share, model_width), bf16),
            pltpu.VMEM((share, model_width), bf16),
            pltpu.VMEM((EXPERTS, CAP, model_width), bf16),
            pltpu.VMEM((EXPERTS, CAP, model_width), bf16),
            pltpu.VMEM((EXPERTS, 1, LANES), f32),
            pltpu.VMEM((2 * EXPERTS, 1, LANES), f32),
            pltpu.VMEM((units, n, EXPERTS, UNIT), bf16),
            pltpu.VMEM((model_width // UNIT // 2, EXPERTS, UNIT), bf16),
            pltpu.VMEM((units, n, 2 * EXPERTS, UNIT), bf16),
            pltpu.VMEM((model_width // UNIT // 2, 2 * EXPERTS, UNIT), bf16),
            pltpu.VMEM((n, depth), f32),
            pltpu.VMEM((1, model_width), f32),
            pltpu.VMEM((1, model_width), f32),
            pltpu.VMEM((n, 1, depth), f32),
            pltpu.VMEM((n, depth), f32),
            pltpu.VMEM((n, model_width), f32),
            pltpu.VMEM((n * line_count, LANES), f32),
            pltpu.VMEM((parts, n // 2, line_count // parts, LANES), bf16),
            pltpu.VMEM((parts, n // 2, line_count // parts, LANES), bf16),
            pltpu.VMEM((parts, n // 2, line_count // parts, LANES), bf16),
            pltpu.VMEM((parts, n // 2, line_count // parts, LANES), bf16),
            dma((10,)),
            dma((12,)),
            dma,
            dma((chunks,)),
            dma,
            dma((chunks, 2)),
            dma,
            dma((pieces,)),
            dma,
            dma((pieces,)),
            dma,
            dma,
            dma,
            dma,
            dma,
            dma,
            dma((2,)),
            dma,
            dma,
            dma,
            dma((parts,)),
            dma,
            dma,
        ],
        compiler_params=pltpu.CompilerParams(
            collective_id=0, has_side_effects=True, vmem_limit_bytes=62_000_000
        ),
        name="fused",
    )(
        lengths.reshape(1, 1),
        parents,
        routes.T,
        accepted.reshape(1, 1),
        queries,
        tree_key_value,
        key_value_cache,
        residual,
        ffn_gain.reshape(line_count, LANES),
        router.T,
        next_embed,
        gate_weight,
        up_weight,
        down_weight,
        draft_fc,
    )
    return pl.pallas_call(
        finish_kernel,
        out_shape=(
            jax.ShapeDtypeStruct((TREE_NODES, model_width), bf16),
            jax.ShapeDtypeStruct((1, model_width), bf16),
        ),
        in_specs=[whole, whole],
        out_specs=(whole, whole),
        name="finish",
    )(pinned(layer, pltpu.VMEM), pinned(draft_lines, pltpu.VMEM))


def fits(lengths, gate_weight, draft_fc, n):
    model_width, width = gate_weight.shape
    depth = draft_fc.shape[0]
    return (
        lengths.shape[0] == 1
        and n == 4 * EXPERTS
        and width == 2 * SLICE
        and model_width == 6 * SLICE
        and depth % UNIT == 0
        and depth > UNIT
        and depth <= SLICE
        and n * depth == 2 * model_width
        and model_width // depth * depth == model_width
        and model_width // depth // 2 * depth == 3 * SLICE
    )


def per_device(
    queries,
    tree_key_value,
    key_value_cache,
    lengths,
    parents,
    residual,
    ffn_gain,
    router,
    routes,
    gate_weight,
    up_weight,
    down_weight,
    accepted,
    next_embed,
    draft_fc,
):
    devices = lax.axis_size("expert")
    if fits(lengths, gate_weight, draft_fc, devices):
        return fused(
            queries,
            tree_key_value,
            key_value_cache,
            lengths,
            parents,
            residual,
            ffn_gain,
            router,
            routes,
            gate_weight,
            up_weight,
            down_weight,
            accepted,
            next_embed,
            draft_fc,
            devices,
        )
    context = attention(queries, tree_key_value, key_value_cache, lengths, parents)
    hidden_state = residual.astype(jnp.float32) + context
    normed = (
        hidden_state
        * lax.rsqrt(jnp.mean(hidden_state * hidden_state, axis=-1, keepdims=True) + EPSILON)
        * ffn_gain.astype(jnp.float32)
    ).astype(jnp.bfloat16)
    tokens_here, model_width = normed.shape
    logits = jnp.dot(normed, router, preferred_element_type=jnp.float32)
    expert_ids = jnp.arange(EXPERTS, dtype=jnp.int32)
    first_hit = (routes[:, 0:1] == expert_ids[None, :]).astype(jnp.float32)
    second_hit = (routes[:, 1:2] == expert_ids[None, :]).astype(jnp.float32)
    first_logit = jnp.sum(logits * first_hit, axis=-1)
    second_logit = jnp.sum(logits * second_hit, axis=-1)
    first_share = jax.nn.sigmoid(first_logit - second_logit)
    mixing = first_share[:, None] * first_hit + (1.0 - first_share)[:, None] * second_hit
    hit_table = first_hit + second_hit
    slot_rank = jnp.cumsum(hit_table, axis=0) - 1.0
    slot_ids = jnp.arange(CAP, dtype=jnp.float32)
    placing = hit_table.T[:, None, :] * (slot_rank.T[:, None, :] == slot_ids[None, :, None]).astype(
        jnp.float32
    )
    packed = jnp.einsum(
        "ect,td->ecd", placing.astype(jnp.bfloat16), normed, preferred_element_type=jnp.float32
    ).astype(jnp.bfloat16)
    grouped = moe(packed, gate_weight, up_weight, down_weight, devices)
    weighted = placing * mixing.T[:, None, :]
    expert_sum = jnp.einsum("ect,ecd->td", weighted, grouped, precision=lax.Precision.HIGHEST)
    layer_out = (hidden_state + expert_sum).astype(jnp.bfloat16)
    request_total = lengths.shape[0]
    picker = (accepted[:, None] == jnp.arange(TREE_NODES, dtype=jnp.int32)[None, :]).astype(
        jnp.bfloat16
    )
    picked = jnp.einsum(
        "rt,rtd->rd",
        picker,
        layer_out.reshape(request_total, TREE_NODES, model_width),
        preferred_element_type=jnp.float32,
    ).astype(jnp.bfloat16)
    draft_in = jnp.concatenate([picked, next_embed], axis=1)
    depth = draft_fc.shape[0]
    blocks = draft_in.reshape(request_total, devices, depth).transpose(1, 0, 2)
    draft_out = draft(blocks.astype(jnp.float32), draft_fc).astype(jnp.bfloat16)
    return (layer_out, draft_out)


def solution(mesh):
    return jax.shard_map(
        per_device,
        mesh=mesh,
        in_specs=(
            P(("groups", "expert"), None),
            P(("groups", "expert"), None, None),
            P(("groups", "expert"), None, None, None),
            P(("groups", "expert")),
            P(("groups", "expert")),
            P(("groups", "expert"), None),
            P(),
            P(),
            P(("groups", "expert"), None),
            P(None, "expert"),
            P(None, "expert"),
            P("expert", None),
            P(("groups", "expert")),
            P(("groups", "expert"), None),
            P("expert", None),
        ),
        out_specs=(P(("groups", "expert"), None), P(("groups", "expert"), None)),
        check_vma=False,
    )
```

```python
import functools

import jax
import jax.numpy as jnp
from jax import lax
from jax.experimental import pallas as pl
from jax.experimental.pallas import tpu as pltpu
from jax.sharding import PartitionSpec as P

QUERY_HEADS = 48
KEY_VALUE_HEADS = 8
HEAD_SIZE = 128
EXPERTS = 4
TREE_NODES = 6
CACHE_SLOTS = 512
CAP = 4


EPSILON = 1e-05


def related_kernel(parents, out):
    node_ids = lax.broadcasted_iota(jnp.int32, (1, out.shape[2]), 1)
    for request in range(out.shape[0]):
        reached = []
        for node in range(TREE_NODES):
            row = (node_ids == node).astype(jnp.float32)
            parent = parents[request * TREE_NODES + node]
            for earlier in range(node):
                row = row + jnp.where(parent == earlier, reached[earlier], 0.0)
            reached.append(row)
            out[request, node : node + 1, :] = row


def ancestors(parent_ids):
    table = pl.pallas_call(
        related_kernel,
        out_shape=jax.ShapeDtypeStruct((parent_ids.shape[0] // TREE_NODES, TREE_NODES, 128), jnp.float32),
        in_specs=[pl.BlockSpec(memory_space=pltpu.SMEM)],
        out_specs=pl.BlockSpec(memory_space=pltpu.VMEM),
        name="related",
    )(parent_ids)
    return table[:, :, :TREE_NODES] > 0.5


def attention(queries, tree_key_value, key_value_cache, lengths, parents):
    request_total = lengths.shape[0]
    query_head_count = queries.reshape(
        request_total, TREE_NODES, KEY_VALUE_HEADS, QUERY_HEADS // KEY_VALUE_HEADS, HEAD_SIZE
    )
    cached_key_rows = key_value_cache[:, 0].reshape(
        request_total, CACHE_SLOTS, KEY_VALUE_HEADS, HEAD_SIZE
    )
    cached_value_rows = key_value_cache[:, 1].reshape(
        request_total, CACHE_SLOTS, KEY_VALUE_HEADS, HEAD_SIZE
    )
    tree_key_rows = tree_key_value[:, 0].reshape(
        request_total, TREE_NODES, KEY_VALUE_HEADS, HEAD_SIZE
    )
    tree_value_rows = tree_key_value[:, 1].reshape(
        request_total, TREE_NODES, KEY_VALUE_HEADS, HEAD_SIZE
    )
    score_scale = HEAD_SIZE ** (-0.5)
    cache_scores = (
        jnp.einsum(
            "rtgqd,rlgd->rgtql",
            query_head_count,
            cached_key_rows,
            preferred_element_type=jnp.float32,
        )
        * score_scale
    )
    tree_scores = (
        jnp.einsum(
            "rtgqd,rugd->rgtqu", query_head_count, tree_key_rows, preferred_element_type=jnp.float32
        )
        * score_scale
    )
    visible = jnp.arange(CACHE_SLOTS, dtype=jnp.int32)[None, :] < lengths[:, None]
    related = ancestors(parents)
    cache_scores = jnp.where(visible[:, None, None, None, :], cache_scores, -1e30)
    tree_scores = jnp.where(related[:, None, :, None, :], tree_scores, -1e30)
    row_peak = jnp.maximum(jnp.max(cache_scores, axis=-1), jnp.max(tree_scores, axis=-1))[..., None]
    cache_exp = jnp.exp(cache_scores - row_peak)
    tree_exp = jnp.exp(tree_scores - row_peak)
    denominator = (jnp.sum(cache_exp, axis=-1) + jnp.sum(tree_exp, axis=-1))[..., None]
    cache_weights = (cache_exp / denominator).astype(jnp.bfloat16)
    tree_weights = (tree_exp / denominator).astype(jnp.bfloat16)
    context = jnp.einsum(
        "rgtql,rlgd->rtgqd", cache_weights, cached_value_rows, preferred_element_type=jnp.float32
    ) + jnp.einsum(
        "rgtqu,rugd->rtgqd", tree_weights, tree_value_rows, preferred_element_type=jnp.float32
    )
    return context.reshape(request_total * TREE_NODES, QUERY_HEADS * HEAD_SIZE)


VMEM_LIMIT = 66_000_000


def greet(n, me):
    barrier = pltpu.get_barrier_semaphore()

    def hello(k, carry):
        pl.semaphore_signal(barrier, inc=1, device_id={"expert": lax.rem(me + k, n)})
        return carry

    lax.fori_loop(1, n, hello, 0)
    pl.semaphore_wait(barrier, n - 1)


def push(src, dst, send_sem, recv_sem, peer):
    return pltpu.make_async_remote_copy(
        src_ref=src,
        dst_ref=dst,
        send_sem=send_sem,
        recv_sem=recv_sem,
        device_id={"expert": peer},
        device_id_type=pl.DeviceIdType.MESH,
    )


def moe_kernel(
    n,
    group_size,
    pair_slots,
    down_slots,
    packed,
    gate_hbm,
    up_hbm,
    down_hbm,
    grouped,
    gate_buf,
    up_buf,
    down_buf,
    arrived,
    rows_wide,
    rows,
    activation,
    result,
    leaving,
    returned,
    pair_sem,
    down_sem,
    out_sem,
    in_sem,
    back_out_sem,
    back_in_sem,
    own_sem,
):
    me = lax.axis_index("expert")
    width = gate_hbm.shape[1]
    chunk = gate_buf.shape[2]
    pair_count = width // chunk
    piece = down_buf.shape[2]
    piece_count = down_hbm.shape[1] // piece

    def pair_copies(i):
        slot = lax.rem(i, pair_slots)
        cols = pl.ds(pl.multiple_of(i * chunk, chunk), chunk)
        return (
            pltpu.make_async_copy(gate_hbm.at[:, cols], gate_buf.at[slot], pair_sem.at[0, slot]),
            pltpu.make_async_copy(up_hbm.at[:, cols], up_buf.at[slot], pair_sem.at[1, slot]),
        )

    def down_copy(i):
        slot = lax.rem(i, down_slots)
        cols = pl.ds(pl.multiple_of(i * piece, piece), piece)
        return pltpu.make_async_copy(down_hbm.at[:, cols], down_buf.at[slot], down_sem.at[slot])

    def start_pair(i, carry):
        for copy in pair_copies(i):
            copy.start()
        return carry

    def start_down(i, carry):
        down_copy(i).start()
        return carry

    lax.fori_loop(0, pair_slots, start_pair, 0)
    greet(n, me)

    def dispatch(k, carry):
        peer = lax.rem(me + k, n)
        push(
            packed.at[peer // group_size], arrived.at[me], out_sem.at[peer], in_sem.at[me], peer
        ).start()
        return carry

    lax.fori_loop(1, n, dispatch, 0)
    own = pltpu.make_async_copy(packed.at[me // group_size], arrived.at[me], own_sem)
    own.start()
    lax.fori_loop(0, down_slots, start_down, 0)
    own.wait()

    def take(k, carry):
        source = lax.rem(me + n - k, n)
        push(
            packed.at[0], arrived.at[source], out_sem.at[source], in_sem.at[source], source
        ).wait_recv()
        return carry

    lax.fori_loop(1, n, take, 0)

    def both(pair):
        return pl.ds(pl.multiple_of(pair * 2 * CAP, 2 * CAP), 2 * CAP)

    def widen(pair, carry):
        rows_wide[both(pair), :] = jnp.concatenate(
            [arrived[2 * pair].astype(jnp.float32), arrived[2 * pair + 1].astype(jnp.float32)],
            axis=0,
        )
        return carry

    lax.fori_loop(0, n // 2, widen, 0)
    rows[...] = rows_wide[...].astype(jnp.bfloat16)

    def pair_step(i, carry):
        slot = lax.rem(i, pair_slots)
        for copy in pair_copies(i):
            copy.wait()
        gate_val = jnp.dot(rows[...], gate_buf[slot], preferred_element_type=jnp.float32)
        up_val = jnp.dot(rows[...], up_buf[slot], preferred_element_type=jnp.float32)
        cols = pl.ds(pl.multiple_of(i * chunk, chunk), chunk)
        activation[:, cols] = (jax.nn.silu(gate_val) * up_val).astype(jnp.bfloat16)

        @pl.when(i + pair_slots < pair_count)
        def _():
            start_pair(i + pair_slots, 0)

        return carry

    lax.fori_loop(0, pair_count, pair_step, 0)

    def down_step(i, carry):
        slot = lax.rem(i, down_slots)
        down_copy(i).wait()
        result[...] = jnp.dot(
            activation[...], down_buf[slot], preferred_element_type=jnp.float32
        )

        @pl.when(i + down_slots < piece_count)
        def _():
            start_down(i + down_slots, 0)

        def narrow(pair, inner):
            block = result[both(pair), :]
            leaving[2 * pair, i] = block[:CAP].astype(jnp.bfloat16)
            leaving[2 * pair + 1, i] = block[CAP:].astype(jnp.bfloat16)
            return inner

        lax.fori_loop(0, n // 2, narrow, 0)

        def send_back(k, inner):
            peer = lax.rem(me + k, n)
            push(
                leaving.at[peer, i],
                returned.at[me, i],
                back_out_sem.at[peer],
                back_in_sem.at[me],
                peer,
            ).start()
            return inner

        lax.fori_loop(1, n, send_back, 0)
        return carry

    lax.fori_loop(0, piece_count, down_step, 0)
    returned[me] = leaving[me]

    def drain(k, carry):
        peer = lax.rem(me + n - k, n)
        push(
            leaving.at[peer], returned.at[peer], back_out_sem.at[peer], back_in_sem.at[peer], peer
        ).wait()
        push(
            packed.at[0], arrived.at[peer], out_sem.at[peer], in_sem.at[peer], peer
        ).wait_send()
        return carry

    lax.fori_loop(1, n, drain, 0)

    def gather(expert, carry):
        for i in range(piece_count):

            def add(member, total):
                return total + returned[expert * group_size + member, i].astype(jnp.float32)

            grouped[expert, :, i * piece : (i + 1) * piece] = lax.fori_loop(
                0, group_size, add, jnp.zeros((CAP, piece), jnp.float32)
            )
        return carry

    lax.fori_loop(0, EXPERTS, gather, 0)


def moe(packed, gate_weight, up_weight, down_weight, n):
    model_width, width = gate_weight.shape
    row_count = n * CAP
    chunk = min(512, width)
    piece = model_width // 4
    pair_slots = min(3, width // chunk)
    down_slots = min(2, model_width // piece)
    anywhere = pl.BlockSpec(memory_space=pl.ANY)
    whole = pl.BlockSpec(memory_space=pltpu.VMEM)
    bf16, f32 = jnp.bfloat16, jnp.float32
    return pl.pallas_call(
        functools.partial(moe_kernel, n, n // EXPERTS, pair_slots, down_slots),
        out_shape=jax.ShapeDtypeStruct((EXPERTS, CAP, model_width), f32),
        in_specs=[whole, anywhere, anywhere, anywhere],
        out_specs=whole,
        scratch_shapes=[
            pltpu.VMEM((pair_slots, model_width, chunk), bf16),
            pltpu.VMEM((pair_slots, model_width, chunk), bf16),
            pltpu.VMEM((down_slots, width, piece), bf16),
            pltpu.VMEM((n, CAP, model_width), bf16),
            pltpu.VMEM((row_count, model_width), f32),
            pltpu.VMEM((row_count, model_width), bf16),
            pltpu.VMEM((row_count, width), bf16),
            pltpu.VMEM((row_count, piece), f32),
            pltpu.VMEM((n, model_width // piece, CAP, piece), bf16),
            pltpu.VMEM((n, model_width // piece, CAP, piece), bf16),
            pltpu.SemaphoreType.DMA((2, pair_slots)),
            pltpu.SemaphoreType.DMA((down_slots,)),
            pltpu.SemaphoreType.DMA((n,)),
            pltpu.SemaphoreType.DMA((n,)),
            pltpu.SemaphoreType.DMA((n,)),
            pltpu.SemaphoreType.DMA((n,)),
            pltpu.SemaphoreType.DMA,
        ],
        compiler_params=pltpu.CompilerParams(
            collective_id=0, has_side_effects=True, vmem_limit_bytes=VMEM_LIMIT
        ),
        name="moe",
    )(packed, gate_weight, up_weight, down_weight)


def draft_kernel(
    n,
    share,
    piece,
    blocks,
    fc_hbm,
    out,
    fc_buf,
    arrived,
    rows_wide,
    result,
    leaving,
    returned,
    fc_sem,
    out_sem,
    in_sem,
    back_out_sem,
    back_in_sem,
):
    me = lax.axis_index("expert")
    piece_count = fc_hbm.shape[1] // piece
    half = piece // 2

    def fc_copy(i):
        cols = pl.ds(pl.multiple_of(i * piece, piece), piece)
        return pltpu.make_async_copy(fc_hbm.at[:, cols], fc_buf.at[i], fc_sem.at[i])

    def start_fc(i, carry):
        fc_copy(i).start()
        return carry

    lax.fori_loop(0, piece_count, start_fc, 0)
    greet(n, me)

    def dispatch(k, carry):
        peer = lax.rem(me + k, n)
        push(blocks.at[peer], arrived.at[me], out_sem.at[peer], in_sem.at[me], peer).start()
        return carry

    lax.fori_loop(1, n, dispatch, 0)
    rows_wide[pl.ds(me * share, share), :] = blocks[me]

    def take(k, carry):
        source = lax.rem(me + n - k, n)
        push(
            blocks.at[source], arrived.at[source], out_sem.at[source], in_sem.at[source], source
        ).wait()
        rows_wide[pl.ds(source * share, share), :] = arrived[source]
        return carry

    lax.fori_loop(1, n, take, 0)

    def step(i, carry):
        fc_copy(i).wait()
        result[...] = jnp.dot(
            rows_wide[...].astype(jnp.bfloat16), fc_buf[i], preferred_element_type=jnp.float32
        )

        def split(source, inner):
            block = result[pl.ds(source * share, share), :]
            leaving[source, i] = jnp.concatenate(
                [block[:, :half], block[:, half:]], axis=0
            ).astype(jnp.bfloat16)
            return inner

        lax.fori_loop(0, n, split, 0)

        def send_back(k, inner):
            peer = lax.rem(me + k, n)
            push(
                leaving.at[peer, i],
                returned.at[me, i],
                back_out_sem.at[peer],
                back_in_sem.at[me],
                peer,
            ).start()
            return inner

        lax.fori_loop(1, n, send_back, 0)
        return carry

    lax.fori_loop(0, piece_count, step, 0)
    returned[me] = leaving[me]

    def drain(k, carry):
        peer = lax.rem(me + n - k, n)
        push(
            leaving.at[peer], returned.at[peer], back_out_sem.at[peer], back_in_sem.at[peer], peer
        ).wait()
        return carry

    lax.fori_loop(1, n, drain, 0)
    for i in range(piece_count):

        def add(source, total):
            return total + returned[source, i].astype(jnp.float32)

        total = lax.fori_loop(0, n, add, jnp.zeros((2 * share, half), jnp.float32))
        out[:, i * piece : i * piece + half] = total[:share]
        out[:, i * piece + half : (i + 1) * piece] = total[share:]


def draft(blocks, draft_fc):
    n, share, depth = blocks.shape
    model_width = draft_fc.shape[1]
    piece = model_width // 4
    pieces = model_width // piece
    whole = pl.BlockSpec(memory_space=pltpu.VMEM)
    f32 = jnp.float32
    return pl.pallas_call(
        functools.partial(draft_kernel, n, share, piece),
        out_shape=jax.ShapeDtypeStruct((share, model_width), f32),
        in_specs=[whole, pl.BlockSpec(memory_space=pl.ANY)],
        out_specs=whole,
        scratch_shapes=[
            pltpu.VMEM((pieces, depth, piece), jnp.bfloat16),
            pltpu.VMEM((n, share, depth), f32),
            pltpu.VMEM((n * share, depth), f32),
            pltpu.VMEM((n * share, piece), f32),
            pltpu.VMEM((n, pieces, 2 * share, piece // 2), jnp.bfloat16),
            pltpu.VMEM((n, pieces, 2 * share, piece // 2), jnp.bfloat16),
            pltpu.SemaphoreType.DMA((pieces,)),
            pltpu.SemaphoreType.DMA((n,)),
            pltpu.SemaphoreType.DMA((n,)),
            pltpu.SemaphoreType.DMA((n,)),
            pltpu.SemaphoreType.DMA((n,)),
        ],
        compiler_params=pltpu.CompilerParams(
            collective_id=1, has_side_effects=True, vmem_limit_bytes=VMEM_LIMIT
        ),
        name="draft",
    )(blocks, draft_fc)


SLICE = 1024
LANES = 128
UNIT = 256


def greet_near(group, mine, lane):
    barrier = pltpu.get_barrier_semaphore()
    for step in range(1, EXPERTS):
        peer = lax.rem(mine + step, EXPERTS) * group + lane
        pl.semaphore_signal(barrier, inc=1, device_id={"expert": peer})
    for step in range(1, group):
        peer = mine * group + lax.rem(lane + step, group)
        pl.semaphore_signal(barrier, inc=1, device_id={"expert": peer})
    return barrier


def fused_kernel(
    n,
    slots,
    lengths_hbm,
    parents_hbm,
    routes_hbm,
    accepted_hbm,
    queries_hbm,
    tree_hbm,
    cache_hbm,
    residual_hbm,
    gain_hbm,
    router_hbm,
    embed_hbm,
    gate_hbm,
    up_hbm,
    down_hbm,
    fc_hbm,
    layer_out,
    draft_out,
    lengths,
    parents,
    routes,
    accepted,
    weights,
    queries,
    tree,
    keys,
    values,
    residual,
    gain,
    router,
    embed,
    tree_rows,
    hidden,
    normed,
    packed,
    arrived,
    rows,
    gate_sum,
    up_sum,
    activation,
    leaving,
    returned,
    chip_sum,
    chip_leaving,
    chip_returned,
    home_leaving,
    home_returned,
    pick_rows,
    pick_arrived,
    shares,
    share_leaving,
    late_shares,
    late_leaving,
    share_rows,
    hidden_row,
    embed_row,
    blocks,
    block_rows,
    draft_sum,
    draft_wide,
    pair_leaving,
    pair_returned,
    draft_leaving,
    draft_returned,
    load_sem,
    input_sem,
    out_sem,
    in_sem,
    plane_out_sem,
    plane_in_sem,
    core_out_sem,
    core_in_sem,
    chip_out_sem,
    chip_in_sem,
    home_out_sem,
    home_in_sem,
    pick_out_sem,
    pick_in_sem,
    share_out_sem,
    late_out_sem,
    share_in_sem,
    block_out_sem,
    block_in_sem,
    pair_out_sem,
    pair_in_sem,
    draft_out_sem,
    draft_in_sem,
):
    bf16, f32 = jnp.bfloat16, jnp.float32
    me = lax.axis_index("expert")
    group = n // EXPERTS
    mine = me // group
    lane = lax.rem(me, group)
    core = lax.rem(lane, 2)
    across = lane // 2
    core_peer = mine * group + across * 2 + (1 - core)
    chip_peer = mine * group + (1 - across) * 2 + core
    model_width = down_hbm.shape[1]
    width = down_hbm.shape[0]
    depth = fc_hbm.shape[0]
    slice_count = model_width // SLICE
    half_count = width // SLICE
    half = SLICE // 2
    chunks = [(0, UNIT), (UNIT, SLICE - UNIT)] + [(k * SLICE, SLICE) for k in range(1, slice_count)]
    last = model_width - SLICE
    pieces = [(k * SLICE, SLICE) for k in range(slice_count - 1)]
    pieces += [(last, SLICE - UNIT), (model_width - UNIT, UNIT)]
    piece_count = len(pieces)
    unit_count = depth // UNIT
    block_count = model_width // depth
    late_block = block_count // 2
    late_unit = late_block * unit_count
    padded = 8
    share = EXPERTS * CAP
    cache_slots = cache_hbm.shape[2]
    key_rows = keys.shape[0]
    line_count = model_width // LANES
    lines = SLICE // LANES
    part_count = draft_leaving.shape[0]
    each = line_count // part_count

    pairs = [
        ("pair", k, h, i) for k in range(slice_count) for h in range(half_count) for i in range(2)
    ]
    downs = [("down", p, a) for p in range(piece_count) for a in range(half_count)]
    order = pairs + downs + [("fc", p) for p in range(slice_count)]
    place = {item: i for i, item in enumerate(order)}
    sem_count = load_sem.shape[0]

    def load_group(item):
        if item[0] == "pair":
            return item[1]
        if item[0] == "down":
            return slice_count + item[1]
        return slice_count + piece_count

    def wait_loads(item):
        if item[0] == "pair":
            view = weights.at[0 : 2 * half_count]
        elif item[0] == "down":
            view = weights.at[0:half_count, :, 0 : pieces[item[1]][1]]
        else:
            view = weights.at[0:slice_count, 0:depth, :]
        pltpu.make_async_copy(view, view, load_sem.at[load_group(item) % sem_count]).wait()

    def load_copy(item):
        i = place[item]
        slot = weights.at[i % slots]
        if item[0] == "pair":
            k, h = item[1], item[2]
            source = (gate_hbm, up_hbm)[item[3]]
            view = source.at[k * SLICE : (k + 1) * SLICE, h * SLICE : (h + 1) * SLICE]
        elif item[0] == "down":
            a = item[2]
            start, size = pieces[item[1]]
            view = down_hbm.at[a * SLICE : (a + 1) * SLICE, start : start + size]
            slot = weights.at[i % slots, :, 0:size]
        else:
            p = item[1]
            view = fc_hbm.at[:, p * SLICE : (p + 1) * SLICE]
            slot = weights.at[i % slots, 0:depth, :]
        return pltpu.make_async_copy(view, slot, load_sem.at[load_group(item) % sem_count])

    def start_load(i):
        if i < len(order):
            load_copy(order[i]).start()

    inputs = [
        pltpu.make_async_copy(source, target, input_sem.at[i])
        for i, (source, target) in enumerate(
            [
                (queries_hbm, queries),
                (tree_hbm, tree),
                (cache_hbm.at[0, 0], keys.at[0:cache_slots, :]),
                (residual_hbm, residual),
                (cache_hbm.at[0, 1], values.at[0:cache_slots, :]),
                (gain_hbm, gain),
                (router_hbm, router),
                (embed_hbm, embed),
                (lengths_hbm, lengths),
                (parents_hbm, parents),
                (routes_hbm, routes),
                (accepted_hbm, accepted),
            ]
        )
    ]
    for copy in inputs[8:] + inputs[:8]:
        copy.start()
    barrier = greet_near(group, mine, lane)
    for copy in inputs[8:]:
        copy.wait()

    row8 = lax.broadcasted_iota(jnp.int32, (padded, LANES), 0)
    col8 = lax.broadcasted_iota(jnp.int32, (padded, LANES), 1)
    node_ids = lax.broadcasted_iota(jnp.int32, (1, LANES), 1)
    reached = []
    related = jnp.zeros((padded, LANES), f32)
    for node in range(TREE_NODES):
        row = (node_ids == node).astype(f32)
        parent = parents[node]
        for earlier in range(node):
            row = row + jnp.where(parent == earlier, reached[earlier], 0.0)
        reached.append(row)
        related = related + jnp.where(row8 == node, row, 0.0)
    slot_ids = lax.broadcasted_iota(jnp.int32, (padded, cache_slots), 1)
    bias = jnp.concatenate(
        [
            jnp.where(slot_ids < lengths[0, 0], 0.0, -1e30),
            jnp.where(related > 0.5, 0.0, -1e30),
        ],
        axis=1,
    )
    heads_each = QUERY_HEADS // KEY_VALUE_HEADS
    bias = jnp.concatenate([bias] * heads_each, axis=0)

    def named(choice, token):
        expert = routes[choice, token]
        rank = jnp.int32(0)
        for earlier in range(token):
            for other in range(2):
                rank = rank + jnp.where(routes[other, earlier] == expert, 1, 0)
        return expert, rank

    places = [[named(choice, token) for choice in range(2)] for token in range(TREE_NODES)]

    for copy in inputs[:3]:
        copy.wait()
    for i in range(slots):
        start_load(i)
    tree_rows[...] = jnp.zeros_like(tree_rows)
    for token in range(TREE_NODES):
        both = tree[token].astype(f32)
        tree_rows[0, token : token + 1, :] = both[0:1]
        tree_rows[1, token : token + 1, :] = both[1:2]
    tile = tree_rows.shape[1]
    blank = jnp.zeros((key_rows - cache_slots - tile, keys.shape[1]), bf16)
    keys[cache_slots : cache_slots + tile, :] = tree_rows[0].astype(bf16)
    keys[cache_slots + tile :, :] = blank
    values[cache_slots : cache_slots + tile, :] = tree_rows[1].astype(bf16)
    values[cache_slots + tile :, :] = blank
    spare = jnp.zeros((padded - TREE_NODES, HEAD_SIZE), f32)
    score_scale = HEAD_SIZE ** (-0.5)
    weights_of = []
    for g in range(KEY_VALUE_HEADS):
        parts = []
        for q in range(heads_each):
            head = g * heads_each + q
            parts.append(queries[:, head * HEAD_SIZE : (head + 1) * HEAD_SIZE].astype(f32))
            parts.append(spare)
        head_queries = jnp.concatenate(parts, axis=0).astype(bf16)
        scores = (
            lax.dot_general(
                head_queries,
                keys[:, g * HEAD_SIZE : (g + 1) * HEAD_SIZE],
                (((1,), (1,)), ((), ())),
                preferred_element_type=f32,
            )
            * score_scale
            + bias
        )
        peak = jnp.max(scores, axis=-1, keepdims=True)
        grown = jnp.exp(scores - peak)
        total = jnp.sum(grown, axis=-1, keepdims=True)
        weights_of.append((grown * (1.0 / total)).astype(bf16))
    for copy in inputs[3:5]:
        copy.wait()
    square = jnp.zeros((padded, HEAD_SIZE), f32)
    for g in range(KEY_VALUE_HEADS):
        context = jnp.dot(
            weights_of[g],
            values[:, g * HEAD_SIZE : (g + 1) * HEAD_SIZE],
            preferred_element_type=f32,
        )
        for q in range(heads_each):
            head = g * heads_each + q
            cols = slice(head * HEAD_SIZE, (head + 1) * HEAD_SIZE)
            state = context[q * padded : (q + 1) * padded] + jnp.concatenate(
                [residual[:, cols].astype(f32), spare], axis=0
            )
            hidden[:, cols] = state
            square = square + state * state
    for copy in inputs[5:8]:
        copy.wait()
    level = lax.rsqrt(jnp.sum(square, axis=-1, keepdims=True) / model_width + EPSILON)

    slot_row = lax.broadcasted_iota(jnp.int32, (EXPERTS * padded, padded), 0)
    slot_col = lax.broadcasted_iota(jnp.int32, (EXPERTS * padded, padded), 1)
    placing = jnp.zeros((EXPERTS * padded, padded), f32)
    for token, choices in enumerate(places):
        for expert, rank in choices:
            placing = placing + jnp.where(
                (slot_row == expert * padded + rank) & (slot_col == token), 1.0, 0.0
            )
    placing = placing.astype(bf16)

    def to_plane(c, step):
        plane = lax.rem(mine + step, EXPERTS)
        cols = pl.ds(chunks[c][0], chunks[c][1])
        return push(
            packed.at[plane, :, cols],
            arrived.at[mine, :, cols],
            out_sem,
            in_sem.at[c],
            plane * group + lane,
        )

    def awaited(ref, sem):
        return push(ref, ref, sem, sem, core_peer)

    def pack_step(c):
        start, size = chunks[c]
        cols = slice(start, start + size)
        gains = [
            gain[t : t + 1, :].astype(f32)
            for t in range(start // LANES, (start + size) // LANES)
        ]
        normal = (hidden[:, cols] * level * jnp.concatenate(gains, axis=1)).astype(bf16)
        normed[:, cols] = normal
        spread = jnp.dot(placing, normal, preferred_element_type=f32)
        for e in range(EXPERTS):
            packed[e, :, cols] = spread[e * padded : e * padded + CAP].astype(bf16)
        arrived[mine, :, cols] = packed[mine, :, cols]

    pack_step(0)
    pl.semaphore_wait(barrier, EXPERTS + group - 2)
    for c in range(len(chunks)):
        if c > 0:
            pack_step(c)
        for step in range(1, EXPERTS):
            to_plane(c, step).start()

    token_row = row8[:, 0:1]
    embed_row[...] = embed[...].astype(f32)
    for k in range(slice_count):
        cols = slice(k * SLICE, (k + 1) * SLICE)
        hidden_row[:, cols] = jnp.sum(
            jnp.where(token_row == accepted[0, 0], hidden[:, cols], 0.0), axis=0, keepdims=True
        )

    def block_push(row, b, j):
        source = row.at[:, b * depth : (b + 1) * depth]
        return push(source, blocks.at[me], block_out_sem, block_in_sem, j)

    def send_block(row, b, j):
        @pl.when(me != j)
        def _():
            block_push(row, b, j).start()

        @pl.when(me == j)
        def _():
            blocks[j] = row[:, b * depth : (b + 1) * depth]

    logits = [jnp.zeros((padded, 1), f32) for _ in range(EXPERTS)]
    for k in range(slice_count):
        cols = slice(k * SLICE, (k + 1) * SLICE)
        normal = normed[:, cols].astype(f32)
        for e in range(EXPERTS):
            logits[e] = logits[e] + jnp.sum(
                normal * router[e : e + 1, cols].astype(f32), axis=-1, keepdims=True
            )
    ids = [jnp.full((padded, 1), -1, jnp.int32) for _ in range(4)]
    for token, choices in enumerate(places):
        for choice, (expert, rank) in enumerate(choices):
            ids[choice] = jnp.where(token_row == token, expert, ids[choice])
            ids[2 + choice] = jnp.where(token_row == token, expert * CAP + rank, ids[2 + choice])
    first_logit = jnp.zeros((padded, 1), f32)
    second_logit = jnp.zeros((padded, 1), f32)
    for e in range(EXPERTS):
        first_logit = first_logit + jnp.where(ids[0] == e, logits[e], 0.0)
        second_logit = second_logit + jnp.where(ids[1] == e, logits[e], 0.0)
    first_share = jax.nn.sigmoid(first_logit - second_logit)
    share_col = col8[:, :share]
    weighted = jnp.where(share_col == ids[2], first_share, 0.0) + jnp.where(
        share_col == ids[3], 1.0 - first_share, 0.0
    )

    def split(exact):
        high = exact.astype(bf16).astype(f32)
        middle = (exact - high).astype(bf16).astype(f32)
        low = exact - high - middle
        return jnp.concatenate([high, middle, low], axis=0).astype(bf16)

    mixers = split(weighted)

    def pick_push(step, turn):
        plane = lax.rem(mine + step, EXPERTS)
        column = lax.rem(across + turn, 2)
        return push(
            pick_rows.at[plane],
            pick_arrived.at[across * EXPERTS + mine],
            pick_out_sem,
            pick_in_sem,
            plane * group + column * 2 + core,
        )

    for e in range(EXPERTS):
        chosen = jnp.zeros((padded, LANES), f32)
        for expert, position, portion in (
            (ids[0], ids[2], first_share),
            (ids[1], ids[3], 1.0 - first_share),
        ):
            here = (col8 == mine * CAP + position - expert * CAP) & (expert == e)
            chosen = chosen + jnp.where(here, portion, 0.0)
        pick_rows[e] = jnp.sum(
            jnp.where(token_row == accepted[0, 0], chosen, 0.0), axis=0, keepdims=True
        )
    def send_early():
        for step in range(EXPERTS):
            for turn in range(2):
                if step + turn > 0:
                    pick_push(step, turn).start()
        for b in range(block_count):
            send_block(embed_row, b, block_count + b)
            send_block(hidden_row, b, b)

    pick_arrived[across * EXPERTS + mine] = pick_rows[mine]

    def row_push(c, which, sem, peer):
        start, size = chunks[c]
        block = rows.at[pl.ds(pl.multiple_of(which * share, share), share), pl.ds(start, size)]
        return push(block, block, plane_out_sem, plane_in_sem.at[c, sem], peer)

    chip_lane = (1 - across) * 2 + core

    def gather_step(k):
        start, size = chunks[k]
        cols = slice(start, start + size)
        awaited(arrived.at[0 : EXPERTS - 1, :, pl.ds(start, size)], in_sem.at[k]).wait_recv()
        rows[pl.ds(pl.multiple_of(lane * share, share), share), cols] = jnp.concatenate(
            [arrived[s, :, cols].astype(f32) for s in range(EXPERTS)], axis=0
        ).astype(bf16)
        row_push(k, lane, 0, chip_peer).start()
        row_push(k, lane, 1, core_peer).start()

    def forward_step(k):
        row_push(k, chip_lane, 0, chip_peer).wait_recv()
        row_push(k, chip_lane, 1, core_peer).start()

    def expert_step(c):
        start, size = chunks[c]
        pair_rows = rows.at[0 : 2 * share, pl.ds(start, size)]
        awaited(pair_rows, plane_in_sem.at[c, 1]).wait_recv()
        k, first = start // SLICE, start % SLICE
        final = start + size == model_width
        if first == 0:
            wait_loads(("pair", k))
        for h in range(half_count):
            cols = slice(h * SLICE, (h + 1) * SLICE)
            sums = []
            for i, total in ((0, gate_sum), (1, up_sum)):
                item = ("pair", k, h, i)
                value = jnp.dot(
                    rows[:, start : start + size],
                    weights[place[item] % slots, first : first + size, :],
                    preferred_element_type=f32,
                )
                if start > 0:
                    value = value + total[:, cols]
                if not final:
                    total[:, cols] = value
                sums.append(value)
                if first + size == SLICE:
                    start_load(place[item] + slots)
            if final:
                activation[h] = (jax.nn.silu(sums[0]) * sums[1]).astype(bf16)

    for t in range(len(chunks) + 3):
        if t < len(chunks):
            gather_step(t)
        if t == 2:
            send_early()
        if 0 <= t - 2 < len(chunks):
            forward_step(t - 2)
        if 0 <= t - 3 < len(chunks):
            expert_step(t - 3)

    def piece_cols(p):
        return pl.ds(pieces[p][0], pieces[p][1])

    def core_push(p):
        cols = piece_cols(p)
        return push(
            leaving.at[1 - core, :, :, cols],
            returned.at[:, :, cols],
            core_out_sem,
            core_in_sem.at[p],
            core_peer,
        )

    def chip_push(p):
        cols = piece_cols(p)
        return push(
            chip_leaving.at[:, cols],
            chip_returned.at[:, cols],
            chip_out_sem,
            chip_in_sem.at[p],
            chip_peer,
        )

    def to_home(p, step):
        plane = lax.rem(mine + step, EXPERTS)
        return push(
            home_leaving.at[plane, :, piece_cols(p)],
            home_returned.at[mine, :, piece_cols(p)],
            home_out_sem,
            home_in_sem,
            plane * group + lane,
        )

    def partial_step(p):
        start, size = pieces[p]
        cols = slice(start, start + size)
        partial = None
        wait_loads(("down", p))
        for a in range(half_count):
            item = ("down", p, a)
            value = jnp.dot(
                activation[a], weights[place[item] % slots, :, 0:size], preferred_element_type=f32
            )
            partial = value if partial is None else partial + value
            start_load(place[item] + slots)
        for member in range(group):
            block = partial[member * share : (member + 1) * share].astype(bf16)
            leaving[member % 2, member // 2, :, cols] = block

        core_push(p).start()

    def core_step(p):
        core_push(p).wait_recv()
        start, size = pieces[p]
        cols = slice(start, start + size)
        far = 1 - across
        chip_leaving[:, cols] = (
            leaving[core, far, :, cols].astype(f32) + returned[far, :, cols].astype(f32)
        ).astype(bf16)
        chip_push(p).start()
        chip_sum[:, cols] = leaving[core, across, :, cols].astype(f32) + returned[across, :, cols].astype(
            f32
        )
        if start < late_unit * UNIT:
            return
        portions = [
            portion_of(
                both_mixers[column],
                leaving[core, column, :, cols].astype(f32) + returned[column, :, cols].astype(f32),
            )
            for column in range(2)
        ]
        send_shares(start, size, jnp.concatenate(portions, axis=0))

    def portion_of(pick_mixers, total):
        mixed = jnp.dot(pick_mixers, total.astype(bf16), preferred_element_type=f32)
        portion = mixed[:padded] + mixed[padded : 2 * padded] + mixed[2 * padded :]
        return portion[:EXPERTS]

    def send_shares(start, size, portion):
        for unit in range(start // UNIT, (start + size) // UNIT):
            b, part = unit // unit_count, unit % unit_count
            first = unit * UNIT - start
            value = portion[:, first : first + UNIT].astype(bf16)
            if unit < late_unit:
                source, target, sem = share_leaving.at[unit], shares, share_out_sem
            else:
                source, target, sem = late_leaving.at[unit - late_unit], late_shares, late_out_sem

            source[...] = value

            @pl.when(me != b)
            def _():
                push(
                    source,
                    target.at[part, me],
                    sem,
                    share_in_sem.at[part // (unit_count - 1)],
                    b,
                ).start()

            @pl.when(me == b)
            def _():
                target[part, b] = value

    held_back = 3

    def leave_step(p):
        for step in range(1, EXPERTS):
            to_home(p, step).start()

    def chip_step(p):
        start, size = pieces[p]
        cols = slice(start, start + size)
        chip_push(p).wait_recv()
        total = chip_sum[:, cols] + chip_returned[:, cols].astype(f32)
        if start < late_unit * UNIT:
            send_shares(start, size, portion_of(own_mixers, total))
        for s in range(EXPERTS):
            home_leaving[s, :, cols] = total[s * CAP : (s + 1) * CAP].astype(bf16)
        home_returned[mine, :, cols] = home_leaving[mine, :, cols]
        if p >= held_back:
            leave_step(p)

    def home_step(p):
        start, size = pieces[p]
        cols = slice(start, start + size)
        block = jnp.concatenate(
            [home_returned[e, :, cols].astype(f32) for e in range(EXPERTS)], axis=0
        ).astype(bf16)
        mixed = jnp.dot(mixers, block, preferred_element_type=f32)
        expert_sum = mixed[:padded] + mixed[padded : 2 * padded] + mixed[2 * padded :]
        result = (hidden[:, cols] + expert_sum).astype(bf16)
        layer_out[:, cols] = result[:TREE_NODES]

    pair_rows_count = n // 2
    own_place = across * EXPERTS + mine

    def pair_push(q):
        return push(
            pair_leaving.at[q], pair_returned.at[q], pair_out_sem, pair_in_sem.at[q], core_peer
        )

    def draft_push(q, row):
        peer = lax.rem(row, EXPERTS) * group + row // EXPERTS * 2 + core
        return push(
            draft_leaving.at[q, row],
            draft_returned.at[q, me // 2],
            draft_out_sem,
            draft_in_sem,
            peer,
        )

    def row_of(device):
        column = lax.rem(device, group) // 2
        return lax.rem(device, 2) * pair_rows_count + column * EXPERTS + device // group

    def block_step():
        awaited(blocks.at[0 : n - 1], block_in_sem).wait_recv()

        def take(source, carry):
            block_rows[pl.ds(row_of(source), 1), :] = blocks[source]
            return carry

        lax.fori_loop(0, n, take, 0)
        share_rows[...] = jnp.zeros_like(share_rows)

    def share_step(first, past):
        sem = share_in_sem.at[first // (unit_count - 1)]

        @pl.when((me >= late_block) & (me < block_count))
        def _():
            awaited(late_shares.at[first:past, 0 : n - 1], sem).wait_recv()
            for part in range(first, past):
                totals = []
                for c in range(2):
                    total = late_shares[part, c].astype(f32)
                    for member in range(c + 2, n, 2):
                        total = total + late_shares[part, member].astype(f32)
                    totals.append(total)
                sums = [
                    totals[c][column * EXPERTS : (column + 1) * EXPERTS]
                    for c in range(2)
                    for column in range(2)
                ]
                share_rows[:, part * UNIT : (part + 1) * UNIT] = jnp.concatenate(sums, axis=0)

        @pl.when(me < late_block)
        def _():
            awaited(shares.at[first:past, 0 : n - 1], sem).wait_recv()
            for part in range(first, past):
                sums = []
                for member in (0, 2, 1, 3):
                    total = shares[part, member].astype(f32)
                    for e in range(1, EXPERTS):
                        total = total + shares[part, e * group + member].astype(f32)
                    sums.append(total)
                share_rows[:, part * UNIT : (part + 1) * UNIT] = jnp.concatenate(sums, axis=0)

    def draft_step(first, past, final):
        share_step(first, past)
        deep = slice(first * UNIT, past * UNIT)
        draft_rows = (block_rows[:, deep] + share_rows[:, deep]).astype(bf16)
        per_part = slice_count // part_count
        if first == 0:
            wait_loads(("fc",))
        for q in range(part_count):
            for p in range(q * per_part, (q + 1) * per_part):
                item = ("fc", p)
                partial = jnp.dot(
                    draft_rows, weights[place[item] % slots, deep, :], preferred_element_type=f32
                )
                cols = slice(p * SLICE, (p + 1) * SLICE)
                if first > 0:
                    partial = partial + draft_sum[:, cols]
                if not final:
                    draft_sum[:, cols] = partial
                    continue
                for t in range(lines):
                    draft_wide[pl.ds(p * lines + t, n, stride=line_count), :] = partial[
                        :, t * LANES : (t + 1) * LANES
                    ]
            if not final:
                continue
            for i in range(pair_rows_count):
                start = ((1 - core) * pair_rows_count + i) * line_count + q * each
                pair_leaving[q, i] = draft_wide[
                    pl.ds(pl.multiple_of(start, each), each), :
                ].astype(bf16)
            pair_push(q).start()

    def pair_step(q):
        pair_push(q).wait_recv()
        for i in range(pair_rows_count):
            start = (core * pair_rows_count + i) * line_count + q * each
            total = draft_wide[pl.ds(pl.multiple_of(start, each), each), :] + pair_returned[
                q, i
            ].astype(f32)
            draft_leaving[q, i] = total.astype(bf16)

        def send_partial(k, carry):
            draft_push(q, lax.rem(own_place + k, pair_rows_count)).start()
            return carry

        lax.fori_loop(1, pair_rows_count, send_partial, 0)
        draft_returned[q, me // 2] = draft_leaving[q, own_place]

    pick_total = pick_arrived.shape[0]
    awaited(pick_arrived.at[0 : pick_total - 1], pick_in_sem).wait_recv()

    def mixers_of(column):
        picks = [pick_arrived[column * EXPERTS + s][:, :share] for s in range(EXPERTS)]
        picks.append(jnp.zeros((padded - EXPERTS, share), f32))
        return split(jnp.concatenate(picks, axis=0))

    own_mixers = mixers_of(across)
    both_mixers = [mixers_of(column) for column in range(2)]

    for p in range(piece_count):
        partial_step(p)
        if p > 0:
            core_step(p - 1)
        if p >= 4:
            chip_step(p - 4)
    core_step(piece_count - 1)
    for p in range(held_back):
        leave_step(p)
    block_step()
    for p in range(piece_count - 4, piece_count):
        chip_step(p)
    draft_step(0, unit_count - 1, False)
    draft_step(unit_count - 1, unit_count, True)
    for q in range(part_count):
        pair_step(q)
    awaited(home_returned.at[0 : EXPERTS - 1], home_in_sem).wait_recv()
    for p in range(piece_count):
        home_step(p)

    awaited(packed.at[0 : EXPERTS - 1], out_sem).wait_send()
    awaited(rows.at[0 : 3 * share, :], plane_out_sem).wait_send()
    awaited(pick_arrived.at[0 : pick_total - 1], pick_out_sem).wait_send()
    awaited(leaving.at[0], core_out_sem).wait_send()
    awaited(chip_leaving, chip_out_sem).wait_send()
    awaited(home_leaving.at[0 : EXPERTS - 1], home_out_sem).wait_send()
    awaited(blocks.at[0 : n - 1], block_out_sem).wait_send()
    for low, past, buffer, sem in (
        (0, late_block, share_leaving, share_out_sem),
        (late_block, block_count, late_leaving, late_out_sem),
    ):
        total = buffer.shape[0]
        owner = (me >= low) & (me < past)

        @pl.when(owner)
        def _():
            awaited(buffer.at[0 : total - unit_count], sem).wait_send()

        @pl.when(jnp.logical_not(owner))
        def _():
            awaited(buffer, sem).wait_send()

    awaited(pair_leaving, pair_out_sem).wait_send()
    awaited(draft_leaving.at[:, 0 : pair_rows_count - 1], draft_out_sem).wait_send()
    awaited(draft_returned.at[:, 0 : pair_rows_count - 1], draft_in_sem).wait_recv()
    for q in range(part_count):
        total = draft_returned[q, 0].astype(f32)
        for source in range(1, pair_rows_count):
            total = total + draft_returned[q, source].astype(f32)
        draft_out[q * each : (q + 1) * each, :] = total


def finish_kernel(layer, draft_lines, layer_out, draft_out):
    layer_out[...] = layer[...]
    for t in range(draft_lines.shape[0]):
        draft_out[:, t * LANES : (t + 1) * LANES] = draft_lines[t : t + 1, :].astype(jnp.bfloat16)


def fused(
    queries,
    tree_key_value,
    key_value_cache,
    lengths,
    parents,
    residual,
    ffn_gain,
    router,
    routes,
    gate_weight,
    up_weight,
    down_weight,
    accepted,
    next_embed,
    draft_fc,
    n,
):
    width, model_width = down_weight.shape
    depth = draft_fc.shape[0]
    group = n // EXPERTS
    share = EXPERTS * CAP
    slots = 24
    slices = model_width // SLICE
    halves = width // SLICE
    parts = 3
    pieces = slices + 1
    chunks = slices + 1
    units = depth // UNIT
    line_count = model_width // LANES
    kv_width = tree_key_value.shape[2]
    key_rows = key_value_cache.shape[2] + LANES
    in_hbm = pl.BlockSpec(memory_space=pltpu.HBM)
    whole = pl.BlockSpec(memory_space=pltpu.VMEM)
    bf16, f32 = jnp.bfloat16, jnp.float32
    dma = pltpu.SemaphoreType.DMA
    pinned = pltpu.with_memory_space_constraint
    layer, draft_lines = pl.pallas_call(
        functools.partial(fused_kernel, n, slots),
        out_shape=(
            pltpu.VMEM((TREE_NODES, model_width), bf16),
            pltpu.VMEM((line_count, LANES), f32),
        ),
        in_specs=[in_hbm] * 15,
        out_specs=(whole, whole),
        scratch_shapes=[
            pltpu.SMEM((1, 1), jnp.int32),
            pltpu.SMEM(parents.shape, jnp.int32),
            pltpu.SMEM(routes.T.shape, jnp.int32),
            pltpu.SMEM((1, 1), jnp.int32),
            pltpu.VMEM((slots, SLICE, SLICE), bf16),
            pltpu.VMEM((TREE_NODES, model_width), bf16),
            pltpu.VMEM((TREE_NODES, 2, kv_width), bf16),
            pltpu.VMEM((key_rows, kv_width), bf16),
            pltpu.VMEM((key_rows, kv_width), bf16),
            pltpu.VMEM((TREE_NODES, model_width), bf16),
            pltpu.VMEM((line_count, LANES), bf16),
            pltpu.VMEM((EXPERTS, model_width), bf16),
            pltpu.VMEM((1, model_width), bf16),
            pltpu.VMEM((2, 16, kv_width), f32),
            pltpu.VMEM((8, model_width), f32),
            pltpu.VMEM((8, model_width), bf16),
            pltpu.VMEM((EXPERTS, CAP, model_width), bf16),
            pltpu.VMEM((EXPERTS, CAP, model_width), bf16),
            pltpu.VMEM((group * share, model_width), bf16),
            pltpu.VMEM((group * share, width), f32),
            pltpu.VMEM((group * share, width), f32),
            pltpu.VMEM((halves, group * share, SLICE), bf16),
            pltpu.VMEM((2, 2, share, model_width), bf16),
            pltpu.VMEM((2, share, model_width), bf16),
            pltpu.VMEM((share, model_width), f32),
            pltpu.VMEM((share, model_width), bf16),
            pltpu.VMEM((share, model_width), bf16),
            pltpu.VMEM((EXPERTS, CAP, model_width), bf16),
            pltpu.VMEM((EXPERTS, CAP, model_width), bf16),
            pltpu.VMEM((EXPERTS, 1, LANES), f32),
            pltpu.VMEM((2 * EXPERTS, 1, LANES), f32),
            pltpu.VMEM((units, n, EXPERTS, UNIT), bf16),
            pltpu.VMEM((model_width // UNIT // 2, EXPERTS, UNIT), bf16),
            pltpu.VMEM((units, n, 2 * EXPERTS, UNIT), bf16),
            pltpu.VMEM((model_width // UNIT // 2, 2 * EXPERTS, UNIT), bf16),
            pltpu.VMEM((n, depth), f32),
            pltpu.VMEM((1, model_width), f32),
            pltpu.VMEM((1, model_width), f32),
            pltpu.VMEM((n, 1, depth), f32),
            pltpu.VMEM((n, depth), f32),
            pltpu.VMEM((n, model_width), f32),
            pltpu.VMEM((n * line_count, LANES), f32),
            pltpu.VMEM((parts, n // 2, line_count // parts, LANES), bf16),
            pltpu.VMEM((parts, n // 2, line_count // parts, LANES), bf16),
            pltpu.VMEM((parts, n // 2, line_count // parts, LANES), bf16),
            pltpu.VMEM((parts, n // 2, line_count // parts, LANES), bf16),
            dma((10,)),
            dma((12,)),
            dma,
            dma((chunks,)),
            dma,
            dma((chunks, 2)),
            dma,
            dma((pieces,)),
            dma,
            dma((pieces,)),
            dma,
            dma,
            dma,
            dma,
            dma,
            dma,
            dma((2,)),
            dma,
            dma,
            dma,
            dma((parts,)),
            dma,
            dma,
        ],
        compiler_params=pltpu.CompilerParams(
            collective_id=0, has_side_effects=True, vmem_limit_bytes=62_000_000
        ),
        name="fused",
    )(
        lengths.reshape(1, 1),
        parents,
        routes.T,
        accepted.reshape(1, 1),
        queries,
        tree_key_value,
        key_value_cache,
        residual,
        ffn_gain.reshape(line_count, LANES),
        router.T,
        next_embed,
        gate_weight,
        up_weight,
        down_weight,
        draft_fc,
    )
    return pl.pallas_call(
        finish_kernel,
        out_shape=(
            jax.ShapeDtypeStruct((TREE_NODES, model_width), bf16),
            jax.ShapeDtypeStruct((1, model_width), bf16),
        ),
        in_specs=[whole, whole],
        out_specs=(whole, whole),
        name="finish",
    )(pinned(layer, pltpu.VMEM), pinned(draft_lines, pltpu.VMEM))


def fits(lengths, gate_weight, draft_fc, n):
    model_width, width = gate_weight.shape
    depth = draft_fc.shape[0]
    return (
        lengths.shape[0] == 1
        and n == 4 * EXPERTS
        and width == 2 * SLICE
        and model_width == 6 * SLICE
        and depth % UNIT == 0
        and depth > UNIT
        and depth <= SLICE
        and n * depth == 2 * model_width
        and model_width // depth * depth == model_width
        and model_width // depth // 2 * depth == 3 * SLICE
    )


def per_device(
    queries,
    tree_key_value,
    key_value_cache,
    lengths,
    parents,
    residual,
    ffn_gain,
    router,
    routes,
    gate_weight,
    up_weight,
    down_weight,
    accepted,
    next_embed,
    draft_fc,
):
    devices = lax.axis_size("expert")
    if fits(lengths, gate_weight, draft_fc, devices):
        return fused(
            queries,
            tree_key_value,
            key_value_cache,
            lengths,
            parents,
            residual,
            ffn_gain,
            router,
            routes,
            gate_weight,
            up_weight,
            down_weight,
            accepted,
            next_embed,
            draft_fc,
            devices,
        )
    context = attention(queries, tree_key_value, key_value_cache, lengths, parents)
    hidden_state = residual.astype(jnp.float32) + context
    normed = (
        hidden_state
        * lax.rsqrt(jnp.mean(hidden_state * hidden_state, axis=-1, keepdims=True) + EPSILON)
        * ffn_gain.astype(jnp.float32)
    ).astype(jnp.bfloat16)
    tokens_here, model_width = normed.shape
    logits = jnp.dot(normed, router, preferred_element_type=jnp.float32)
    expert_ids = jnp.arange(EXPERTS, dtype=jnp.int32)
    first_hit = (routes[:, 0:1] == expert_ids[None, :]).astype(jnp.float32)
    second_hit = (routes[:, 1:2] == expert_ids[None, :]).astype(jnp.float32)
    first_logit = jnp.sum(logits * first_hit, axis=-1)
    second_logit = jnp.sum(logits * second_hit, axis=-1)
    first_share = jax.nn.sigmoid(first_logit - second_logit)
    mixing = first_share[:, None] * first_hit + (1.0 - first_share)[:, None] * second_hit
    hit_table = first_hit + second_hit
    slot_rank = jnp.cumsum(hit_table, axis=0) - 1.0
    slot_ids = jnp.arange(CAP, dtype=jnp.float32)
    placing = hit_table.T[:, None, :] * (slot_rank.T[:, None, :] == slot_ids[None, :, None]).astype(
        jnp.float32
    )
    packed = jnp.einsum(
        "ect,td->ecd", placing.astype(jnp.bfloat16), normed, preferred_element_type=jnp.float32
    ).astype(jnp.bfloat16)
    grouped = moe(packed, gate_weight, up_weight, down_weight, devices)
    weighted = placing * mixing.T[:, None, :]
    expert_sum = jnp.einsum("ect,ecd->td", weighted, grouped, precision=lax.Precision.HIGHEST)
    layer_out = (hidden_state + expert_sum).astype(jnp.bfloat16)
    request_total = lengths.shape[0]
    picker = (accepted[:, None] == jnp.arange(TREE_NODES, dtype=jnp.int32)[None, :]).astype(
        jnp.bfloat16
    )
    picked = jnp.einsum(
        "rt,rtd->rd",
        picker,
        layer_out.reshape(request_total, TREE_NODES, model_width),
        preferred_element_type=jnp.float32,
    ).astype(jnp.bfloat16)
    draft_in = jnp.concatenate([picked, next_embed], axis=1)
    depth = draft_fc.shape[0]
    blocks = draft_in.reshape(request_total, devices, depth).transpose(1, 0, 2)
    draft_out = draft(blocks.astype(jnp.float32), draft_fc).astype(jnp.bfloat16)
    return (layer_out, draft_out)


def solution(mesh):
    return jax.shard_map(
        per_device,
        mesh=mesh,
        in_specs=(
            P(("groups", "expert"), None),
            P(("groups", "expert"), None, None),
            P(("groups", "expert"), None, None, None),
            P(("groups", "expert")),
            P(("groups", "expert")),
            P(("groups", "expert"), None),
            P(),
            P(),
            P(("groups", "expert"), None),
            P(None, "expert"),
            P(None, "expert"),
            P("expert", None),
            P(("groups", "expert")),
            P(("groups", "expert"), None),
            P("expert", None),
        ),
        out_specs=(P(("groups", "expert"), None), P(("groups", "expert"), None)),
        check_vma=False,
    )
```
